32 devices in a mesh: dp: 8 (over z, y), mp: 4 (over x, core).
Axes of the slice: x: 2, y: 2, z: 4, core: 2. Of those that a mesh axis runs over, the one named last changes fastest.
Arguments:
- hidden_in: bfloat16 [32768, 768], P(('dp', 'mp')), may hold values from -37 to 37
- out_grad: bfloat16 [32768, 768], P(('dp', 'mp')), may hold values from -18 to 18
- seq_len: int32 [8], P('dp'), may hold values from 1024 to 4096, as said below
- owner_list: int32 [24], replicated, may hold values from 0 to 7, as said below
- block_master: float32 [4, 8, 768, 194], P('mp', 'dp'), may hold values from -0.4690971 to 0.4690971
- block_first: float32 [4, 8, 768, 194], P('mp', 'dp'), may hold values from -2048 to 2048
- block_second: float32 [4, 8, 768, 194], P('mp', 'dp'), may hold values from 131072 to 524288
- block_ema: float32 [4, 8, 768, 194], P('mp', 'dp'), may hold values from -0.21875 to 0.21875
- head_small: float32 [24, 10, 64], P('mp'), may hold values from -10 to 3
- head_first: float32 [24, 10, 64], P('mp'), may hold values from -1024 to 1024
- head_second: float32 [24, 10, 64], P('mp'), may hold values from 32768 to 131072
- head_ema: float32 [24, 10, 64], P('mp'), may hold values from -6 to 6
- bc_weight: float32 [768, 256], replicated, may hold values from -0.21875 to 0.21875
- bc_first: float32 [768, 256], replicated, may hold values from -1024 to 1024
- bc_second: float32 [768, 256], replicated, may hold values from 32768 to 131072
- bc_ema: float32 [768, 256], replicated, may hold values from -0.21875 to 0.21875
- shared_small: float32 [10, 256], replicated, may hold values from 0.25 to 1.25
- shared_first: float32 [10, 256], replicated, may hold values from -1024 to 1024
- shared_second: float32 [10, 256], replicated, may hold values from 32768 to 131072
- shared_ema: float32 [10, 256], replicated, may hold values from 0.25 to 1.25
Outputs:
- hidden_out: bfloat16 [32768, 768], P(('dp', 'mp'))
- hidden_grad: float32 [32768, 768], P(('dp', 'mp'))
- block_master_new: float32 [4, 8, 768, 194], P('mp', 'dp')
- block_first_new: float32 [4, 8, 768, 194], P('mp', 'dp')
- block_second_new: float32 [4, 8, 768, 194], P('mp', 'dp')
- block_ema_new: float32 [4, 8, 768, 194], P('mp', 'dp')
- head_small_new: float32 [24, 10, 64], P('mp')
- head_first_new: float32 [24, 10, 64], P('mp')
- head_second_new: float32 [24, 10, 64], P('mp')
- head_ema_new: float32 [24, 10, 64], P('mp')
- bc_weight_new: float32 [768, 256], replicated
- bc_first_new: float32 [768, 256], replicated
- bc_second_new: float32 [768, 256], replicated
- bc_ema_new: float32 [768, 256], replicated
- shared_small_new: float32 [10, 256], replicated
- shared_first_new: float32 [10, 256], replicated
- shared_second_new: float32 [10, 256], replicated
- shared_ema_new: float32 [10, 256], replicated
The draws below stay inside these ranges and needn't reach their ends.
Inputs may be any that keep to these rules, and one draw needn't show every extreme that they name: `seq_len`: all sequences of a group have the same length, one of 1024, 2048, 4096; each of the three occurs in every draw. `owner_list`: the 6 heads of one index of mp (heads i * 6 to (i + 1) * 6 - 1) have distinct owners.
All inputs are finite; a program needn't handle non-finite values.
Results may differ from the reference program's by a relative error of at most 0.01.
Values may be sent and summed in bfloat16 or wider, within the bound.
No kernel may reach another device: no remote copies, remote signals or barrier semaphores. Data moves between devices by JAX's collectives and lax.ppermute only.
A program may use at most 448 MiB of HBM per device.

```python
import math
import jax
import jax.numpy as jnp
from jax import lax

D = 768
H = 24
P_SIZE = 64
N = 64
K = 7
SHORT = 1024
BLOCK_LEN = 256
STEP = 3
GROUP_TOK = 4096
GROUPS = 8
TOKENS = 32768
HEAD_DEV = 6
N_DP = 8
N_MP = 4


def draw_hidden_in(key, part):
    first_key, column_key, row_key = jax.random.split(key, 3)
    base_draw = jnp.clip(jax.random.normal(first_key, (TOKENS, D), jnp.float32), -6.0, 6.0)
    columns = jnp.exp(jax.random.uniform(column_key, (1, D), jnp.float32, -1.2, 1.1))
    row_scale = jnp.exp(jax.random.uniform(row_key, (TOKENS, 1), jnp.float32, -0.69, 0.69))
    return (base_draw * columns * row_scale).astype(jnp.bfloat16)


def draw_out_grad(key, part):
    first_key = jax.random.fold_in(key, 0)
    base_draw = jnp.clip(jax.random.normal(first_key, (TOKENS, D), jnp.float32), -6.0, 6.0)
    group_index = (jnp.arange(TOKENS, dtype=jnp.int32) // GROUP_TOK).astype(jnp.float32)
    rising = 1.0 + 2.0 * group_index / max(GROUPS - 1, 1)
    return (base_draw * rising[:, None]).astype(jnp.bfloat16)


def draw_seq_len(key, part):
    order = jax.random.permutation(key, GROUPS)
    kinds = order % 3
    lengths = jnp.where(kinds == 0, SHORT, jnp.where(kinds == 1, 2 * SHORT, 4 * SHORT))
    return lengths.astype(jnp.int32)


def draw_owner_list(key, part):
    rank_count = H // HEAD_DEV
    key_list = jax.random.split(key, rank_count + 2)
    picks = jnp.stack([jax.random.permutation(key_list[rank_index], GROUPS)[:HEAD_DEV] for rank_index in range(rank_count)])
    chosen = jax.random.randint(key_list[rank_count], (), 0, rank_count)
    remaining = 1 + jax.random.permutation(key_list[rank_count + 1], GROUPS - 2)[:HEAD_DEV - 2]
    forced = jnp.concatenate([jnp.array([GROUPS - 1, 0], jnp.int32), remaining.astype(jnp.int32)])
    picks = jnp.where((jnp.arange(rank_count) == chosen)[:, None], forced[None, :], picks)
    return picks.reshape(H).astype(jnp.int32)


def draw_block_master(key, part):
    rank_count = H // HEAD_DEV
    block_width = 3 * P_SIZE + 2
    shape_all = (rank_count, GROUPS, D, block_width)
    base_draw = jnp.clip(jax.random.normal(key, shape_all, jnp.float32), -6.0, 6.0)
    column = jnp.arange(block_width)
    rank_rise = 1.0 + jnp.arange(rank_count, dtype=jnp.float32) / max(rank_count - 1, 1)
    value_cols = ((column >= P_SIZE) & (column < 2 * P_SIZE)).astype(jnp.float32)
    column_scale = jnp.where(column < 2 * P_SIZE, 1.0, jnp.where(column < 2 * P_SIZE + 2, 0.5, math.sqrt(D / (H * P_SIZE))))
    value_rise = 1.0 + value_cols[None, :] * (rank_rise[:, None] - 1.0)
    scale_all = column_scale[None, :] * value_rise / math.sqrt(D)
    return base_draw * scale_all[:, None, None, :]


def draw_head_small(key, part):
    key_list = jax.random.split(key, 5)
    gains = 1.0 + 0.15 * jnp.clip(jax.random.normal(key_list[0], (H, 1, P_SIZE), jnp.float32), -6.0, 6.0)
    slow_end = math.log(1.0 / 30.0)
    filter_taps = 0.5 * jnp.clip(jax.random.normal(key_list[1], (H, K, P_SIZE), jnp.float32), -6.0, 6.0)
    diagonal = jax.random.uniform(key_list[2], (H, 1, P_SIZE), jnp.float32, 0.5, 1.5)
    biases = jax.random.uniform(key_list[3], (H, 1, 2), jnp.float32, math.log(0.2 / (4 * SHORT)), slow_end)
    unused = 0.1 * jnp.clip(jax.random.normal(key_list[4], (H, 1, P_SIZE - 2), jnp.float32), -6.0, 6.0)
    return jnp.concatenate([gains, filter_taps, diagonal, jnp.concatenate([biases, unused], axis=2)], axis=1)


def block_levels(key, extent, cuts, low, top_value):
    def one(dim, blocks):
        draws = jax.random.uniform(jax.random.fold_in(jax.random.fold_in(key, 6), dim), (blocks,), jnp.float32, low / len(cuts), top_value / len(cuts))
        return jnp.repeat(jnp.exp(draws), extent[dim] // blocks).reshape((-1,) + (1,) * (len(extent) - dim - 1))

    level = one(*cuts[0])
    for cut in cuts[1:]:
        level = level * one(*cut)
    return level


def bell_draw(stream_key, extent, scale, reach, cuts=(), held_as=jnp.bfloat16):
    drawn = jax.random.normal(stream_key, extent, jnp.float32) * scale
    if len(cuts) > 0:
        drawn = block_levels(stream_key, extent, cuts, -0.22, 0.18) * drawn
    return jnp.clip(drawn, min=-reach, max=reach).astype(held_as)


def setup_inputs(seed: int = 0) -> dict:
    seeds = jax.random.split(jax.random.key(seed), 21)
    hidden_in = draw_hidden_in(jax.random.fold_in(seeds[20], 71), 0)
    out_grad = draw_out_grad(jax.random.fold_in(seeds[20], 71), 0)
    seq_len = draw_seq_len(jax.random.fold_in(seeds[20], 71), 0)
    owner_list = draw_owner_list(jax.random.fold_in(seeds[20], 71), 0)
    block_master = draw_block_master(jax.random.fold_in(seeds[20], 71), 0)
    block_first = bell_draw(seeds[5], (N_MP, N_DP, D, 3 * P_SIZE + 2), (2 * TOKENS ** 0.5), 2048.0, ((0, 4), (1, 8)), jnp.float32)
    block_second = jnp.clip(jnp.exp(math.log(524288.0) - 1.3862944 * jax.random.uniform(seeds[6], (N_MP, N_DP, D, 3 * P_SIZE + 2), jnp.float32) ** block_levels(seeds[6], (N_MP, N_DP, D, 3 * P_SIZE + 2), ((0, 4), (1, 8)), -0.2, 0.2)), 131072.0, 524288.0)
    block_ema = bell_draw(seeds[7], (N_MP, N_DP, D, 3 * P_SIZE + 2), D ** -0.5, 0.21875, ((0, 4), (1, 8)), jnp.float32)
    head_small = draw_head_small(jax.random.fold_in(seeds[20], 71), 0)
    head_first = bell_draw(seeds[9], (H, K + 3, P_SIZE), (TOKENS ** 0.5), 1024.0, ((0, 4),), jnp.float32)
    head_second = jnp.clip(jnp.exp(math.log(131072.0) - 1.3862944 * jax.random.uniform(seeds[10], (H, K + 3, P_SIZE), jnp.float32) ** block_levels(seeds[10], (H, K + 3, P_SIZE), ((0, 4),), -0.2, 0.2)), 32768.0, 131072.0)
    head_ema = bell_draw(seeds[11], (H, K + 3, P_SIZE), 1.0, 6.0, ((0, 4),), jnp.float32)
    bc_weight = bell_draw(seeds[12], (D, 4 * N), D ** -0.5, 0.21875, (), jnp.float32)
    bc_first = bell_draw(seeds[13], (D, 4 * N), (TOKENS ** 0.5), 1024.0, (), jnp.float32)
    bc_second = jnp.clip(jnp.exp(jax.random.uniform(seeds[14], (D, 4 * N), jnp.float32, math.log(32768.0), math.log(131072.0))), 32768.0, 131072.0)
    bc_ema = bell_draw(seeds[15], (D, 4 * N), D ** -0.5, 0.21875, (), jnp.float32)
    shared_small = jnp.clip(jax.random.uniform(seeds[16], (K + D // (4 * N), 4 * N), jnp.float32, 0.25, 1.25), 0.25, 1.25)
    shared_first = bell_draw(seeds[17], (K + D // (4 * N), 4 * N), (TOKENS ** 0.5), 1024.0, (), jnp.float32)
    shared_second = jnp.clip(jnp.exp(jax.random.uniform(seeds[18], (K + D // (4 * N), 4 * N), jnp.float32, math.log(32768.0), math.log(131072.0))), 32768.0, 131072.0)
    shared_ema = jnp.clip(jax.random.uniform(seeds[19], (K + D // (4 * N), 4 * N), jnp.float32, 0.25, 1.25), 0.25, 1.25)
    return dict(hidden_in=hidden_in, out_grad=out_grad, seq_len=seq_len, owner_list=owner_list, block_master=block_master, block_first=block_first, block_second=block_second, block_ema=block_ema, head_small=head_small, head_first=head_first, head_second=head_second, head_ema=head_ema, bc_weight=bc_weight, bc_first=bc_first, bc_second=bc_second, bc_ema=bc_ema, shared_small=shared_small, shared_first=shared_first, shared_second=shared_second, shared_ema=shared_ema)


PRECISE = lax.Precision.HIGHEST
NORM_EPS = 1e-05
BETA_ONE = 0.5
BETA_TWO = 0.5
ADAM_EPS = 1e-08
WEIGHT_DECAY = 0.1
MATRIX_RATE = 0.04
SMALL_RATE = 0.2
AVERAGE_KEEP = 0.75

@jax.custom_vjp
def low(v):
    return lax.optimization_barrier(v.astype(jnp.bfloat16)).astype(jnp.float32)

@jax.custom_vjp
def low_back(v):
    return v

def low_keep(v):
    return (low(v), None)

def low_pass(kept, grad):
    return (grad,)

def back_keep(v):
    return (v, None)

def back_low(kept, grad):
    return (low(grad),)
low.defvjp(low_keep, low_pass)
low_back.defvjp(back_keep, back_low)

def conv_centered(signal, filter_taps, seq_length):
    row_count = signal.shape[0]
    tap_count = filter_taps.shape[0]
    position = jnp.arange(row_count, dtype=jnp.int32) % seq_length
    summed = jnp.zeros_like(signal)
    for tap_index in range(tap_count):
        offset = tap_index - tap_count // 2
        shifted = jnp.roll(signal, -offset, axis=0)
        inside = (position + offset >= 0) & (position + offset < seq_length)
        summed = summed + jnp.where(inside[:, None], shifted, 0.0) * filter_taps[tap_index][None, :]
    return summed

def shift_down(values, seq_length):
    shifted = jnp.concatenate([jnp.zeros_like(values[:1]), values[:-1]], axis=0)
    position = jnp.arange(values.shape[0], dtype=jnp.int32) % seq_length
    return jnp.where((position > 0)[:, None, None], shifted, 0.0)

def mix_block(state_in, pieces):
    values, b_vectors, c_vectors, step_rates, keep_flag = pieces
    log_decay = jnp.cumsum(-step_rates, axis=0).T
    entering = state_in * keep_flag
    scores = jnp.dot(c_vectors, b_vectors.T, precision=PRECISE)
    block_size = step_rates.shape[0]
    causal_mask = (jnp.arange(block_size)[:, None] >= jnp.arange(block_size)[None, :])[None]
    log_gap = log_decay[:, :, None] - log_decay[:, None, :]
    decay_mat = jnp.where(causal_mask, jnp.exp(jnp.where(causal_mask, log_gap, -60.0)), 0.0)
    weights = decay_mat * scores[None] * step_rates.T[:, None, :]
    inner_part = jnp.einsum('hij,jhp->ihp', weights, values, precision=PRECISE)
    cross_part = jnp.einsum('in,hnp->ihp', c_vectors, entering, precision=PRECISE) * jnp.exp(log_decay).T[:, :, None]
    tail_decay = jnp.exp(log_decay[:, -1:] - log_decay) * step_rates.T
    new_state = entering * jnp.exp(log_decay[:, -1])[:, None, None] + jnp.einsum('jn,hj,jhp->hnp', b_vectors, tail_decay, values, precision=PRECISE)
    return (new_state, inner_part + cross_part)

def state_mix(values, b_vectors, c_vectors, step_rates, seq_length):
    row_count, head_count, head_width = values.shape
    blocks = row_count // BLOCK_LEN
    keep_flags = (jnp.arange(blocks, dtype=jnp.int32) * BLOCK_LEN % seq_length != 0).astype(jnp.float32)
    shaped = (values.reshape(blocks, BLOCK_LEN, head_count, head_width), b_vectors.reshape(blocks, BLOCK_LEN, -1), c_vectors.reshape(blocks, BLOCK_LEN, -1), step_rates.reshape(blocks, BLOCK_LEN, head_count), keep_flags)
    initial = jnp.zeros((head_count, b_vectors.shape[1], head_width), jnp.float32)
    _, results = lax.scan(jax.checkpoint(mix_block), initial, shaped)
    return results.reshape(row_count, head_count, head_width)

def local_mix(proj_heads, proj_keys, head_params, key_taps, seq_length):
    row_count, head_count, _ = proj_heads.shape
    head_width = head_params.shape[2]
    tap_count = key_taps.shape[0]
    gate_part = proj_heads[:, :, :head_width]
    value_part = proj_heads[:, :, head_width:2 * head_width].reshape(row_count, head_count * head_width)
    rate_part = proj_heads[:, :, 2 * head_width:2 * head_width + 2]
    value_taps = jnp.transpose(head_params[:, 1:1 + tap_count, :], (1, 0, 2)).reshape(tap_count, head_count * head_width)
    values = jax.nn.silu(conv_centered(value_part, value_taps, seq_length)).reshape(row_count, head_count, head_width)
    key_signal = jax.nn.silu(conv_centered(proj_keys, key_taps, seq_length))
    state_size = key_signal.shape[1] // 4
    forward_b = key_signal[:, :state_size]
    forward_c = key_signal[:, state_size:2 * state_size]
    reverse_b = key_signal[:, 2 * state_size:3 * state_size]
    reverse_c = key_signal[:, 3 * state_size:]
    step_rates = jax.nn.softplus(rate_part + head_params[None, :, tap_count + 2, :2])
    diagonal = head_params[:, tap_count + 1, :]
    forward = shift_down(state_mix(values, forward_b, forward_c, step_rates[:, :, 0], seq_length), seq_length)
    backward = shift_down(state_mix(values[::-1], reverse_b[::-1], reverse_c[::-1], step_rates[::-1, :, 1], seq_length), seq_length)[::-1]
    mixture = forward + backward + values * diagonal[None]
    return mixture * jax.nn.silu(gate_part)

def adamw_update(weight, gradient, first_moment, second, average, step_rate):
    first_new = BETA_ONE * first_moment + (1.0 - BETA_ONE) * gradient
    second_new = BETA_TWO * second + (1.0 - BETA_TWO) * gradient * gradient
    correct_one = 1.0 - BETA_ONE ** STEP
    correct_two = 1.0 - BETA_TWO ** STEP
    normalized = first_new / correct_one / (jnp.sqrt(second_new / correct_two) + ADAM_EPS)
    weight_new = weight - step_rate * (normalized + WEIGHT_DECAY * weight)
    average_new = AVERAGE_KEEP * average + (1.0 - AVERAGE_KEEP) * weight_new
    return (weight_new, first_new, second_new, average_new)

def group_forward(hidden, seq_length, blocks_low, head_params, key_low, shared):
    key_taps = shared[:K]
    gain_in = shared[K:].reshape(-1)
    scale_in = lax.rsqrt(lax.optimization_barrier(jnp.mean(hidden * hidden, axis=1, keepdims=True)) + NORM_EPS)
    features = low(hidden * scale_in * gain_in)
    in_width = 2 * P_SIZE + 2
    proj_heads = low_back(jnp.einsum('td,hdc->thc', features, blocks_low[:, :, :in_width], precision=PRECISE))
    proj_keys = low_back(jnp.dot(features, key_low, precision=PRECISE))
    gated_mix = local_mix(proj_heads, proj_keys, head_params, key_taps, seq_length)
    scale_mix = lax.rsqrt(lax.optimization_barrier(jnp.mean(gated_mix * gated_mix, axis=(1, 2), keepdims=True)) + NORM_EPS)
    result_low = low(gated_mix * scale_mix * head_params[None, :, 0, :])
    branch_out = jnp.einsum('thp,hdp->td', result_low, blocks_low[:, :, in_width:], precision=PRECISE)
    return hidden + branch_out

def reference(hidden_in, out_grad, seq_len, owner_list, block_master, block_first, block_second, block_ema, head_small, head_first, head_second, head_ema, bc_weight, bc_first, bc_second, bc_ema, shared_small, shared_first, shared_second, shared_ema):
    head_rank = jnp.arange(H, dtype=jnp.int32) // HEAD_DEV
    blocks = block_master[head_rank, owner_list]

    def whole_layer(hidden, blocks_in, params_in, key_weight, shared_in):
        blocks_low = low(blocks_in)
        key_low = low(key_weight)

        def per_group(group_item):
            return group_forward(group_item[0], group_item[1], blocks_low, params_in, key_low, shared_in)
        grouped = lax.map(jax.checkpoint(per_group), (hidden.reshape(GROUPS, GROUP_TOK, D), seq_len))
        return grouped.reshape(TOKENS, D)
    hidden = hidden_in.astype(jnp.float32)
    outputs, pullback = jax.vjp(whole_layer, hidden, blocks, head_small, bc_weight, shared_small)
    gradients = pullback(out_grad.astype(jnp.float32))
    hidden_out = outputs.astype(jnp.bfloat16)
    hidden_grad = gradients[0]
    block_new = adamw_update(blocks, gradients[1], block_first[head_rank, owner_list], block_second[head_rank, owner_list], block_ema[head_rank, owner_list], MATRIX_RATE)
    master_new = block_master.at[head_rank, owner_list].set(block_new[0])
    first_new = block_first.at[head_rank, owner_list].set(block_new[1])
    second_new = block_second.at[head_rank, owner_list].set(block_new[2])
    ema_new = block_ema.at[head_rank, owner_list].set(block_new[3])
    head_new = adamw_update(head_small, gradients[2], head_first, head_second, head_ema, SMALL_RATE)
    key_new = adamw_update(bc_weight, gradients[3], bc_first, bc_second, bc_ema, MATRIX_RATE)
    shared_new = adamw_update(shared_small, gradients[4], shared_first, shared_second, shared_ema, SMALL_RATE)
    return (hidden_out, hidden_grad, master_new, first_new, second_new, ema_new, head_new[0], head_new[1], head_new[2], head_new[3], key_new[0], key_new[1], key_new[2], key_new[3], shared_new[0], shared_new[1], shared_new[2], shared_new[3])
```

```python
import jax
import jax.numpy as jnp
from jax import lax
from jax.experimental import pallas as pl
from jax.experimental.pallas import tpu as pltpu
from jax.sharding import PartitionSpec as P

D = 768
H = 24
PS = 64
NS = 64
K = 7
STEP = 3
CH = H * PS
BL = 128
GH = 8
NG = H // GH
WV = 80
PAD = 128
HALO = 8
NORM_EPS = 1e-05
BETA_ONE = 0.5
BETA_TWO = 0.5
ADAM_EPS = 1e-08
WEIGHT_DECAY = 0.1
MATRIX_RATE = 0.04
SMALL_RATE = 0.2
AVERAGE_KEEP = 0.75

f32 = jnp.float32
bf16 = jnp.bfloat16
LQ, RQ, KF, KR, WF, WR, EF, ER, XF, XR, RF, RR = range(12)
KINDS = 12


def params(mb=56):
    return pltpu.CompilerParams(
        dimension_semantics=("arbitrary",), vmem_limit_bytes=mb * 1024 * 1024
    )


def cost(micros):
    return pl.CostEstimate(flops=0, transcendentals=0, bytes_accessed=micros * 1_000_000)


def nt(a, b, precision=None):
    return lax.dot_general(
        a, b, (((1,), (1,)), ((), ())), preferred_element_type=f32, precision=precision
    )


def nn(a, b, precision=None):
    return lax.dot_general(
        a, b, (((1,), (0,)), ((), ())), preferred_element_type=f32, precision=precision
    )


def tn(a, b):
    return lax.dot_general(a, b, (((0,), (0,)), ((), ())), preferred_element_type=f32)


def sigmoid(v):
    return 1.0 / (1.0 + jnp.exp(-v))


def lane_first(shape):
    return lax.broadcasted_iota(jnp.int32, shape, len(shape) - 1) < NS


def conv_taps(signal, taps, sign):
    ext = signal.shape[1]
    total = None
    for k in range(K):
        shift = (sign * (k - K // 2)) % ext
        moved = signal if shift == 0 else pltpu.roll(signal, shift, axis=1)
        term = moved * taps[:, k : k + 1]
        total = term if total is None else total + term
    return total


def causal_masks():
    row = lax.broadcasted_iota(jnp.int32, (BL, BL), 0)
    col = lax.broadcasted_iota(jnp.int32, (BL, BL), 1)
    return row < col, row > col


def stacked_keys(a, b):
    zero = jnp.zeros_like(a)
    return jnp.concatenate(
        [jnp.concatenate([a, zero], axis=1), jnp.concatenate([zero, b], axis=1)], axis=0
    )


def key_kernel(nx_ref, w_ref, taps_ref, p_ref, u_ref, k_ref, st_ref):
    tokens = u_ref.shape[1]
    proj = nt(w_ref[...], nx_ref[...])
    pre = conv_taps(proj, taps_ref[...], -1)
    key = pre * sigmoid(pre)
    ext = key.shape[1]
    b_f = key[:NS, :tokens].astype(bf16)
    c_f = pltpu.roll(key[NS : 2 * NS], 1, axis=1)[:, :tokens].astype(bf16)
    b_r = key[2 * NS : 3 * NS, :tokens].astype(bf16)
    c_r = pltpu.roll(key[3 * NS :], ext - 1, axis=1)[:, :tokens].astype(bf16)
    p_ref[...] = proj
    u_ref[...] = pre[:, :tokens]
    k_ref[...] = jnp.concatenate([b_f, c_f, b_r, c_r], axis=0)
    lower, upper = causal_masks()
    for blk in range(tokens // BL):
        part = slice(blk * BL, (blk + 1) * BL)
        s_f = tn(b_f[:, part], c_f[:, part])
        s_r = tn(b_r[:, part], c_r[:, part])
        st_ref[blk] = jnp.where(lower, s_f, jnp.where(upper, s_r, 0.0))


def key_stage(nx, key_low, taps, tokens):
    ext = nx.shape[0]
    blocks = tokens // BL
    return pl.pallas_call(
        key_kernel,
        out_shape=(
            jax.ShapeDtypeStruct((4 * NS, ext), f32),
            jax.ShapeDtypeStruct((4 * NS, tokens), f32),
            jax.ShapeDtypeStruct((4 * NS, tokens), bf16),
            jax.ShapeDtypeStruct((blocks, BL, BL), f32),
        ),
        compiler_params=pltpu.CompilerParams(vmem_limit_bytes=56 * 1024 * 1024),
        cost_estimate=cost(6),
        name="key_stage",
    )(nx, key_low, taps)


def value_kernel(
    nx_ref, wv_ref, taps_ref, bias_ref, k4_ref, tri_ref,
    v_ref, u_ref, s_ref, rows_ref, tot_ref, sblk_ref, sdev_ref, tdev_ref,
    p_scr, lhs_scr,
):
    tokens = v_ref.shape[1]
    blocks = tokens // BL
    p_scr[...] = nt(wv_ref[...].reshape(GH * WV, D), nx_ref[...])
    for h in range(GH):
        for c in range(PS // 16):
            src = h * WV + c * 16
            dst = h * PS + c * 16
            signal = p_scr[src : src + 16, :]
            pre = conv_taps(signal, taps_ref[dst : dst + 16, :], -1)[:, :tokens]
            s_ref[dst : dst + 16, :] = signal.astype(bf16)
            u_ref[dst : dst + 16, :] = pre.astype(bf16)
            v_ref[dst : dst + 16, :] = (pre * sigmoid(pre)).astype(bf16)
    x_f = jnp.concatenate(
        [p_scr[h * WV + PS : h * WV + PS + 1, :tokens] for h in range(GH)], axis=0
    )
    x_r = jnp.concatenate(
        [p_scr[h * WV + PS + 1 : h * WV + PS + 2, :tokens] for h in range(GH)], axis=0
    )
    x_f = x_f + bias_ref[:, 0:1]
    x_r = x_r + bias_ref[:, 1:2]
    rate_f = jnp.maximum(x_f, 0.0) + jnp.log1p(jnp.exp(-jnp.abs(x_f)))
    rate_r = jnp.maximum(x_r, 0.0) + jnp.log1p(jnp.exp(-jnp.abs(x_r)))
    rows_ref[XF] = x_f
    rows_ref[XR] = x_r
    rows_ref[RF] = rate_f
    rows_ref[RR] = rate_r
    cuts = [slice(b * BL, (b + 1) * BL) for b in range(blocks)]
    stack = jnp.concatenate([rate_f[:, c] for c in cuts] + [rate_r[:, c] for c in cuts], axis=0)
    sums = -nn(stack, tri_ref[...], lax.Precision.HIGHEST)
    first = lane_first((GH, BL))
    cum_r = jnp.zeros((GH, BL), f32)
    cum_f = jnp.zeros((GH, BL), f32)
    state = jnp.zeros((GH * PS, BL), f32)
    for b in range(blocks):
        l_f = sums[b * GH : (b + 1) * GH]
        l_r = sums[(blocks + b) * GH : (blocks + b + 1) * GH]
        r_f = rate_f[:, cuts[b]]
        r_r = rate_r[:, cuts[b]]
        end_f = jnp.broadcast_to(l_f[:, BL - 1 : BL], (GH, BL))
        end_r = jnp.broadcast_to(l_r[:, BL - 1 : BL], (GH, BL))
        w_f = jnp.exp(end_f - l_f) * r_f
        w_r = jnp.exp(l_r + r_r) * r_r
        rows_ref[LQ, :, cuts[b]] = l_f + r_f
        rows_ref[RQ, :, cuts[b]] = -l_r
        rows_ref[KF, :, cuts[b]] = l_f - jnp.log(r_f)
        rows_ref[KR, :, cuts[b]] = -(l_r + r_r + jnp.log(r_r))
        rows_ref[WF, :, cuts[b]] = w_f
        rows_ref[WR, :, cuts[b]] = w_r
        rows_ref[EF, :, cuts[b]] = jnp.exp(l_f + r_f)
        rows_ref[ER, :, cuts[b]] = jnp.exp(end_r - l_r)
        tot_ref[b] = jnp.where(first, end_f, end_r)
        for h in range(GH):
            span = slice(h * PS, (h + 1) * PS)
            vals = v_ref[span, cuts[b]].astype(f32)
            lhs_scr[span, :BL] = (vals * w_f[h : h + 1]).astype(bf16)
            lhs_scr[span, BL:] = (vals * w_r[h : h + 1]).astype(bf16)
        keys = stacked_keys(k4_ref[:NS, cuts[b]], k4_ref[2 * NS : 3 * NS, cuts[b]])
        local_state = nt(lhs_scr[...], keys)
        sblk_ref[b] = local_state
        keep = jnp.where(first, jnp.exp(end_f), 1.0)
        gain = jnp.where(first, 1.0, jnp.exp(cum_r))
        state = jnp.concatenate(
            [
                state[h * PS : (h + 1) * PS] * keep[h : h + 1]
                + local_state[h * PS : (h + 1) * PS] * gain[h : h + 1]
                for h in range(GH)
            ],
            axis=0,
        )
        cum_f = cum_f + end_f
        cum_r = cum_r + end_r
    sdev_ref[...] = state.astype(bf16)
    tdev_ref[...] = jnp.where(first, cum_f, cum_r)


def value_stage(nx, wv, taps, bias, k4, tri, tokens):
    ext = nx.shape[0]
    blocks = tokens // BL
    rows = GH * PS
    return pl.pallas_call(
        value_kernel,
        grid=(NG,),
        in_specs=[
            pl.BlockSpec((ext, D), lambda g: (0, 0), pipeline_mode=pl.Buffered(1)),
            pl.BlockSpec((GH, WV, D), lambda g: (g, 0, 0)),
            pl.BlockSpec((rows, 8), lambda g: (g, 0)),
            pl.BlockSpec((GH, 2), lambda g: (g, 0)),
            pl.BlockSpec((4 * NS, tokens), lambda g: (0, 0)),
            pl.BlockSpec((BL, BL), lambda g: (0, 0)),
        ],
        out_specs=[
            pl.BlockSpec((rows, tokens), lambda g: (g, 0)),
            pl.BlockSpec((rows, tokens), lambda g: (g, 0)),
            pl.BlockSpec((rows, ext), lambda g: (g, 0)),
            pl.BlockSpec((KINDS, GH, tokens), lambda g: (0, g, 0)),
            pl.BlockSpec((blocks, GH, BL), lambda g: (0, g, 0)),
            pl.BlockSpec((blocks, rows, BL), lambda g: (0, g, 0)),
            pl.BlockSpec((rows, BL), lambda g: (g, 0)),
            pl.BlockSpec((GH, BL), lambda g: (g, 0)),
        ],
        out_shape=(
            jax.ShapeDtypeStruct((CH, tokens), bf16),
            jax.ShapeDtypeStruct((CH, tokens), bf16),
            jax.ShapeDtypeStruct((CH, ext), bf16),
            jax.ShapeDtypeStruct((KINDS, H, tokens), f32),
            jax.ShapeDtypeStruct((blocks, H, BL), f32),
            jax.ShapeDtypeStruct((blocks, CH, BL), f32),
            jax.ShapeDtypeStruct((CH, BL), bf16),
            jax.ShapeDtypeStruct((H, BL), f32),
        ),
        scratch_shapes=[pltpu.VMEM((GH * WV, ext), f32), pltpu.VMEM((rows, 2 * BL), bf16)],
        compiler_params=params(),
        cost_estimate=cost(27),
        name="value_stage",
    )(nx, wv, taps, bias, k4, tri)


def chain_kernel(flip, copies, tokens, twist, meta_ref, sblk_ref, tot_ref, far_ref, *refs):
    states = refs[:copies]
    if flip:
        other_ref, out_ref, dot_ref = refs[copies:]
    else:
        (out_ref,) = refs[copies:]
    blocks = sblk_ref.shape[0]
    per = sblk_ref.shape[1] // PS
    step = pl.program_id(0)
    first = lane_first((1, BL))
    wide = lane_first((PS, BL))
    up_lanes = jnp.logical_not(wide) if flip else wide
    here = meta_ref[0]
    length = meta_ref[1]
    sequence = here * tokens // length
    places = [meta_ref[2 + k] for k in range(copies)]
    same = [(place * tokens // length) == sequence for place in places]
    for i in range(per):
        span = slice(i * PS, (i + 1) * PS)
        head = step * per + i
        totals = []
        for k in range(copies):
            place = twist(k, step) * per + i
            parts = [far_ref[k, pl.ds(part * H + place, 1), :] for part in range(3)]
            totals.append(parts[0] + parts[1] + parts[2])
        entering = jnp.zeros((PS, BL), f32)
        for k in range(copies):
            left = jnp.zeros((1, BL), f32)
            right = jnp.zeros((1, BL), f32)
            for q in range(copies):
                if q != k:
                    between = (places[q] > places[k]) & (places[q] < here)
                    left = left + totals[q] * between.astype(f32)
                    between = (places[q] < places[k]) & (places[q] > here)
                    right = right + totals[q] * between.astype(f32)
            from_left = jnp.exp(left) * (same[k] & (places[k] < here)).astype(f32)
            from_right = jnp.exp(right) * (same[k] & (places[k] > here)).astype(f32)
            if flip:
                weight = jnp.where(first, from_right, from_left)
            else:
                weight = jnp.where(first, from_left, from_right)
            entering = entering + weight * states[k][span, :].astype(f32)
        decay = [jnp.exp(tot_ref[b, pl.ds(head, 1), :]) for b in range(blocks)]
        up = [entering]
        for b in range(blocks):
            up.append(up[-1] * decay[b] + sblk_ref[b, span, :])
        down = entering
        for b in range(blocks, -1, -1):
            if b < blocks:
                down = down * decay[b] + sblk_ref[b, span, :]
            both = jnp.where(up_lanes, up[b], down)
            out_ref[b, span, :] = both.astype(bf16)
            if flip:
                dot_ref[b, pl.ds(head, 1), :] = jnp.sum(
                    both * other_ref[b, span, :].astype(f32), axis=0, keepdims=True
                )


def chain_stage(meta, sblk, tot, far_tot, states, twist, tokens, other=None):
    blocks = sblk.shape[0]
    copies = len(states)
    rows = CH // copies
    flip = other is not None
    in_specs = [
        pl.BlockSpec((blocks, rows, BL), lambda q, meta: (0, q, 0)),
        pl.BlockSpec((blocks, H, BL), lambda q, meta: (0, 0, 0)),
        pl.BlockSpec((copies, 3 * H, BL), lambda q, meta: (0, 0, 0)),
    ]
    for k in range(copies):
        in_specs.append(pl.BlockSpec((rows, BL), lambda q, meta, k=k: (twist(k, q), 0)))
    out_specs = [pl.BlockSpec((blocks + 1, rows, BL), lambda q, meta: (0, q, 0))]
    out_shape = [jax.ShapeDtypeStruct((blocks + 1, CH, BL), bf16)]
    args = [meta, sblk, tot, far_tot, *states]
    if flip:
        in_specs.append(pl.BlockSpec((blocks + 1, rows, BL), lambda q, meta: (0, q, 0)))
        out_specs.append(pl.BlockSpec((blocks + 1, H, BL), lambda q, meta: (0, 0, 0)))
        out_shape.append(jax.ShapeDtypeStruct((blocks + 1, H, BL), f32))
        args.append(other)

    def body(*refs):
        chain_kernel(flip, copies, tokens, twist, *refs)

    return pl.pallas_call(
        body,
        grid_spec=pltpu.PrefetchScalarGridSpec(
            num_scalar_prefetch=1, grid=(copies,), in_specs=in_specs, out_specs=out_specs
        ),
        out_shape=out_shape,
        compiler_params=params(),
        cost_estimate=cost(7),
        name="chain_back" if flip else "chain_stage",
    )(*args)


def pair_blocks(value):
    zero = jnp.zeros((PS, BL), value.dtype)
    return jnp.concatenate(
        [
            jnp.concatenate([value[:PS], zero], axis=1),
            jnp.concatenate([zero, value[PS:]], axis=1),
        ],
        axis=0,
    )


def intra_kernel(v_ref, rows_ref, st_ref, o_ref):
    lower, _ = causal_masks()
    kf_cols = jnp.transpose(rows_ref[KF])
    kr_cols = jnp.transpose(rows_ref[KR])
    for pair in range(H // 2):
        mats = []
        for h in (2 * pair, 2 * pair + 1):
            gap = jnp.where(
                lower,
                rows_ref[LQ, h : h + 1, :] - kf_cols[:, h : h + 1],
                rows_ref[RQ, h : h + 1, :] - kr_cols[:, h : h + 1],
            )
            decay = jnp.exp(jnp.minimum(gap, 80.0))
            mats.append((decay * st_ref[0]).astype(bf16))
        span = slice(pair * 2 * PS, (pair + 1) * 2 * PS)
        out = nn(pair_blocks(v_ref[span, :]), jnp.concatenate(mats, axis=0))
        o_ref[span, :] = out.astype(o_ref.dtype)


def intra_stage(v, rows, scores):
    tokens = v.shape[1]
    return pl.pallas_call(
        intra_kernel,
        grid=(tokens // BL,),
        in_specs=[
            pl.BlockSpec((CH, BL), lambda b: (0, b)),
            pl.BlockSpec((KINDS, H, BL), lambda b: (0, 0, b)),
            pl.BlockSpec((1, BL, BL), lambda b: (b, 0, 0)),
        ],
        out_specs=pl.BlockSpec((CH, BL), lambda b: (0, b)),
        out_shape=jax.ShapeDtypeStruct((CH, tokens), bf16),
        compiler_params=params(),
        cost_estimate=cost(12),
        name="intra_stage",
    )(v, rows, scores)


def token_kernel(
    oi_ref, v_ref, sa_ref, sb_ref, k4_ref, rows_ref, tot_ref, wg_ref, wo_ref,
    nx_ref, hid_ref, go_ref, cols_ref,
    ho_ref, r_ref, dg_ref, do_ref, dsblk_ref, dsdev_ref, rc_ref, small_ref,
    cf_scr, cr_scr, g_scr, dres_scr, mix_scr, gated_scr, lhs_scr, gain_scr, diag_scr,
    dev_scr, cum_scr,
):
    step = pl.program_id(0)
    last = pl.num_programs(0) - 1

    @pl.when(step == 0)
    def _():
        gain_scr[...] = jnp.zeros_like(gain_scr)
        diag_scr[...] = jnp.zeros_like(diag_scr)
        dev_scr[...] = jnp.zeros_like(dev_scr)
        cum_scr[...] = jnp.zeros_like(cum_scr)

    c_f = k4_ref[NS : 2 * NS, :]
    c_r = k4_ref[3 * NS :, :]
    zero = jnp.zeros_like(c_f)
    cf_scr[...] = nn(sa_ref[0], jnp.concatenate([c_f, zero], axis=0))
    cr_scr[...] = nn(sb_ref[0], jnp.concatenate([zero, c_r], axis=0))
    g_scr[...] = nt(wg_ref[...], nx_ref[...])
    dres_scr[...] = nt(wo_ref[...], go_ref[...])
    squares = jnp.zeros((8, BL), f32)
    for h in range(H):
        span = slice(h * PS, (h + 1) * PS)
        part_f = cf_scr[span, :] * rows_ref[EF, h : h + 1, :]
        part_r = cr_scr[span, :] * rows_ref[ER, h : h + 1, :]
        cf_scr[span, :] = part_f
        cr_scr[span, :] = part_r
        mix = (
            oi_ref[span, :].astype(f32)
            + part_f
            + part_r
            + cols_ref[span, 1:2] * v_ref[span, :].astype(f32)
        )
        gate = g_scr[span, :]
        gated = mix * (gate * sigmoid(gate))
        mix_scr[span, :] = mix
        gated_scr[span, :] = gated
        squares = squares + jnp.sum((gated * gated).reshape(PS // 8, 8, BL), axis=0)
    scale = lax.rsqrt(jnp.sum(squares, axis=0, keepdims=True) / CH + NORM_EPS)
    cross = jnp.zeros((8, BL), f32)
    for h in range(H):
        span = slice(h * PS, (h + 1) * PS)
        gated = gated_scr[span, :]
        gain = cols_ref[span, 0:1]
        normal = gated * scale
        r_ref[span, :] = (normal * gain).astype(bf16)
        dres = dres_scr[span, :]
        gain_scr[span, :] += dres * normal
        cross = cross + jnp.sum((dres * gain * gated).reshape(PS // 8, 8, BL), axis=0)
    out = tn(r_ref[...], wo_ref[...])
    ho_ref[...] = (hid_ref[...].astype(f32) + out).astype(bf16)
    pull = scale * scale * scale * (jnp.sum(cross, axis=0, keepdims=True) / CH)
    for h in range(H):
        span = slice(h * PS, (h + 1) * PS)
        dgated = scale * (dres_scr[span, :] * cols_ref[span, 0:1]) - gated_scr[span, :] * pull
        gate = g_scr[span, :]
        soft = sigmoid(gate)
        grad_mix = dgated * (gate * soft)
        dg_ref[span, :] = (dgated * mix_scr[span, :] * (soft * (1.0 + gate * (1.0 - soft)))).astype(
            bf16
        )
        diag_scr[span, :] += grad_mix * v_ref[span, :].astype(f32)
        do_ref[span, :] = grad_mix.astype(bf16)
        rc_ref[0, h : h + 1, :] = jnp.sum(grad_mix * cf_scr[span, :], axis=0, keepdims=True)
        rc_ref[1, h : h + 1, :] = jnp.sum(grad_mix * cr_scr[span, :], axis=0, keepdims=True)
        lhs_scr[span, :BL] = (grad_mix * rows_ref[EF, h : h + 1, :]).astype(bf16)
        lhs_scr[span, BL:] = (grad_mix * rows_ref[ER, h : h + 1, :]).astype(bf16)
    dstate = nt(lhs_scr[...], stacked_keys(c_f, c_r))
    dsblk_ref[0] = dstate
    first = lane_first((H, BL))
    total = tot_ref[0]
    keep = jnp.where(first, 1.0, jnp.exp(total))
    grow = jnp.where(first, jnp.exp(cum_scr[...]), 1.0)
    for h in range(H):
        span = slice(h * PS, (h + 1) * PS)
        dev_scr[span, :] = (
            dev_scr[span, :] * keep[h : h + 1] + dstate[span, :] * grow[h : h + 1]
        )
    cum_scr[...] += total

    @pl.when(step == last)
    def _():
        dsdev_ref[...] = dev_scr[...].astype(bf16)
        ones = jnp.ones((8, BL), f32)
        small_ref[0] = nt(ones, gain_scr[...], lax.Precision.HIGHEST)
        small_ref[1] = nt(ones, diag_scr[...], lax.Precision.HIGHEST)


def token_stage(oi, v, s9, k4, rows, tot, wg, wo, nx, hid, go, cols):
    tokens = v.shape[1]
    blocks = tokens // BL
    whole = dict(pipeline_mode=pl.Buffered(1))
    chan = pl.BlockSpec((CH, BL), lambda b: (0, b))
    toks = pl.BlockSpec((BL, D), lambda b: (b, 0))
    big = pltpu.VMEM((CH, BL), f32)
    return pl.pallas_call(
        token_kernel,
        grid=(blocks,),
        in_specs=[
            chan,
            chan,
            pl.BlockSpec((1, CH, BL), lambda b: (b, 0, 0)),
            pl.BlockSpec((1, CH, BL), lambda b: (b + 1, 0, 0)),
            pl.BlockSpec((4 * NS, BL), lambda b: (0, b)),
            pl.BlockSpec((KINDS, H, BL), lambda b: (0, 0, b)),
            pl.BlockSpec((1, H, BL), lambda b: (b, 0, 0)),
            pl.BlockSpec((CH, D), lambda b: (0, 0), **whole),
            pl.BlockSpec((CH, D), lambda b: (0, 0), **whole),
            toks,
            toks,
            toks,
            pl.BlockSpec((CH, 8), lambda b: (0, 0), **whole),
        ],
        out_specs=[
            toks,
            chan,
            chan,
            chan,
            pl.BlockSpec((1, CH, BL), lambda b: (b, 0, 0)),
            pl.BlockSpec((CH, BL), lambda b: (0, 0)),
            pl.BlockSpec((2, H, BL), lambda b: (0, 0, b)),
            pl.BlockSpec((2, 8, CH), lambda b: (0, 0, 0)),
        ],
        out_shape=(
            jax.ShapeDtypeStruct((tokens, D), bf16),
            jax.ShapeDtypeStruct((CH, tokens), bf16),
            jax.ShapeDtypeStruct((CH, tokens), bf16),
            jax.ShapeDtypeStruct((CH, tokens), bf16),
            jax.ShapeDtypeStruct((blocks, CH, BL), f32),
            jax.ShapeDtypeStruct((CH, BL), bf16),
            jax.ShapeDtypeStruct((2, H, tokens), f32),
            jax.ShapeDtypeStruct((2, 8, CH), f32),
        ),
        scratch_shapes=[big] * 6
        + [pltpu.VMEM((CH, 2 * BL), bf16)]
        + [big] * 3
        + [pltpu.VMEM((H, BL), f32)],
        compiler_params=params(),
        cost_estimate=cost(35),
        name="token_stage",
    )(oi, v, s9, s9, k4, rows, tot, wg, wo, nx, hid, go, cols)


def early_grad_kernel(dg_ref, r_ref, nx_ref, go_ref, wg_ref, out_ref, dn_ref):
    gate = nn(dg_ref[...], nx_ref[...]).astype(bf16)
    outp = nn(r_ref[...], go_ref[...]).astype(bf16)
    out_ref[:, :PS, :] = gate.reshape(GH, PS, D)
    out_ref[:, PS:, :] = outp.reshape(GH, PS, D)
    part = tn(dg_ref[...], wg_ref[...])
    step = pl.program_id(0)

    @pl.when(step == 0)
    def _():
        dn_ref[...] = part

    @pl.when(step > 0)
    def _():
        dn_ref[...] += part


def early_grad_stage(dgate, result, nx, go, wg):
    tokens = dgate.shape[1]
    rows = GH * PS
    return pl.pallas_call(
        early_grad_kernel,
        grid=(NG,),
        in_specs=[
            pl.BlockSpec((rows, tokens), lambda g: (g, 0)),
            pl.BlockSpec((rows, tokens), lambda g: (g, 0)),
            pl.BlockSpec((tokens, D), lambda g: (0, 0)),
            pl.BlockSpec((tokens, D), lambda g: (0, 0)),
            pl.BlockSpec((rows, D), lambda g: (g, 0)),
        ],
        out_specs=[
            pl.BlockSpec((GH, 2 * PS, D), lambda g: (g, 0, 0)),
            pl.BlockSpec((tokens, D), lambda g: (0, 0)),
        ],
        out_shape=(
            jax.ShapeDtypeStruct((H, 2 * PS, D), bf16),
            jax.ShapeDtypeStruct((tokens, D), f32),
        ),
        compiler_params=params(),
        cost_estimate=cost(12),
        name="early_grad",
    )(dgate, result, nx, go, wg)


def intra_back_kernel(
    v_ref, do_ref, rows_ref, st_ref, sa_ref, sb_ref, k4_ref, dv_ref, rc_ref, dk_ref, dos_scr
):
    lower, upper = causal_masks()
    kf_cols = jnp.transpose(rows_ref[KF])
    kr_cols = jnp.transpose(rows_ref[KR])
    score_grad = jnp.zeros((BL, BL), f32)
    for pair in range(H // 2):
        span = slice(pair * 2 * PS, (pair + 1) * 2 * PS)
        grads = pair_blocks(do_ref[span, :])
        mat_grads = tn(v_ref[span, :], grads)
        down = []
        over = []
        for i, h in enumerate((2 * pair, 2 * pair + 1)):
            gap = jnp.where(
                lower,
                rows_ref[LQ, h : h + 1, :] - kf_cols[:, h : h + 1],
                rows_ref[RQ, h : h + 1, :] - kr_cols[:, h : h + 1],
            )
            decay = jnp.exp(jnp.minimum(gap, 80.0))
            mat = decay * st_ref[0]
            term = decay * mat_grads[:, i * BL : (i + 1) * BL]
            score_grad = score_grad + term
            flow = term * st_ref[0]
            flow_f = jnp.where(lower, flow, 0.0)
            row_f = jnp.sum(flow_f, axis=0, keepdims=True)
            row_all = jnp.sum(flow, axis=0, keepdims=True)
            rc_ref[0, h : h + 1, :] = row_f
            rc_ref[1, h : h + 1, :] = row_all - row_f
            down.append(jnp.where(lower, mat, 0.0).astype(bf16))
            over.append(jnp.where(lower, 0.0, mat).astype(bf16))
        dv_f = nt(grads, jnp.concatenate(down, axis=1))
        dv_r = nt(grads, jnp.concatenate(over, axis=1))
        vals = v_ref[span, :].astype(f32)
        for i, h in enumerate((2 * pair, 2 * pair + 1)):
            half = slice(i * PS, (i + 1) * PS)
            rc_ref[2, h : h + 1, :] = jnp.sum(vals[half] * dv_f[half], axis=0, keepdims=True)
            rc_ref[3, h : h + 1, :] = jnp.sum(vals[half] * dv_r[half], axis=0, keepdims=True)
        dv_ref[span, :] = (dv_f + dv_r).astype(dv_ref.dtype)
    grad_f = jnp.where(lower, score_grad, 0.0).astype(bf16)
    grad_r = jnp.where(upper, score_grad, 0.0).astype(bf16)
    b_f = k4_ref[:NS, :]
    c_f = k4_ref[NS : 2 * NS, :]
    b_r = k4_ref[2 * NS : 3 * NS, :]
    c_r = k4_ref[3 * NS :, :]
    for h in range(H):
        span = slice(h * PS, (h + 1) * PS)
        grad = do_ref[span, :].astype(f32)
        dos_scr[span, :BL] = (grad * rows_ref[EF, h : h + 1, :]).astype(bf16)
        dos_scr[span, BL:] = (grad * rows_ref[ER, h : h + 1, :]).astype(bf16)
    cross_f = tn(sa_ref[0], dos_scr[:, :BL])
    cross_r = tn(sb_ref[0], dos_scr[:, BL:])
    dk_ref[:NS, :] = nt(c_f, grad_f)
    dk_ref[NS : 2 * NS, :] = nn(b_f, grad_f) + cross_f[:NS]
    dk_ref[2 * NS : 3 * NS, :] = nt(c_r, grad_r)
    dk_ref[3 * NS :, :] = nn(b_r, grad_r) + cross_r[NS:]


def intra_back_stage(v, do, rows, scores, s9, k4):
    tokens = v.shape[1]
    chan = pl.BlockSpec((CH, BL), lambda b: (0, b))
    return pl.pallas_call(
        intra_back_kernel,
        grid=(tokens // BL,),
        in_specs=[
            chan,
            chan,
            pl.BlockSpec((KINDS, H, BL), lambda b: (0, 0, b)),
            pl.BlockSpec((1, BL, BL), lambda b: (b, 0, 0)),
            pl.BlockSpec((1, CH, BL), lambda b: (b, 0, 0)),
            pl.BlockSpec((1, CH, BL), lambda b: (b + 1, 0, 0)),
            pl.BlockSpec((4 * NS, BL), lambda b: (0, b)),
        ],
        out_specs=[
            chan,
            pl.BlockSpec((4, H, BL), lambda b: (0, 0, b)),
            pl.BlockSpec((4 * NS, BL), lambda b: (0, b)),
        ],
        out_shape=(
            jax.ShapeDtypeStruct((CH, tokens), bf16),
            jax.ShapeDtypeStruct((4, H, tokens), f32),
            jax.ShapeDtypeStruct((4 * NS, tokens), f32),
        ),
        scratch_shapes=[pltpu.VMEM((CH, 2 * BL), bf16)],
        compiler_params=params(),
        cost_estimate=cost(18),
        name="intra_back",
    )(v, do, rows, scores, s9, s9, k4)


def cross_back_kernel(
    dvi_ref, v_ref, do_ref, u_ref, dsa_ref, dsb_ref, k4_ref, rows_ref, rci_ref, rcc_ref,
    xa_ref, xb_ref, dki_ref, cols_ref, after_ref,
    dpre_ref, dx_ref, dk_ref,
    f_scr, r_scr, lhs_scr, c_scr,
):
    b_f = k4_ref[:NS, :]
    b_r = k4_ref[2 * NS : 3 * NS, :]
    zero = jnp.zeros_like(b_f)
    f_scr[...] = nn(dsb_ref[0], jnp.concatenate([b_f, zero], axis=0))
    r_scr[...] = nn(dsa_ref[0], jnp.concatenate([zero, b_r], axis=0))
    for h in range(H):
        span = slice(h * PS, (h + 1) * PS)
        vals = v_ref[span, :].astype(f32)
        w_f = rows_ref[WF, h : h + 1, :]
        w_r = rows_ref[WR, h : h + 1, :]
        dv_f = f_scr[span, :] * w_f
        dv_r = r_scr[span, :] * w_r
        c_scr[0, h : h + 1, :] = jnp.sum(vals * dv_f, axis=0, keepdims=True)
        c_scr[1, h : h + 1, :] = jnp.sum(vals * dv_r, axis=0, keepdims=True)
        lhs_scr[span, :BL] = (vals * w_f).astype(bf16)
        lhs_scr[span, BL:] = (vals * w_r).astype(bf16)
        grad = (
            dvi_ref[span, :].astype(f32)
            + dv_f
            + dv_r
            + cols_ref[span, 1:2] * do_ref[span, :].astype(f32)
        )
        pre = u_ref[span, :].astype(f32)
        soft = sigmoid(pre)
        dpre_ref[span, :] = (grad * (soft * (1.0 + pre * (1.0 - soft)))).astype(dpre_ref.dtype)
    db_f = tn(dsb_ref[0], lhs_scr[:, :BL])
    db_r = tn(dsa_ref[0], lhs_scr[:, BL:])
    dk_ref[...] = dki_ref[...]
    dk_ref[:NS, :] += db_f[:NS]
    dk_ref[2 * NS : 3 * NS, :] += db_r[NS:]
    first = lane_first((H, BL))
    through_f = jnp.sum(jnp.where(first, xb_ref[0], 0.0), axis=1, keepdims=True)
    through_r = jnp.sum(jnp.where(first, 0.0, xa_ref[0]), axis=1, keepdims=True)
    row_f = rci_ref[0] + rcc_ref[0]
    row_r = rci_ref[1] + rcc_ref[1]
    col_f = rci_ref[2] + c_scr[0]
    col_r = rci_ref[3] + c_scr[1]
    after = after_ref[...]
    strict = lax.Precision.HIGHEST
    sum_f = nn(row_f, after, strict) - nn(col_f, after, strict) - col_f + through_f
    sum_r = nt(row_r, after, strict) - nt(col_r, after, strict) - col_r + through_r
    for kind, (total, col, x_kind, r_kind) in enumerate(
        ((sum_f, col_f, XF, RF), (sum_r, col_r, XR, RR))
    ):
        soft = sigmoid(rows_ref[x_kind])
        rate = rows_ref[r_kind]
        live = rate > 0.0
        ratio = jnp.where(live, soft / jnp.where(live, rate, 1.0), 1.0)
        dx_ref[kind] = col * ratio - total * soft


def cross_back_stage(dvi, v, do, u, ds9, k4, rows, rci, rcc, x9, dki, cols, after):
    tokens = v.shape[1]
    chan = pl.BlockSpec((CH, BL), lambda b: (0, b))
    keys = pl.BlockSpec((4 * NS, BL), lambda b: (0, b))
    return pl.pallas_call(
        cross_back_kernel,
        grid=(tokens // BL,),
        in_specs=[
            chan,
            chan,
            chan,
            chan,
            pl.BlockSpec((1, CH, BL), lambda b: (b, 0, 0)),
            pl.BlockSpec((1, CH, BL), lambda b: (b + 1, 0, 0)),
            keys,
            pl.BlockSpec((KINDS, H, BL), lambda b: (0, 0, b)),
            pl.BlockSpec((4, H, BL), lambda b: (0, 0, b)),
            pl.BlockSpec((2, H, BL), lambda b: (0, 0, b)),
            pl.BlockSpec((1, H, BL), lambda b: (b, 0, 0)),
            pl.BlockSpec((1, H, BL), lambda b: (b + 1, 0, 0)),
            keys,
            pl.BlockSpec((CH, 8), lambda b: (0, 0)),
            pl.BlockSpec((BL, BL), lambda b: (0, 0)),
        ],
        out_specs=[chan, pl.BlockSpec((2, H, BL), lambda b: (0, 0, b)), keys],
        out_shape=(
            jax.ShapeDtypeStruct((CH, tokens), bf16),
            jax.ShapeDtypeStruct((2, H, tokens), f32),
            jax.ShapeDtypeStruct((4 * NS, tokens), f32),
        ),
        scratch_shapes=[
            pltpu.VMEM((CH, BL), f32),
            pltpu.VMEM((CH, BL), f32),
            pltpu.VMEM((CH, 2 * BL), bf16),
            pltpu.VMEM((2, H, BL), f32),
        ],
        compiler_params=params(),
        cost_estimate=cost(16),
        name="cross_back",
    )(dvi, v, do, u, ds9, ds9, k4, rows, rci, rcc, x9, x9, dki, cols, after)


def key_pre_kernel(dk_ref, u_ref, edge_ref, out_ref):
    tokens = u_ref.shape[1]
    lane = lax.broadcasted_iota(jnp.int32, (NS, tokens), 1)
    d_cf = pltpu.roll(dk_ref[NS : 2 * NS, :], tokens - 1, axis=1)
    d_cf = jnp.where(lane == tokens - 1, edge_ref[:, 0:1], d_cf)
    d_cr = pltpu.roll(dk_ref[3 * NS :, :], 1, axis=1)
    d_cr = jnp.where(lane == 0, edge_ref[:, 1:2], d_cr)
    grad = jnp.concatenate([dk_ref[:NS, :], d_cf, dk_ref[2 * NS : 3 * NS, :], d_cr], axis=0)
    pre = u_ref[...]
    soft = sigmoid(pre)
    out_ref[...] = grad * (soft * (1.0 + pre * (1.0 - soft)))


def key_pre_stage(dk, u, edge):
    return pl.pallas_call(
        key_pre_kernel,
        out_shape=jax.ShapeDtypeStruct(u.shape, f32),
        compiler_params=pltpu.CompilerParams(vmem_limit_bytes=56 * 1024 * 1024),
        cost_estimate=cost(3),
        name="key_pre",
    )(dk, u, edge)


def conv_back_rows(dpre, taps, signal):
    rows, tokens = dpre.shape
    ext = signal.shape[1]
    wide = jnp.concatenate([dpre, jnp.zeros((rows, ext - tokens), f32)], axis=1)
    total = None
    sums = []
    for k in range(K):
        shift = (k - K // 2) % ext
        moved = wide if shift == 0 else pltpu.roll(wide, shift, axis=1)
        term = moved * taps[:, k : k + 1]
        total = term if total is None else total + term
        prod = moved * signal
        part = prod[:, :BL]
        for b in range(1, ext // BL):
            part = part + prod[:, b * BL : (b + 1) * BL]
        sums.append(part)
    return total, sums


def key_back_kernel(
    meta_ref, dpre_ref, taps_ref, p_ref, nx_ref, w_ref, g_ref, dn_ref, t_ref, low_scr, g_scr
):
    for c in range(4 * NS // 16):
        span = slice(c * 16, (c + 1) * 16)
        total, sums = conv_back_rows(dpre_ref[span, :], taps_ref[span, :], p_ref[span, :])
        low_scr[span, :] = total.astype(bf16)
        for k in range(K):
            t_ref[k, span, :] = sums[k]
    g_scr[...] = nn(low_scr[...], nx_ref[...])
    count, rows, _ = g_ref.shape
    for q in range(count):
        start = pl.multiple_of(meta_ref[2 + q] * rows, 8)
        g_ref[q] = g_scr[pl.ds(start, rows), :].astype(g_ref.dtype)
    dn_ref[...] = tn(low_scr[...], w_ref[...])


def key_back_stage(meta, dpre, taps, proj, nx, key_low):
    ext = nx.shape[0]
    count = meta.shape[0] - 2
    args = (dpre, taps, proj, nx, key_low)
    outs = (
        jax.ShapeDtypeStruct((count, 4 * NS // count, D), bf16),
        jax.ShapeDtypeStruct((ext, D), f32),
        jax.ShapeDtypeStruct((K, 4 * NS, BL), f32),
    )

    def whole(shape):
        return pl.BlockSpec(shape, lambda i, meta: (0,) * len(shape))

    return pl.pallas_call(
        key_back_kernel,
        grid_spec=pltpu.PrefetchScalarGridSpec(
            num_scalar_prefetch=1,
            grid=(1,),
            in_specs=[whole(x.shape) for x in args],
            out_specs=[whole(x.shape) for x in outs],
            scratch_shapes=[pltpu.VMEM((4 * NS, ext), bf16), pltpu.VMEM((4 * NS, D), f32)],
        ),
        out_shape=outs,
        compiler_params=params(),
        cost_estimate=cost(8),
        name="key_back",
    )(meta, *args)


def value_back_kernel(
    dpre_ref, taps_ref, s_ref, dx_ref, nx_ref, wv_ref, g_ref, dn_ref, t_ref, low_scr, tap_scr
):
    tokens = dpre_ref.shape[1]
    ext = s_ref.shape[1]
    step = pl.program_id(0)
    for h in range(GH):
        for c in range(PS // 16):
            src = h * PS + c * 16
            span = slice(src, src + 16)
            total, sums = conv_back_rows(
                dpre_ref[span, :].astype(f32), taps_ref[span, :], s_ref[span, :].astype(f32)
            )
            low_scr[h * WV + c * 16 : h * WV + (c + 1) * 16, :] = total.astype(bf16)
            for k in range(K):
                tap_scr[k, span, :] = sums[k]
        tail = jnp.concatenate(
            [
                dx_ref[0, h : h + 1, :],
                dx_ref[1, h : h + 1, :],
                jnp.zeros((14, tokens), f32),
            ],
            axis=0,
        )
        low_scr[h * WV + PS : (h + 1) * WV, :tokens] = tail.astype(bf16)
        low_scr[h * WV + PS : (h + 1) * WV, tokens:] = jnp.zeros((16, ext - tokens), bf16)
    ones = jnp.ones((8, BL), f32)
    for k in range(K):
        t_ref[0, k : k + 1, :] = nt(ones, tap_scr[k], lax.Precision.HIGHEST)[:1]
    t_ref[0, K : K + 1, :] = jnp.zeros((1, GH * PS), f32)
    g_ref[...] = nn(low_scr[...], nx_ref[...]).reshape(GH, WV, D).astype(g_ref.dtype)
    part = tn(low_scr[...], wv_ref[...].reshape(GH * WV, D))

    @pl.when(step == 0)
    def _():
        dn_ref[...] = part

    @pl.when(step > 0)
    def _():
        dn_ref[...] += part


def value_back_stage(dpre, taps, s, dx, nx, wv):
    tokens = dpre.shape[1]
    ext = nx.shape[0]
    rows = GH * PS
    return pl.pallas_call(
        value_back_kernel,
        grid=(NG,),
        in_specs=[
            pl.BlockSpec((rows, tokens), lambda g: (g, 0)),
            pl.BlockSpec((rows, 8), lambda g: (g, 0)),
            pl.BlockSpec((rows, ext), lambda g: (g, 0)),
            pl.BlockSpec((2, GH, tokens), lambda g: (0, g, 0)),
            pl.BlockSpec((ext, D), lambda g: (0, 0), pipeline_mode=pl.Buffered(1)),
            pl.BlockSpec((GH, WV, D), lambda g: (g, 0, 0)),
        ],
        out_specs=[
            pl.BlockSpec((GH, WV, D), lambda g: (g, 0, 0)),
            pl.BlockSpec((ext, D), lambda g: (0, 0)),
            pl.BlockSpec((1, 8, rows), lambda g: (g, 0, 0)),
        ],
        out_shape=(
            jax.ShapeDtypeStruct((H, WV, D), bf16),
            jax.ShapeDtypeStruct((ext, D), f32),
            jax.ShapeDtypeStruct((NG, 8, rows), f32),
        ),
        scratch_shapes=[
            pltpu.VMEM((GH * WV, ext), bf16),
            pltpu.VMEM((K, rows, BL), f32),
        ],
        compiler_params=params(),
        cost_estimate=cost(27),
        name="value_back",
    )(dpre, taps, s, dx, nx, wv)


def pick(sources, index):
    count = index.shape[0]
    rows, width = sources[0].shape[1:]

    def body(index_ref, *refs):
        out_ref = refs[-1]
        for i in range(count):
            first = 0
            for ref in refs[:-1]:
                n = ref.shape[0]
                local = index_ref[i] - first

                @pl.when((local >= 0) & (local < n))
                def _(ref=ref, local=local, i=i):
                    out_ref[i] = ref[local]

                first += n

    return pl.pallas_call(
        body,
        grid_spec=pltpu.PrefetchScalarGridSpec(
            num_scalar_prefetch=1,
            grid=(1,),
            in_specs=[pl.BlockSpec(x.shape, lambda i, index: (0, 0, 0)) for x in sources],
            out_specs=pl.BlockSpec((count, rows, width), lambda i, index: (0, 0, 0)),
        ),
        out_shape=jax.ShapeDtypeStruct((count, rows, width), sources[0].dtype),
        compiler_params=params(),
        cost_estimate=cost(3),
        name="pick",
    )(index, *sources)


def pick_two_kernel(index_ref, slots_ref, gate_ref, out_ref):
    for h in range(H):
        gate_ref[h] = slots_ref[index_ref[h], :PS, :]
        out_ref[h] = slots_ref[index_ref[h], PS:, :]


def pick_two(slots, index):
    half = jax.ShapeDtypeStruct((H, PS, D), slots.dtype)
    return pl.pallas_call(
        pick_two_kernel,
        grid_spec=pltpu.PrefetchScalarGridSpec(
            num_scalar_prefetch=1,
            grid=(1,),
            in_specs=[pl.BlockSpec(slots.shape, lambda i, index: (0, 0, 0))],
            out_specs=[pl.BlockSpec((H, PS, D), lambda i, index: (0, 0, 0))] * 2,
        ),
        out_shape=(half, half),
        compiler_params=params(),
        cost_estimate=cost(6),
        name="pick_two",
    )(index, slots)


def deal(source, index, live, target=None, extra=None, single=None, joined=0):
    count = index.shape[0]
    rows, width = source.shape[1:]
    more = 0 if extra is None else extra.shape[0] // count
    plan = [index, live] if extra is None else [index, live, target]
    args = [source] if extra is None else [source, extra, single]

    def body(*refs):
        index_ref, live_ref = refs[:2]
        source_ref = refs[len(plan)]
        outs = refs[len(plan) + len(args) :]
        for k in range(count):
            value = source_ref[index_ref[k]]
            value = jnp.where(live_ref[k] > 0, value, jnp.zeros_like(value))
            if joined:
                outs[k // joined][k % joined] = value
            elif more:
                start = pl.multiple_of(refs[2][k] * more, 8)
                last = refs[len(plan) + 1][pl.ds(start, more), :]
                one = refs[len(plan) + 2][pl.ds(refs[2][k], 1), :]
                space = jnp.zeros((16 - more - 1, width), f32)
                last = jnp.concatenate([space, one, last], axis=0)
                outs[k][: rows - 16] = value[: rows - 16]
                outs[k][rows - 16 :] = (value[rows - 16 :].astype(f32) + last).astype(bf16)
            else:
                outs[k][...] = value

    def whole(shape):
        return pl.BlockSpec(shape, lambda i, *plan: (0,) * len(shape))

    if joined:
        shapes = [jax.ShapeDtypeStruct((joined, rows, width), source.dtype)] * (count // joined)
    else:
        shapes = [jax.ShapeDtypeStruct((rows, width), source.dtype)] * count
    return pl.pallas_call(
        body,
        grid_spec=pltpu.PrefetchScalarGridSpec(
            num_scalar_prefetch=len(plan),
            grid=(1,),
            in_specs=[whole(x.shape) for x in args],
            out_specs=[whole(x.shape) for x in shapes],
        ),
        out_shape=shapes,
        compiler_params=params(),
        cost_estimate=cost(3),
        name="deal",
    )(*plan, *args)


def adamw_update(weight, gradient, first_moment, second, average, step_rate):
    first_new = BETA_ONE * first_moment + (1.0 - BETA_ONE) * gradient
    second_new = BETA_TWO * second + (1.0 - BETA_TWO) * gradient * gradient
    correct_one = 1.0 - BETA_ONE**STEP
    correct_two = 1.0 - BETA_TWO**STEP
    normalized = first_new / correct_one / (jnp.sqrt(second_new / correct_two) + ADAM_EPS)
    weight_new = weight - step_rate * (normalized + WEIGHT_DECAY * weight)
    average_new = AVERAGE_KEEP * average + (1.0 - AVERAGE_KEEP) * weight_new
    return (weight_new, first_new, second_new, average_new)


def finish_kernel(
    code_ref, share_ref, w_ref, m_ref, v_ref, a_ref,
    w_out, m_out, v_out, a_out, small_ref, gain_ref, scr,
):
    count, rows, _ = share_ref.shape
    keys = 4 * NS // count
    total = jnp.zeros((1, D), f32)
    for i in range(count):
        share = share_ref[code_ref[i]].astype(f32)
        scr[i * keys : (i + 1) * keys, :] = share[rows - keys :]
        small_ref[i : i + 1, :] = share[rows - keys - 1 : rows - keys]
        total = total + share[:1]
    gain_ref[...] = jnp.broadcast_to(total, (8, D))
    new = adamw_update(
        w_ref[...], jnp.transpose(scr[...]), m_ref[...], v_ref[...], a_ref[...], MATRIX_RATE
    )
    for out, value in zip((w_out, m_out, v_out, a_out), new):
        out[...] = value


def finish_stage(code, shares, weight, first, second, ema):
    count = shares.shape[0]
    args = (shares, weight, first, second, ema)
    outs = [jax.ShapeDtypeStruct(weight.shape, f32)] * 4 + [
        jax.ShapeDtypeStruct((count, D), f32),
        jax.ShapeDtypeStruct((8, D), f32),
    ]

    def whole(shape):
        return pl.BlockSpec(shape, lambda i, code: (0,) * len(shape))

    return pl.pallas_call(
        finish_kernel,
        grid_spec=pltpu.PrefetchScalarGridSpec(
            num_scalar_prefetch=1,
            grid=(1,),
            in_specs=[whole(x.shape) for x in args],
            out_specs=[whole(x.shape) for x in outs],
            scratch_shapes=[pltpu.VMEM((4 * NS, D), f32)],
        ),
        out_shape=outs,
        compiler_params=params(),
        cost_estimate=cost(5),
        name="finish_stage",
    )(code, *args)


def make_local(n_dp, n_mp):
    per = H // n_mp
    direct = n_mp == 4 and n_dp == 8

    def swap(x, axis, size, bit):
        return lax.ppermute(x, axis, [(i, i ^ bit) for i in range(size)])

    def head_rows(mp_index):
        rows = jnp.arange(n_mp, dtype=jnp.int32)
        return jnp.bitwise_xor(rows, mp_index) if direct else rows

    def over_mp(x):
        if direct:
            far = swap(x, "mp", n_mp, 2)
            return [x, swap(x, "mp", n_mp, 1), far, swap(far, "mp", n_mp, 1)]
        copies = lax.all_gather(x, "mp", axis=0)
        return [copies[k] for k in range(n_mp)]

    def gather_dp(part):
        return [part[None]] + [swap(part, "dp", n_dp, k)[None] for k in range(1, n_dp)]

    def pick_own(pieces, owners, dp_index):
        return pick(pieces, jnp.bitwise_xor(owners, dp_index))

    def scatter_mp(grads):
        got = swap(jnp.stack([grads[1], grads[3]]), "mp", n_mp, 1)
        away = (grads[2].astype(f32) + got[1].astype(f32)).astype(bf16)
        mine = grads[0].astype(f32) + got[0].astype(f32)
        return mine + swap(away, "mp", n_mp, 2).astype(f32)

    def deal_targets(owners, targets):
        match = targets[:, None] == owners[None, :]
        return jnp.argmax(match, axis=1).astype(jnp.int32), jnp.any(match, axis=1).astype(jnp.int32)

    def gather_all(x, mp_index, dp_index):
        both = x[None]
        for axis, size, bit in (
            ("dp", n_dp, 2), ("dp", n_dp, 4), ("dp", n_dp, 1), ("mp", n_mp, 2), ("mp", n_mp, 1)
        ):
            both = jnp.concatenate([both, swap(both, axis, size, bit)], axis=0)
        far = jnp.bitwise_xor(jnp.arange(n_mp, dtype=jnp.int32), mp_index)[:, None]
        off = jnp.bitwise_xor(jnp.arange(n_dp, dtype=jnp.int32), dp_index)[None, :]
        code = ((off >> 1) & 3) + 4 * (off & 1) + 8 * (far >> 1) + 16 * (far & 1)
        return both, code.reshape(-1)

    def local(
        hidden_in, out_grad, seq_len, owner_list,
        block_master, block_first, block_second, block_ema,
        head_small, head_first, head_second, head_ema,
        bc_weight, bc_first, bc_second, bc_ema,
        shared_small, shared_first, shared_second, shared_ema,
    ):
        tokens = hidden_in.shape[0]
        mp_index = lax.axis_index("mp")
        dp_index = lax.axis_index("dp")
        owners = lax.dynamic_slice_in_dim(owner_list, mp_index * per, per)
        order = head_rows(mp_index)
        bounds = (mp_index + jnp.arange(2, dtype=jnp.int32)) * tokens % seq_len == 0
        starts = bounds[:1].reshape(1, 1)
        ends = bounds[1:].reshape(1, 1)
        meta = jnp.concatenate([mp_index.reshape(1), seq_len, order]).astype(jnp.int32)
        nexts = [(i, i + 1) for i in range(n_mp - 1)]
        prevs = [(i + 1, i) for i in range(n_mp - 1)]

        slot_t = jnp.transpose(block_master[0, 0]).astype(bf16)
        part_v = jnp.concatenate(
            [slot_t[PS : 2 * PS + 2], jnp.zeros((WV - PS - 2, D), bf16)], axis=0
        )
        part_go = jnp.concatenate([slot_t[:PS], slot_t[2 * PS + 2 :]], axis=0)
        if direct:
            pieces_v = gather_dp(part_v)
            mine_v = pick_own(pieces_v, owners, dp_index)
            far_v = swap(mine_v, "mp", n_mp, 2)
            near_v = swap(mine_v, "mp", n_mp, 1)
            slots = lax.all_gather(part_go, ("mp", "dp"), axis=0)
            rows_of = jnp.repeat(order, per)
            heads_of = rows_of * per + jnp.arange(H, dtype=jnp.int32) % per
            wg, wo = pick_two(slots, rows_of * n_dp + jnp.take(owner_list, heads_of))
        else:
            mine_v = pick([lax.all_gather(part_v, "dp", axis=0)], owners)
            wv = jnp.concatenate(over_mp(mine_v), axis=0)
            mine_go = pick([lax.all_gather(part_go, "dp", axis=0)], owners)
            all_go = over_mp(mine_go)
            wg = jnp.concatenate([x[:, :PS] for x in all_go], axis=0)
            wo = jnp.concatenate([x[:, PS:] for x in all_go], axis=0)
        wg = wg.reshape(CH, D)
        wo = wo.reshape(CH, D)

        hidden = hidden_in.astype(f32)
        gain_in = shared_small[K:].reshape(D)
        scale_in = lax.rsqrt(jnp.mean(hidden * hidden, axis=1, keepdims=True) + NORM_EPS)
        normed = (hidden * scale_in * gain_in).astype(bf16)
        from_left = lax.ppermute(normed[-HALO:], "mp", nexts)
        from_right = lax.ppermute(normed[:HALO], "mp", prevs)
        from_left = jnp.where(starts, jnp.zeros_like(from_left), from_left)
        from_right = jnp.where(ends, jnp.zeros_like(from_right), from_right)
        nx = jnp.concatenate(
            [normed, from_right, jnp.zeros((PAD - 2 * HALO, D), bf16), from_left], axis=0
        )

        heads = jnp.concatenate(over_mp(head_small), axis=0)
        taps_v = jnp.transpose(heads[:, 1 : 1 + K, :], (0, 2, 1)).reshape(CH, K)
        taps_v = jnp.pad(taps_v, ((0, 0), (0, 1)))
        cols = jnp.stack([heads[:, 0].reshape(CH), heads[:, K + 1].reshape(CH)], axis=1)
        cols = jnp.pad(cols, ((0, 0), (0, 6)))
        bias = heads[:, K + 2, :2]
        key_low = jnp.transpose(bc_weight).astype(bf16)
        taps_k = jnp.pad(jnp.transpose(shared_small[:K]), ((0, 0), (0, 1)))
        ids = jnp.arange(BL)
        tri = (ids[:, None] <= ids[None, :]).astype(f32)
        after = (ids[:, None] > ids[None, :]).astype(f32)

        key_proj, key_u, k4, scores = key_stage(nx, key_low, taps_k, tokens)
        if direct:
            far_v, k4 = lax.optimization_barrier((far_v, k4))
            wv = jnp.concatenate([mine_v, near_v, far_v, swap(far_v, "mp", n_mp, 1)], axis=0)
        v, u, s, rows, tot, sblk, sdev, tdev = value_stage(
            nx, wv, taps_v, bias, k4, tri, tokens
        )
        tot_hi = lax.reduce_precision(tdev, 8, 7)
        tot_mid = lax.reduce_precision(tdev - tot_hi, 8, 7)
        tot_low = tdev - tot_hi - tot_mid
        message = jnp.concatenate(
            [sdev, tot_hi.astype(bf16), tot_mid.astype(bf16), tot_low.astype(bf16)], axis=0
        )
        def twist(k, q):
            return q ^ k if direct else q

        o_intra = intra_stage(v, rows, scores)
        if direct:
            far = swap(message, "mp", n_mp, 2)
            near = swap(message, "mp", n_mp, 1)
            far, o_intra = lax.optimization_barrier((far, o_intra))
            messages = [message, near, far, swap(far, "mp", n_mp, 1)]
        else:
            messages = over_mp(message)
        far_tot = jnp.stack([x[CH:] for x in messages]).astype(f32)

        (s9,) = chain_stage(meta, sblk, tot, far_tot, messages, twist, tokens)
        hidden_out, result_t, dgate_t, do_t, dsblk, dsdev, rcc, small_mid = token_stage(
            o_intra, v, s9, k4, rows, tot, wg, wo, nx, hidden_in, out_grad, cols
        )
        if direct:
            far_d = swap(dsdev, "mp", n_mp, 2)
            near_d = swap(dsdev, "mp", n_mp, 1)
        grad_go, dn_gate = early_grad_stage(dgate_t, result_t, nx, out_grad, wg)
        grad_go = grad_go.reshape(n_mp, per * 2 * PS, D)
        if direct:
            got = swap(jnp.stack([grad_go[1], grad_go[3]]), "mp", n_mp, 1)
            away = (grad_go[2].astype(f32) + got[1].astype(f32)).astype(bf16)
            far_go = swap(away, "mp", n_mp, 2)
            do_back, away, far_d = lax.optimization_barrier((do_t, away, far_d))
        else:
            do_back = do_t
        dvi, rci, dki = intra_back_stage(v, do_back, rows, scores, s9, k4)
        to_prev = lax.ppermute(dki[NS : 2 * NS, :1].reshape(1, NS), "mp", prevs)
        to_next = lax.ppermute(dki[3 * NS :, tokens - 1 :].reshape(1, NS), "mp", nexts)
        if direct:
            messages = [dsdev, near_d, far_d, swap(far_d, "mp", n_mp, 1)]
        else:
            messages = over_mp(dsdev)
        natural = jnp.arange(n_dp, dtype=jnp.int32)
        if direct:
            far_go, dvi = lax.optimization_barrier((far_go, dvi))
            mine_go = grad_go[0].astype(f32) + got[0].astype(f32) + far_go.astype(f32)
            mine_go = mine_go.astype(bf16)
        else:
            mine_go = lax.psum_scatter(grad_go, "mp", scatter_dimension=0, tiled=True)[0]
        if direct:
            bits = jnp.arange(n_dp, dtype=jnp.int32)
            bits = (bits >> 2) + 4 * ((bits >> 1) & 1) + 2 * (bits & 1)
            keep_go, send_go = deal(
                mine_go.reshape(per, 2 * PS, D),
                *deal_targets(owners, jnp.bitwise_xor(bits, dp_index)),
                joined=n_dp // 2,
            )
            keep_go, dvi = lax.optimization_barrier((keep_go, dvi))
            keep_go = keep_go.astype(f32) + swap(send_go, "dp", n_dp, 1).astype(f32)
        else:
            (dealt,) = deal(
                mine_go.reshape(per, 2 * PS, D), *deal_targets(owners, natural), joined=n_dp
            )
            own_go = lax.psum_scatter(dealt, "dp", scatter_dimension=0, tiled=True)[0]
        ds9, x9 = chain_stage(meta, dsblk, tot, far_tot, messages, twist, tokens, s9)
        dpre, dx, dk = cross_back_stage(
            dvi, v, do_t, u, ds9, k4, rows, rci, rcc, x9, dki, cols, after
        )
        if direct:
            keep_go, dpre, dk = lax.optimization_barrier((keep_go, dpre, dk))
            far_go = swap(keep_go[2:].astype(bf16), "dp", n_dp, 4)
        d_last, d_first = to_prev, to_next
        d_last = jnp.where(ends, 0.0, d_last)
        d_first = jnp.where(starts, 0.0, d_first)
        edge = jnp.transpose(jnp.concatenate([d_last, d_first, jnp.zeros((6, NS), f32)], axis=0))
        dpre_k = key_pre_stage(dk, key_u, edge)
        grad_v, dn_value, tap_v = value_back_stage(dpre, taps_v, s, dx, nx, wv)
        if direct:
            far_go, dpre_k, dn_value = lax.optimization_barrier((far_go, dpre_k, dn_value))
            keep_go = keep_go[:2] + far_go.astype(f32)
            own_go = keep_go[0] + swap(keep_go[1].astype(bf16), "dp", n_dp, 2).astype(f32)
        grad_key, dn_key, tap_key = key_back_stage(meta, dpre_k, taps_k, key_proj, nx, key_low)
        head_grad = jnp.concatenate(
            [
                small_mid[0, 0].reshape(H, 1, PS),
                jnp.transpose(
                    tap_v.reshape(NG, 8, GH, PS)[:, :K], (0, 2, 1, 3)
                ).reshape(H, K, PS),
                small_mid[1, 0].reshape(H, 1, PS),
                jnp.pad(jnp.transpose(jnp.sum(dx, axis=2)), ((0, 0), (0, PS - 2))).reshape(
                    H, 1, PS
                ),
            ],
            axis=1,
        )
        if direct:
            head_grad = jnp.take(head_grad.reshape(n_mp, per, 10, PS), order, axis=0)
        small_grad = jnp.concatenate(
            [head_grad.reshape(-1), jnp.sum(tap_key, axis=2).reshape(-1)]
        )
        count = small_grad.shape[0]

        if direct:
            rows_key = (4 * NS) // (n_mp * n_dp)
            small_rows = jnp.pad(small_grad, (0, n_mp * n_dp * D - count)).reshape(n_mp, n_dp, D)
            small_rows = jnp.take(small_rows, order, axis=0).astype(bf16)
            both = jnp.concatenate([grad_v.reshape(n_mp, per * WV, D), grad_key, small_rows], axis=1)
            mine_v = scatter_mp(both)
            mine_v, own_go = lax.optimization_barrier((mine_v, own_go))
            targets = jnp.bitwise_xor(natural, dp_index)
            dealt = deal(
                mine_v[: per * WV].astype(bf16).reshape(per, WV, D),
                *deal_targets(owners, targets),
                targets,
                mine_v[per * WV : per * WV + n_dp * rows_key],
                mine_v[per * WV + n_dp * rows_key :],
            )
            own_v = dealt[0].astype(f32)
            for k in range(1, n_dp):
                own_v = own_v + swap(dealt[k], "dp", n_dp, k).astype(f32)
        else:
            mine_v = lax.psum_scatter(
                grad_v.reshape(n_mp, per * WV, D), "mp", scatter_dimension=0, tiled=True
            )[0]
            (dealt,) = deal(
                mine_v.reshape(per, WV, D), *deal_targets(owners, natural), joined=n_dp
            )
            own_v = lax.psum_scatter(dealt, "dp", scatter_dimension=0, tiled=True)[0].astype(f32)

        dn_ext = dn_key + dn_value
        halo_l = lax.ppermute(dn_ext[tokens : tokens + HALO], "mp", nexts)
        halo_r = lax.ppermute(dn_ext[-HALO:], "mp", prevs)
        halo_l = jnp.where(starts, 0.0, halo_l)
        halo_r = jnp.where(ends, 0.0, halo_r)
        edges = jnp.concatenate([halo_l, jnp.zeros((tokens - 2 * HALO, D), f32), halo_r], axis=0)
        dnormed = dn_gate + dn_ext[:tokens] + edges
        scaled = dnormed * gain_in
        gain_grad = jnp.sum(dnormed * hidden * scale_in, axis=0)
        cross_in = jnp.sum(scaled * hidden, axis=1, keepdims=True)
        hidden_grad = (
            out_grad.astype(f32) + scale_in * scaled - hidden * scale_in**3 * cross_in / D
        )

        if direct:
            share = jnp.concatenate(
                [jnp.broadcast_to(gain_grad, (15 - rows_key, D)), own_v[WV - rows_key - 1 :]],
                axis=0,
            ).astype(bf16)
            shares, code = gather_all(share, mp_index, dp_index)
            *key_new, small_total, gain_total = finish_stage(
                code, shares, bc_weight, bc_first, bc_second, bc_ema
            )
            small_total = small_total.reshape(-1)[:count]
            gain_total = gain_total[0]
        else:
            key_total, small_total, gain_total = lax.psum(
                (grad_key.reshape(4 * NS, D).astype(f32), small_grad, gain_grad), ("dp", "mp")
            )
            key_new = adamw_update(
                bc_weight, jnp.transpose(key_total), bc_first, bc_second, bc_ema, MATRIX_RATE
            )
        own_go = own_go.astype(f32)
        own_grad = jnp.transpose(
            jnp.concatenate([own_go[:PS], own_v[: PS + 2], own_go[PS:]], axis=0)
        )
        own_grad = lax.optimization_barrier(own_grad)
        is_owner = jnp.any(owners == dp_index)
        previous = (block_master[0, 0], block_first[0, 0], block_second[0, 0], block_ema[0, 0])
        slot_new = adamw_update(
            previous[0], own_grad, previous[1], previous[2], previous[3], MATRIX_RATE
        )
        slot_outs = [
            jnp.where(is_owner, renewed, before)[None, None]
            for renewed, before in zip(slot_new, previous)
        ]
        head_total = lax.dynamic_slice_in_dim(
            small_total[: H * 10 * PS].reshape(H, 10, PS), mp_index * per, per
        )
        head_new = adamw_update(
            head_small, head_total, head_first, head_second, head_ema, SMALL_RATE
        )
        shared_total = jnp.concatenate(
            [
                small_total[H * 10 * PS :].reshape(K, 4 * NS),
                gain_total.reshape(-1, 4 * NS),
            ],
            axis=0,
        )
        shared_new = adamw_update(
            shared_small, shared_total, shared_first, shared_second, shared_ema, SMALL_RATE
        )
        return (hidden_out, hidden_grad, *slot_outs, *head_new, *key_new, *shared_new)

    return local


def solution(mesh):
    rows = P(("dp", "mp"), None)
    slot = P("mp", "dp", None, None)
    head = P("mp", None, None)
    return jax.shard_map(
        make_local(mesh.shape["dp"], mesh.shape["mp"]),
        mesh=mesh,
        in_specs=(rows, rows, P("dp"), P()) + (slot,) * 4 + (head,) * 4 + (P(),) * 8,
        out_specs=(rows, rows) + (slot,) * 4 + (head,) * 4 + (P(),) * 8,
        check_vma=False,
    )
```

```python
import jax
import jax.numpy as jnp
from jax import lax
from jax.experimental import pallas as pl
from jax.experimental.pallas import tpu as pltpu
from jax.sharding import PartitionSpec as P

D = 768
H = 24
PS = 64
NS = 64
K = 7
STEP = 3
CH = H * PS
BL = 128
GH = 8
NG = H // GH
WV = 80
PAD = 128
HALO = 8
NORM_EPS = 1e-05
BETA_ONE = 0.5
BETA_TWO = 0.5
ADAM_EPS = 1e-08
WEIGHT_DECAY = 0.1
MATRIX_RATE = 0.04
SMALL_RATE = 0.2
AVERAGE_KEEP = 0.75

f32 = jnp.float32
bf16 = jnp.bfloat16
LQ, RQ, KF, KR, WF, WR, EF, ER, XF, XR, RF, RR = range(12)
KINDS = 12


def params(mb=56):
    return pltpu.CompilerParams(
        dimension_semantics=("arbitrary",), vmem_limit_bytes=mb * 1024 * 1024
    )


def cost(micros):
    return pl.CostEstimate(flops=0, transcendentals=0, bytes_accessed=micros * 1_000_000)


def nt(a, b, precision=None):
    return lax.dot_general(
        a, b, (((1,), (1,)), ((), ())), preferred_element_type=f32, precision=precision
    )


def nn(a, b, precision=None):
    return lax.dot_general(
        a, b, (((1,), (0,)), ((), ())), preferred_element_type=f32, precision=precision
    )


def tn(a, b):
    return lax.dot_general(a, b, (((0,), (0,)), ((), ())), preferred_element_type=f32)


def lane_sums(x):
    ones = jnp.ones((8, x.shape[1]), bf16)
    high = x.astype(bf16)
    rest = (x - high.astype(f32)).astype(bf16)
    return nt(ones, high) + nt(ones, rest)


def sigmoid(v):
    return 1.0 / (1.0 + jnp.exp(-v))


def lane_first(shape):
    return lax.broadcasted_iota(jnp.int32, shape, len(shape) - 1) < NS


def conv_taps(signal, taps, sign):
    ext = signal.shape[1]
    total = None
    for k in range(K):
        shift = (sign * (k - K // 2)) % ext
        moved = signal if shift == 0 else pltpu.roll(signal, shift, axis=1)
        term = moved.astype(f32) * taps[:, k : k + 1]
        total = term if total is None else total + term
    return total


def causal_masks():
    row = lax.broadcasted_iota(jnp.int32, (BL, BL), 0)
    col = lax.broadcasted_iota(jnp.int32, (BL, BL), 1)
    return row < col, row > col


def stacked_keys(a, b):
    zero = jnp.zeros_like(a)
    return jnp.concatenate(
        [jnp.concatenate([a, zero], axis=1), jnp.concatenate([zero, b], axis=1)], axis=0
    )


def key_kernel(nx_ref, w_ref, taps_ref, p_ref, u_ref, k_ref, st_ref):
    tokens = u_ref.shape[1]
    proj = nt(w_ref[...], nx_ref[...])
    pre = conv_taps(proj, taps_ref[...], -1)
    key = pre * sigmoid(pre)
    ext = key.shape[1]
    b_f = key[:NS, :tokens].astype(bf16)
    c_f = pltpu.roll(key[NS : 2 * NS], 1, axis=1)[:, :tokens].astype(bf16)
    b_r = key[2 * NS : 3 * NS, :tokens].astype(bf16)
    c_r = pltpu.roll(key[3 * NS :], ext - 1, axis=1)[:, :tokens].astype(bf16)
    p_ref[...] = proj
    u_ref[...] = pre[:, :tokens]
    k_ref[...] = jnp.concatenate([b_f, c_f, b_r, c_r], axis=0)
    lower, upper = causal_masks()
    for blk in range(tokens // BL):
        part = slice(blk * BL, (blk + 1) * BL)
        s_f = tn(b_f[:, part], c_f[:, part])
        s_r = tn(b_r[:, part], c_r[:, part])
        st_ref[blk] = jnp.where(lower, s_f, jnp.where(upper, s_r, 0.0))


def key_stage(nx, key_low, taps, tokens):
    ext = nx.shape[0]
    blocks = tokens // BL
    return pl.pallas_call(
        key_kernel,
        out_shape=(
            jax.ShapeDtypeStruct((4 * NS, ext), f32),
            jax.ShapeDtypeStruct((4 * NS, tokens), f32),
            jax.ShapeDtypeStruct((4 * NS, tokens), bf16),
            jax.ShapeDtypeStruct((blocks, BL, BL), f32),
        ),
        compiler_params=pltpu.CompilerParams(vmem_limit_bytes=56 * 1024 * 1024),
        cost_estimate=cost(6),
        name="key_stage",
    )(nx, key_low, taps)


def value_kernel(
    nx_ref, wv_ref, taps_ref, bias_ref, k4_ref, tri_ref,
    v_ref, u_ref, s_ref, rows_ref, tot_ref, sblk_ref, sdev_ref, tdev_ref,
    p_scr, lhs_scr,
):
    tokens = v_ref.shape[1]
    blocks = tokens // BL
    p_scr[...] = nt(wv_ref[...].reshape(GH * WV, D), nx_ref[...])
    for h in range(GH):
        for c in range(PS // 16):
            src = h * WV + c * 16
            dst = h * PS + c * 16
            signal = p_scr[src : src + 16, :].astype(bf16)
            pre = conv_taps(signal, taps_ref[dst : dst + 16, :], -1)[:, :tokens]
            s_ref[dst : dst + 16, :] = signal
            u_ref[dst : dst + 16, :] = pre.astype(bf16)
            v_ref[dst : dst + 16, :] = (pre * sigmoid(pre)).astype(bf16)
    x_f = jnp.concatenate(
        [p_scr[h * WV + PS : h * WV + PS + 1, :tokens] for h in range(GH)], axis=0
    )
    x_r = jnp.concatenate(
        [p_scr[h * WV + PS + 1 : h * WV + PS + 2, :tokens] for h in range(GH)], axis=0
    )
    x_f = x_f + bias_ref[:, 0:1]
    x_r = x_r + bias_ref[:, 1:2]
    rate_f = jnp.maximum(x_f, 0.0) + jnp.log1p(jnp.exp(-jnp.abs(x_f)))
    rate_r = jnp.maximum(x_r, 0.0) + jnp.log1p(jnp.exp(-jnp.abs(x_r)))
    rows_ref[XF] = x_f
    rows_ref[XR] = x_r
    rows_ref[RF] = rate_f
    rows_ref[RR] = rate_r
    cuts = [slice(b * BL, (b + 1) * BL) for b in range(blocks)]
    stack = jnp.concatenate([rate_f[:, c] for c in cuts] + [rate_r[:, c] for c in cuts], axis=0)
    sums = -nn(stack, tri_ref[...], lax.Precision.HIGHEST)
    first = lane_first((GH, BL))
    cum_r = jnp.zeros((GH, BL), f32)
    cum_f = jnp.zeros((GH, BL), f32)
    state = jnp.zeros((GH * PS, BL), f32)
    for b in range(blocks):
        l_f = sums[b * GH : (b + 1) * GH]
        l_r = sums[(blocks + b) * GH : (blocks + b + 1) * GH]
        r_f = rate_f[:, cuts[b]]
        r_r = rate_r[:, cuts[b]]
        end_f = jnp.broadcast_to(l_f[:, BL - 1 : BL], (GH, BL))
        end_r = jnp.broadcast_to(l_r[:, BL - 1 : BL], (GH, BL))
        w_f = jnp.exp(end_f - l_f) * r_f
        w_r = jnp.exp(l_r + r_r) * r_r
        rows_ref[LQ, :, cuts[b]] = l_f + r_f
        rows_ref[RQ, :, cuts[b]] = -l_r
        rows_ref[KF, :, cuts[b]] = l_f - jnp.log(r_f)
        rows_ref[KR, :, cuts[b]] = -(l_r + r_r + jnp.log(r_r))
        rows_ref[WF, :, cuts[b]] = w_f
        rows_ref[WR, :, cuts[b]] = w_r
        rows_ref[EF, :, cuts[b]] = jnp.exp(l_f + r_f)
        rows_ref[ER, :, cuts[b]] = jnp.exp(end_r - l_r)
        tot_ref[b] = jnp.where(first, end_f, end_r)
        for h in range(GH):
            span = slice(h * PS, (h + 1) * PS)
            vals = v_ref[span, cuts[b]].astype(f32)
            lhs_scr[span, :BL] = (vals * w_f[h : h + 1]).astype(bf16)
            lhs_scr[span, BL:] = (vals * w_r[h : h + 1]).astype(bf16)
        keys = stacked_keys(k4_ref[:NS, cuts[b]], k4_ref[2 * NS : 3 * NS, cuts[b]])
        local_state = nt(lhs_scr[...], keys)
        sblk_ref[b] = local_state.astype(bf16)
        keep = jnp.where(first, jnp.exp(end_f), 1.0)
        gain = jnp.where(first, 1.0, jnp.exp(cum_r))
        state = jnp.concatenate(
            [
                state[h * PS : (h + 1) * PS] * keep[h : h + 1]
                + local_state[h * PS : (h + 1) * PS] * gain[h : h + 1]
                for h in range(GH)
            ],
            axis=0,
        )
        cum_f = cum_f + end_f
        cum_r = cum_r + end_r
    sdev_ref[...] = state.astype(bf16)
    tdev_ref[...] = jnp.where(first, cum_f, cum_r)


def value_stage(nx, wv, taps, bias, k4, tri, tokens):
    ext = nx.shape[0]
    blocks = tokens // BL
    rows = GH * PS
    return pl.pallas_call(
        value_kernel,
        grid=(NG,),
        in_specs=[
            pl.BlockSpec((ext, D), lambda g: (0, 0), pipeline_mode=pl.Buffered(1)),
            pl.BlockSpec((GH, WV, D), lambda g: (g, 0, 0)),
            pl.BlockSpec((rows, 8), lambda g: (g, 0)),
            pl.BlockSpec((GH, 2), lambda g: (g, 0)),
            pl.BlockSpec((4 * NS, tokens), lambda g: (0, 0)),
            pl.BlockSpec((BL, BL), lambda g: (0, 0)),
        ],
        out_specs=[
            pl.BlockSpec((rows, tokens), lambda g: (g, 0)),
            pl.BlockSpec((rows, tokens), lambda g: (g, 0)),
            pl.BlockSpec((rows, ext), lambda g: (g, 0)),
            pl.BlockSpec((KINDS, GH, tokens), lambda g: (0, g, 0)),
            pl.BlockSpec((blocks, GH, BL), lambda g: (0, g, 0)),
            pl.BlockSpec((blocks, rows, BL), lambda g: (0, g, 0)),
            pl.BlockSpec((rows, BL), lambda g: (g, 0)),
            pl.BlockSpec((GH, BL), lambda g: (g, 0)),
        ],
        out_shape=(
            jax.ShapeDtypeStruct((CH, tokens), bf16),
            jax.ShapeDtypeStruct((CH, tokens), bf16),
            jax.ShapeDtypeStruct((CH, ext), bf16),
            jax.ShapeDtypeStruct((KINDS, H, tokens), f32),
            jax.ShapeDtypeStruct((blocks, H, BL), f32),
            jax.ShapeDtypeStruct((blocks, CH, BL), bf16),
            jax.ShapeDtypeStruct((CH, BL), bf16),
            jax.ShapeDtypeStruct((H, BL), f32),
        ),
        scratch_shapes=[pltpu.VMEM((GH * WV, ext), f32), pltpu.VMEM((rows, 2 * BL), bf16)],
        compiler_params=params(),
        cost_estimate=cost(27),
        name="value_stage",
    )(nx, wv, taps, bias, k4, tri)


def chain_kernel(flip, copies, tokens, twist, meta_ref, sblk_ref, tot_ref, far_ref, *refs):
    states = refs[:copies]
    if flip:
        other_ref, out_ref, dot_ref = refs[copies:]
    else:
        (out_ref,) = refs[copies:]
    blocks = sblk_ref.shape[0]
    per = sblk_ref.shape[1] // PS
    step = pl.program_id(0)
    first = lane_first((1, BL))
    wide = lane_first((PS, BL))
    up_lanes = jnp.logical_not(wide) if flip else wide
    here = meta_ref[0]
    length = meta_ref[1]
    sequence = here * tokens // length
    places = [meta_ref[2 + k] for k in range(copies)]
    same = [(place * tokens // length) == sequence for place in places]
    for i in range(per):
        span = slice(i * PS, (i + 1) * PS)
        head = step * per + i
        totals = []
        for k in range(copies):
            place = twist(k, step) * per + i
            parts = [far_ref[k, pl.ds(part * H + place, 1), :] for part in range(3)]
            totals.append(parts[0] + parts[1] + parts[2])
        entering = jnp.zeros((PS, BL), f32)
        for k in range(copies):
            left = jnp.zeros((1, BL), f32)
            right = jnp.zeros((1, BL), f32)
            for q in range(copies):
                if q != k:
                    between = (places[q] > places[k]) & (places[q] < here)
                    left = left + totals[q] * between.astype(f32)
                    between = (places[q] < places[k]) & (places[q] > here)
                    right = right + totals[q] * between.astype(f32)
            from_left = jnp.exp(left) * (same[k] & (places[k] < here)).astype(f32)
            from_right = jnp.exp(right) * (same[k] & (places[k] > here)).astype(f32)
            if flip:
                weight = jnp.where(first, from_right, from_left)
            else:
                weight = jnp.where(first, from_left, from_right)
            entering = entering + weight * states[k][span, :].astype(f32)
        decay = [jnp.exp(tot_ref[b, pl.ds(head, 1), :]) for b in range(blocks)]
        locals_ = [sblk_ref[b, span, :].astype(f32) for b in range(blocks)]
        up = [entering]
        down = [entering]
        for b in range(blocks):
            up.append(up[-1] * decay[b] + locals_[b])
            rev = blocks - 1 - b
            down.append(down[-1] * decay[rev] + locals_[rev])
        down = down[::-1]
        for b in range(blocks):
            both = jnp.where(up_lanes, up[b], down[b + 1])
            out_ref[b, span, :] = both.astype(bf16)
            if flip:
                before = other_ref[b - 1 if b > 0 else blocks, span, :]
                beyond = other_ref[b + 1, span, :]
                far = jnp.where(wide, beyond.astype(f32), before.astype(f32))
                dot_ref[b, pl.ds(head, 1), :] = jnp.sum(both * far, axis=0, keepdims=True)
        if not flip:
            out_ref[blocks, span, :] = jnp.where(up_lanes, up[blocks], down[0]).astype(bf16)


def chain_stage(meta, sblk, tot, far_tot, states, twist, tokens, other=None):
    blocks = sblk.shape[0]
    copies = len(states)
    rows = CH // copies
    flip = other is not None
    in_specs = [
        pl.BlockSpec((blocks, rows, BL), lambda q, meta: (0, q, 0)),
        pl.BlockSpec((blocks, H, BL), lambda q, meta: (0, 0, 0)),
        pl.BlockSpec((copies, 3 * H, BL), lambda q, meta: (0, 0, 0)),
    ]
    for k in range(copies):
        in_specs.append(pl.BlockSpec((rows, BL), lambda q, meta, k=k: (twist(k, q), 0)))
    held = blocks if flip else blocks + 1
    out_specs = [pl.BlockSpec((held, rows, BL), lambda q, meta: (0, q, 0))]
    out_shape = [jax.ShapeDtypeStruct((held, CH, BL), bf16)]
    args = [meta, sblk, tot, far_tot, *states]
    if flip:
        in_specs.append(pl.BlockSpec((blocks + 1, rows, BL), lambda q, meta: (0, q, 0)))
        out_specs.append(pl.BlockSpec((blocks, H, BL), lambda q, meta: (0, 0, 0)))
        out_shape.append(jax.ShapeDtypeStruct((blocks, H, BL), f32))
        args.append(other)

    def body(*refs):
        chain_kernel(flip, copies, tokens, twist, *refs)

    return pl.pallas_call(
        body,
        grid_spec=pltpu.PrefetchScalarGridSpec(
            num_scalar_prefetch=1, grid=(copies,), in_specs=in_specs, out_specs=out_specs
        ),
        out_shape=out_shape,
        compiler_params=params(),
        cost_estimate=cost(7),
        name="chain_back" if flip else "chain_stage",
    )(*args)


def pair_blocks(value):
    zero = jnp.zeros((PS, BL), value.dtype)
    return jnp.concatenate(
        [
            jnp.concatenate([value[:PS], zero], axis=1),
            jnp.concatenate([zero, value[PS:]], axis=1),
        ],
        axis=0,
    )


def intra_kernel(v_ref, rows_ref, st_ref, o_ref):
    lower, _ = causal_masks()
    kf_cols = jnp.transpose(rows_ref[KF])
    kr_cols = jnp.transpose(rows_ref[KR])
    for pair in range(H // 2):
        mats = []
        for h in (2 * pair, 2 * pair + 1):
            gap = jnp.where(
                lower,
                rows_ref[LQ, h : h + 1, :] - kf_cols[:, h : h + 1],
                rows_ref[RQ, h : h + 1, :] - kr_cols[:, h : h + 1],
            )
            decay = jnp.exp(jnp.minimum(gap, 80.0))
            mats.append((decay * st_ref[0]).astype(bf16))
        span = slice(pair * 2 * PS, (pair + 1) * 2 * PS)
        out = nn(pair_blocks(v_ref[span, :]), jnp.concatenate(mats, axis=0))
        o_ref[span, :] = out.astype(o_ref.dtype)


def intra_stage(v, rows, scores):
    tokens = v.shape[1]
    return pl.pallas_call(
        intra_kernel,
        grid=(tokens // BL,),
        in_specs=[
            pl.BlockSpec((CH, BL), lambda b: (0, b)),
            pl.BlockSpec((KINDS, H, BL), lambda b: (0, 0, b)),
            pl.BlockSpec((1, BL, BL), lambda b: (b, 0, 0)),
        ],
        out_specs=pl.BlockSpec((CH, BL), lambda b: (0, b)),
        out_shape=jax.ShapeDtypeStruct((CH, tokens), bf16),
        compiler_params=params(),
        cost_estimate=cost(12),
        name="intra_stage",
    )(v, rows, scores)


def token_kernel(
    oi_ref, v_ref, s_ref, k4_ref, rows_ref, tot_ref, wg_ref, wo_ref,
    nx_ref, hid_ref, go_ref, cols_ref,
    ho_ref, r_ref, dg_ref, do_ref, dsblk_ref, dsdev_ref, rc_ref, dk_ref, small_ref,
    cross_scr, g_scr, dres_scr, mix_scr, gated_scr, lhs_scr, gain_scr, diag_scr,
    dev_scr, cum_scr, wide_scr,
):
    step = pl.program_id(0)
    last = pl.num_programs(0) - 1

    @pl.when(step == 0)
    def _():
        gain_scr[...] = jnp.zeros_like(gain_scr)
        diag_scr[...] = jnp.zeros_like(diag_scr)
        dev_scr[...] = jnp.zeros_like(dev_scr)
        cum_scr[...] = jnp.zeros_like(cum_scr)
        wide_scr[0] = jnp.broadcast_to(cols_ref[:, 0:1], (CH, BL))
        wide_scr[1] = jnp.broadcast_to(cols_ref[:, 1:2], (CH, BL))

    c_f = k4_ref[NS : 2 * NS, :]
    c_r = k4_ref[3 * NS :, :]
    both_keys = stacked_keys(c_f, c_r)
    cross_scr[...] = nn(s_ref[0], both_keys)
    g_scr[...] = nt(wg_ref[...], nx_ref[...])
    dres_scr[...] = nt(wo_ref[...], go_ref[...])
    squares = jnp.zeros((8, BL), f32)
    for h in range(H):
        span = slice(h * PS, (h + 1) * PS)
        part_f = cross_scr[span, :BL] * rows_ref[EF, h : h + 1, :]
        part_r = cross_scr[span, BL:] * rows_ref[ER, h : h + 1, :]
        mix = (
            oi_ref[span, :].astype(f32)
            + part_f
            + part_r
            + wide_scr[1, span, :] * v_ref[span, :].astype(f32)
        )
        gate = g_scr[span, :]
        gated = mix * (gate * sigmoid(gate))
        mix_scr[span, :] = mix
        gated_scr[span, :] = gated
        squares = squares + jnp.sum((gated * gated).reshape(PS // 8, 8, BL), axis=0)
    scale = lax.rsqrt(jnp.sum(squares, axis=0, keepdims=True) / CH + NORM_EPS)
    cross = jnp.zeros((8, BL), f32)
    for h in range(H):
        span = slice(h * PS, (h + 1) * PS)
        gated = gated_scr[span, :]
        gain = wide_scr[0, span, :]
        normal = gated * scale
        r_ref[span, :] = (normal * gain).astype(bf16)
        dres = dres_scr[span, :]
        gain_scr[span, :] += dres * normal
        cross = cross + jnp.sum((dres * gain * gated).reshape(PS // 8, 8, BL), axis=0)
    out = tn(r_ref[...], wo_ref[...])
    ho_ref[...] = (hid_ref[...].astype(f32) + out).astype(bf16)
    pull = scale * scale * scale * (jnp.sum(cross, axis=0, keepdims=True) / CH)
    for h in range(H):
        span = slice(h * PS, (h + 1) * PS)
        dgated = scale * (dres_scr[span, :] * wide_scr[0, span, :]) - gated_scr[span, :] * pull
        gate = g_scr[span, :]
        soft = sigmoid(gate)
        grad_mix = dgated * (gate * soft)
        dg_ref[span, :] = (dgated * mix_scr[span, :] * (soft * (1.0 + gate * (1.0 - soft)))).astype(
            bf16
        )
        diag_scr[span, :] += grad_mix * v_ref[span, :].astype(f32)
        do_ref[span, :] = grad_mix.astype(bf16)
        grad_f = grad_mix * rows_ref[EF, h : h + 1, :]
        grad_r = grad_mix * rows_ref[ER, h : h + 1, :]
        rc_ref[0, h : h + 1, :] = jnp.sum(grad_f * cross_scr[span, :BL], axis=0, keepdims=True)
        rc_ref[1, h : h + 1, :] = jnp.sum(grad_r * cross_scr[span, BL:], axis=0, keepdims=True)
        lhs_scr[span, :BL] = grad_f.astype(bf16)
        lhs_scr[span, BL:] = grad_r.astype(bf16)
    dstate = nt(lhs_scr[...], both_keys)
    dkeys = tn(s_ref[0], lhs_scr[...])
    dk_ref[:NS, :] = dkeys[:NS, :BL]
    dk_ref[NS:, :] = dkeys[NS:, BL:]
    dsblk_ref[0] = dstate.astype(bf16)
    first = lane_first((H, BL))
    total = tot_ref[0]
    keep = jnp.where(first, 1.0, jnp.exp(total))
    grow = jnp.where(first, jnp.exp(cum_scr[...]), 1.0)
    for h in range(H):
        span = slice(h * PS, (h + 1) * PS)
        dev_scr[span, :] = (
            dev_scr[span, :] * keep[h : h + 1] + dstate[span, :] * grow[h : h + 1]
        )
    cum_scr[...] += total

    @pl.when(step == last)
    def _():
        dsdev_ref[...] = dev_scr[...].astype(bf16)
        small_ref[0] = lane_sums(gain_scr[...])
        small_ref[1] = lane_sums(diag_scr[...])


def token_stage(oi, v, s9, k4, rows, tot, wg, wo, nx, hid, go, cols):
    tokens = v.shape[1]
    blocks = tokens // BL
    whole = dict(pipeline_mode=pl.Buffered(1))
    chan = pl.BlockSpec((CH, BL), lambda b: (0, b))
    toks = pl.BlockSpec((BL, D), lambda b: (b, 0))
    big = pltpu.VMEM((CH, BL), f32)
    return pl.pallas_call(
        token_kernel,
        grid=(blocks,),
        in_specs=[
            chan,
            chan,
            pl.BlockSpec((1, CH, BL), lambda b: (b, 0, 0)),
            pl.BlockSpec((4 * NS, BL), lambda b: (0, b)),
            pl.BlockSpec((KINDS, H, BL), lambda b: (0, 0, b)),
            pl.BlockSpec((1, H, BL), lambda b: (b, 0, 0)),
            pl.BlockSpec((CH, D), lambda b: (0, 0), **whole),
            pl.BlockSpec((CH, D), lambda b: (0, 0), **whole),
            toks,
            toks,
            toks,
            pl.BlockSpec((CH, 8), lambda b: (0, 0), **whole),
        ],
        out_specs=[
            toks,
            chan,
            chan,
            chan,
            pl.BlockSpec((1, CH, BL), lambda b: (b, 0, 0)),
            pl.BlockSpec((CH, BL), lambda b: (0, 0)),
            pl.BlockSpec((2, H, BL), lambda b: (0, 0, b)),
            pl.BlockSpec((2 * NS, BL), lambda b: (0, b)),
            pl.BlockSpec((2, 8, CH), lambda b: (0, 0, 0)),
        ],
        out_shape=(
            jax.ShapeDtypeStruct((tokens, D), bf16),
            jax.ShapeDtypeStruct((CH, tokens), bf16),
            jax.ShapeDtypeStruct((CH, tokens), bf16),
            jax.ShapeDtypeStruct((CH, tokens), bf16),
            jax.ShapeDtypeStruct((blocks, CH, BL), bf16),
            jax.ShapeDtypeStruct((CH, BL), bf16),
            jax.ShapeDtypeStruct((2, H, tokens), f32),
            jax.ShapeDtypeStruct((2 * NS, tokens), f32),
            jax.ShapeDtypeStruct((2, 8, CH), f32),
        ),
        scratch_shapes=[pltpu.VMEM((CH, 2 * BL), f32)]
        + [big] * 4
        + [pltpu.VMEM((CH, 2 * BL), bf16)]
        + [big] * 3
        + [pltpu.VMEM((H, BL), f32), pltpu.VMEM((2, CH, BL), f32)],
        compiler_params=params(),
        cost_estimate=cost(35),
        name="token_stage",
    )(oi, v, s9, k4, rows, tot, wg, wo, nx, hid, go, cols)


def early_grad_kernel(dg_ref, r_ref, nx_ref, go_ref, wg_ref, out_ref, dn_ref):
    gate = nn(dg_ref[...], nx_ref[...]).astype(bf16)
    outp = nn(r_ref[...], go_ref[...]).astype(bf16)
    out_ref[:, :PS, :] = gate.reshape(GH, PS, D)
    out_ref[:, PS:, :] = outp.reshape(GH, PS, D)
    part = tn(dg_ref[...], wg_ref[...])
    step = pl.program_id(0)

    @pl.when(step == 0)
    def _():
        dn_ref[...] = part

    @pl.when(step > 0)
    def _():
        dn_ref[...] += part


def early_grad_stage(dgate, result, nx, go, wg):
    tokens = dgate.shape[1]
    rows = GH * PS
    return pl.pallas_call(
        early_grad_kernel,
        grid=(NG,),
        in_specs=[
            pl.BlockSpec((rows, tokens), lambda g: (g, 0)),
            pl.BlockSpec((rows, tokens), lambda g: (g, 0)),
            pl.BlockSpec((tokens, D), lambda g: (0, 0)),
            pl.BlockSpec((tokens, D), lambda g: (0, 0)),
            pl.BlockSpec((rows, D), lambda g: (g, 0)),
        ],
        out_specs=[
            pl.BlockSpec((GH, 2 * PS, D), lambda g: (g, 0, 0)),
            pl.BlockSpec((tokens, D), lambda g: (0, 0)),
        ],
        out_shape=(
            jax.ShapeDtypeStruct((H, 2 * PS, D), bf16),
            jax.ShapeDtypeStruct((tokens, D), f32),
        ),
        compiler_params=params(),
        cost_estimate=cost(12),
        name="early_grad",
    )(dgate, result, nx, go, wg)


def intra_back_kernel(
    v_ref, do_ref, rows_ref, st_ref, k4_ref, dkc_ref, dv_ref, rc_ref, dk_ref
):
    lower, upper = causal_masks()
    kf_cols = jnp.transpose(rows_ref[KF])
    kr_cols = jnp.transpose(rows_ref[KR])
    score_grad = jnp.zeros((BL, BL), f32)
    for pair in range(H // 2):
        span = slice(pair * 2 * PS, (pair + 1) * 2 * PS)
        grads = pair_blocks(do_ref[span, :])
        mat_grads = tn(v_ref[span, :], grads)
        down = []
        over = []
        for i, h in enumerate((2 * pair, 2 * pair + 1)):
            gap = jnp.where(
                lower,
                rows_ref[LQ, h : h + 1, :] - kf_cols[:, h : h + 1],
                rows_ref[RQ, h : h + 1, :] - kr_cols[:, h : h + 1],
            )
            decay = jnp.exp(jnp.minimum(gap, 80.0))
            mat = decay * st_ref[0]
            term = decay * mat_grads[:, i * BL : (i + 1) * BL]
            score_grad = score_grad + term
            flow = term * st_ref[0]
            flow_f = jnp.where(lower, flow, 0.0)
            row_f = jnp.sum(flow_f, axis=0, keepdims=True)
            row_all = jnp.sum(flow, axis=0, keepdims=True)
            rc_ref[0, h : h + 1, :] = row_f
            rc_ref[1, h : h + 1, :] = row_all - row_f
            down.append(jnp.where(lower, mat, 0.0).astype(bf16))
            over.append(jnp.where(lower, 0.0, mat).astype(bf16))
        dv_f = nt(grads, jnp.concatenate(down, axis=1))
        dv_r = nt(grads, jnp.concatenate(over, axis=1))
        vals = v_ref[span, :].astype(f32)
        for i, h in enumerate((2 * pair, 2 * pair + 1)):
            half = slice(i * PS, (i + 1) * PS)
            rc_ref[2, h : h + 1, :] = jnp.sum(vals[half] * dv_f[half], axis=0, keepdims=True)
            rc_ref[3, h : h + 1, :] = jnp.sum(vals[half] * dv_r[half], axis=0, keepdims=True)
        dv_ref[span, :] = (dv_f + dv_r).astype(dv_ref.dtype)
    grad_f = jnp.where(lower, score_grad, 0.0).astype(bf16)
    grad_r = jnp.where(upper, score_grad, 0.0).astype(bf16)
    b_f = k4_ref[:NS, :]
    c_f = k4_ref[NS : 2 * NS, :]
    b_r = k4_ref[2 * NS : 3 * NS, :]
    c_r = k4_ref[3 * NS :, :]
    dk_ref[:NS, :] = nt(c_f, grad_f)
    dk_ref[NS : 2 * NS, :] = nn(b_f, grad_f) + dkc_ref[:NS, :]
    dk_ref[2 * NS : 3 * NS, :] = nt(c_r, grad_r)
    dk_ref[3 * NS :, :] = nn(b_r, grad_r) + dkc_ref[NS:, :]


def intra_back_stage(v, do, rows, scores, k4, dkc):
    tokens = v.shape[1]
    chan = pl.BlockSpec((CH, BL), lambda b: (0, b))
    return pl.pallas_call(
        intra_back_kernel,
        grid=(tokens // BL,),
        in_specs=[
            chan,
            chan,
            pl.BlockSpec((KINDS, H, BL), lambda b: (0, 0, b)),
            pl.BlockSpec((1, BL, BL), lambda b: (b, 0, 0)),
            pl.BlockSpec((4 * NS, BL), lambda b: (0, b)),
            pl.BlockSpec((2 * NS, BL), lambda b: (0, b)),
        ],
        out_specs=[
            chan,
            pl.BlockSpec((4, H, BL), lambda b: (0, 0, b)),
            pl.BlockSpec((4 * NS, BL), lambda b: (0, b)),
        ],
        out_shape=(
            jax.ShapeDtypeStruct((CH, tokens), bf16),
            jax.ShapeDtypeStruct((4, H, tokens), f32),
            jax.ShapeDtypeStruct((4 * NS, tokens), f32),
        ),
        compiler_params=params(),
        cost_estimate=cost(18),
        name="intra_back",
    )(v, do, rows, scores, k4, dkc)


def cross_back_kernel(
    dvi_ref, v_ref, do_ref, u_ref, ds_ref, k4_ref, rows_ref, rci_ref, rcc_ref,
    x_ref, dki_ref, cols_ref, after_ref,
    dpre_ref, dx_ref, dk_ref,
    cross_scr, lhs_scr, c_scr, wide_scr,
):
    b_f = k4_ref[:NS, :]
    b_r = k4_ref[2 * NS : 3 * NS, :]

    @pl.when(pl.program_id(0) == 0)
    def _():
        wide_scr[...] = jnp.broadcast_to(cols_ref[:, 1:2], (CH, BL))

    cross_scr[...] = nn(ds_ref[0], stacked_keys(b_f, b_r))
    for h in range(H):
        span = slice(h * PS, (h + 1) * PS)
        vals = v_ref[span, :].astype(f32)
        w_f = rows_ref[WF, h : h + 1, :]
        w_r = rows_ref[WR, h : h + 1, :]
        dv_f = cross_scr[span, :BL] * w_f
        dv_r = cross_scr[span, BL:] * w_r
        c_scr[0, h : h + 1, :] = jnp.sum(vals * dv_f, axis=0, keepdims=True)
        c_scr[1, h : h + 1, :] = jnp.sum(vals * dv_r, axis=0, keepdims=True)
        lhs_scr[span, :BL] = (vals * w_f).astype(bf16)
        lhs_scr[span, BL:] = (vals * w_r).astype(bf16)
        grad = (
            dvi_ref[span, :].astype(f32)
            + dv_f
            + dv_r
            + wide_scr[span, :] * do_ref[span, :].astype(f32)
        )
        pre = u_ref[span, :].astype(f32)
        soft = sigmoid(pre)
        dpre_ref[span, :] = (grad * (soft * (1.0 + pre * (1.0 - soft)))).astype(dpre_ref.dtype)
    dkeys = tn(ds_ref[0], lhs_scr[...])
    dk_ref[...] = dki_ref[...]
    dk_ref[:NS, :] += dkeys[:NS, :BL]
    dk_ref[2 * NS : 3 * NS, :] += dkeys[NS:, BL:]
    first = lane_first((H, BL))
    through_f = jnp.sum(jnp.where(first, x_ref[0], 0.0), axis=1, keepdims=True)
    through_r = jnp.sum(jnp.where(first, 0.0, x_ref[0]), axis=1, keepdims=True)
    row_f = rci_ref[0] + rcc_ref[0]
    row_r = rci_ref[1] + rcc_ref[1]
    col_f = rci_ref[2] + c_scr[0]
    col_r = rci_ref[3] + c_scr[1]
    after = after_ref[...]
    strict = lax.Precision.HIGHEST
    sum_f = nn(row_f, after, strict) - nn(col_f, after, strict) - col_f + through_f
    sum_r = nt(row_r, after, strict) - nt(col_r, after, strict) - col_r + through_r
    for kind, (total, col, x_kind, r_kind) in enumerate(
        ((sum_f, col_f, XF, RF), (sum_r, col_r, XR, RR))
    ):
        soft = sigmoid(rows_ref[x_kind])
        rate = rows_ref[r_kind]
        live = rate > 0.0
        ratio = jnp.where(live, soft / jnp.where(live, rate, 1.0), 1.0)
        dx_ref[kind] = col * ratio - total * soft


def cross_back_stage(dvi, v, do, u, ds9, k4, rows, rci, rcc, x9, dki, cols, after):
    tokens = v.shape[1]
    chan = pl.BlockSpec((CH, BL), lambda b: (0, b))
    keys = pl.BlockSpec((4 * NS, BL), lambda b: (0, b))
    return pl.pallas_call(
        cross_back_kernel,
        grid=(tokens // BL,),
        in_specs=[
            chan,
            chan,
            chan,
            chan,
            pl.BlockSpec((1, CH, BL), lambda b: (b, 0, 0)),
            keys,
            pl.BlockSpec((KINDS, H, BL), lambda b: (0, 0, b)),
            pl.BlockSpec((4, H, BL), lambda b: (0, 0, b)),
            pl.BlockSpec((2, H, BL), lambda b: (0, 0, b)),
            pl.BlockSpec((1, H, BL), lambda b: (b, 0, 0)),
            keys,
            pl.BlockSpec((CH, 8), lambda b: (0, 0)),
            pl.BlockSpec((BL, BL), lambda b: (0, 0)),
        ],
        out_specs=[chan, pl.BlockSpec((2, H, BL), lambda b: (0, 0, b)), keys],
        out_shape=(
            jax.ShapeDtypeStruct((CH, tokens), bf16),
            jax.ShapeDtypeStruct((2, H, tokens), f32),
            jax.ShapeDtypeStruct((4 * NS, tokens), f32),
        ),
        scratch_shapes=[
            pltpu.VMEM((CH, 2 * BL), f32),
            pltpu.VMEM((CH, 2 * BL), bf16),
            pltpu.VMEM((2, H, BL), f32),
            pltpu.VMEM((CH, BL), f32),
        ],
        compiler_params=params(),
        cost_estimate=cost(16),
        name="cross_back",
    )(dvi, v, do, u, ds9, k4, rows, rci, rcc, x9, dki, cols, after)


def key_pre_kernel(dk_ref, u_ref, edge_ref, out_ref):
    tokens = u_ref.shape[1]
    lane = lax.broadcasted_iota(jnp.int32, (NS, tokens), 1)
    d_cf = pltpu.roll(dk_ref[NS : 2 * NS, :], tokens - 1, axis=1)
    d_cf = jnp.where(lane == tokens - 1, edge_ref[:, 0:1], d_cf)
    d_cr = pltpu.roll(dk_ref[3 * NS :, :], 1, axis=1)
    d_cr = jnp.where(lane == 0, edge_ref[:, 1:2], d_cr)
    grad = jnp.concatenate([dk_ref[:NS, :], d_cf, dk_ref[2 * NS : 3 * NS, :], d_cr], axis=0)
    pre = u_ref[...]
    soft = sigmoid(pre)
    out_ref[...] = grad * (soft * (1.0 + pre * (1.0 - soft)))


def key_pre_stage(dk, u, edge):
    return pl.pallas_call(
        key_pre_kernel,
        out_shape=jax.ShapeDtypeStruct(u.shape, f32),
        compiler_params=pltpu.CompilerParams(vmem_limit_bytes=56 * 1024 * 1024),
        cost_estimate=cost(3),
        name="key_pre",
    )(dk, u, edge)


def conv_back_rows(dpre, taps, signal):
    rows, tokens = dpre.shape
    ext = signal.shape[1]
    wide = jnp.concatenate([dpre, jnp.zeros((rows, ext - tokens), dpre.dtype)], axis=1)
    total = None
    sums = []
    for k in range(K):
        shift = (k - K // 2) % ext
        moved = wide if shift == 0 else pltpu.roll(wide, shift, axis=1)
        moved = moved.astype(f32)
        term = moved * taps[:, k : k + 1]
        total = term if total is None else total + term
        prod = moved * signal
        part = prod[:, :BL]
        for b in range(1, ext // BL):
            part = part + prod[:, b * BL : (b + 1) * BL]
        sums.append(part)
    return total, sums


def key_back_kernel(
    meta_ref, dpre_ref, taps_ref, p_ref, nx_ref, w_ref, g_ref, dn_ref, t_ref, low_scr, g_scr, t_scr
):
    for c in range(4 * NS // 16):
        span = slice(c * 16, (c + 1) * 16)
        total, sums = conv_back_rows(dpre_ref[span, :], taps_ref[span, :], p_ref[span, :])
        low_scr[span, :] = total.astype(bf16)
        for k in range(K):
            t_scr[k, span, :] = sums[k]
    for k in range(K):
        t_ref[k : k + 1, :] = lane_sums(t_scr[k])[:1]
    t_ref[K : K + 1, :] = jnp.zeros((1, 4 * NS), f32)
    g_scr[...] = nn(low_scr[...], nx_ref[...])
    count, rows, _ = g_ref.shape
    for q in range(count):
        start = pl.multiple_of(meta_ref[2 + q] * rows, 8)
        g_ref[q] = g_scr[pl.ds(start, rows), :].astype(g_ref.dtype)
    dn_ref[...] = tn(low_scr[...], w_ref[...])


def key_back_stage(meta, dpre, taps, proj, nx, key_low):
    ext = nx.shape[0]
    count = meta.shape[0] - 2
    args = (dpre, taps, proj, nx, key_low)
    outs = (
        jax.ShapeDtypeStruct((count, 4 * NS // count, D), bf16),
        jax.ShapeDtypeStruct((ext, D), f32),
        jax.ShapeDtypeStruct((8, 4 * NS), f32),
    )

    def whole(shape):
        return pl.BlockSpec(shape, lambda i, meta: (0,) * len(shape))

    return pl.pallas_call(
        key_back_kernel,
        grid_spec=pltpu.PrefetchScalarGridSpec(
            num_scalar_prefetch=1,
            grid=(1,),
            in_specs=[whole(x.shape) for x in args],
            out_specs=[whole(x.shape) for x in outs],
            scratch_shapes=[
                pltpu.VMEM((4 * NS, ext), bf16),
                pltpu.VMEM((4 * NS, D), f32),
                pltpu.VMEM((K, 4 * NS, BL), f32),
            ],
        ),
        out_shape=outs,
        compiler_params=params(),
        cost_estimate=cost(8),
        name="key_back",
    )(meta, *args)


def value_back_kernel(
    dpre_ref, taps_ref, s_ref, dx_ref, nx_ref, wv_ref, g_ref, dn_ref, t_ref, low_scr, tap_scr
):
    tokens = dpre_ref.shape[1]
    ext = s_ref.shape[1]
    step = pl.program_id(0)
    for h in range(GH):
        for c in range(PS // 16):
            src = h * PS + c * 16
            span = slice(src, src + 16)
            total, sums = conv_back_rows(
                dpre_ref[span, :], taps_ref[span, :], s_ref[span, :].astype(f32)
            )
            low_scr[h * WV + c * 16 : h * WV + (c + 1) * 16, :] = total.astype(bf16)
            for k in range(K):
                tap_scr[k, span, :] = sums[k]
        tail = jnp.concatenate(
            [
                dx_ref[0, h : h + 1, :],
                dx_ref[1, h : h + 1, :],
                jnp.zeros((14, tokens), f32),
            ],
            axis=0,
        )
        low_scr[h * WV + PS : (h + 1) * WV, :tokens] = tail.astype(bf16)
        low_scr[h * WV + PS : (h + 1) * WV, tokens:] = jnp.zeros((16, ext - tokens), bf16)
    for k in range(K):
        t_ref[0, k : k + 1, :] = lane_sums(tap_scr[k])[:1]
    t_ref[0, K : K + 1, :] = jnp.zeros((1, GH * PS), f32)
    g_ref[...] = nn(low_scr[...], nx_ref[...]).reshape(GH, WV, D).astype(g_ref.dtype)
    part = tn(low_scr[...], wv_ref[...].reshape(GH * WV, D))

    @pl.when(step == 0)
    def _():
        dn_ref[...] = part

    @pl.when(step > 0)
    def _():
        dn_ref[...] += part


def value_back_stage(dpre, taps, s, dx, nx, wv):
    tokens = dpre.shape[1]
    ext = nx.shape[0]
    rows = GH * PS
    return pl.pallas_call(
        value_back_kernel,
        grid=(NG,),
        in_specs=[
            pl.BlockSpec((rows, tokens), lambda g: (g, 0)),
            pl.BlockSpec((rows, 8), lambda g: (g, 0)),
            pl.BlockSpec((rows, ext), lambda g: (g, 0)),
            pl.BlockSpec((2, GH, tokens), lambda g: (0, g, 0)),
            pl.BlockSpec((ext, D), lambda g: (0, 0), pipeline_mode=pl.Buffered(1)),
            pl.BlockSpec((GH, WV, D), lambda g: (g, 0, 0)),
        ],
        out_specs=[
            pl.BlockSpec((GH, WV, D), lambda g: (g, 0, 0)),
            pl.BlockSpec((ext, D), lambda g: (0, 0)),
            pl.BlockSpec((1, 8, rows), lambda g: (g, 0, 0)),
        ],
        out_shape=(
            jax.ShapeDtypeStruct((H, WV, D), bf16),
            jax.ShapeDtypeStruct((ext, D), f32),
            jax.ShapeDtypeStruct((NG, 8, rows), f32),
        ),
        scratch_shapes=[
            pltpu.VMEM((GH * WV, ext), bf16),
            pltpu.VMEM((K, rows, BL), f32),
        ],
        compiler_params=params(),
        cost_estimate=cost(27),
        name="value_back",
    )(dpre, taps, s, dx, nx, wv)


def pick(sources, index):
    count = index.shape[0]
    rows, width = sources[0].shape[1:]

    def body(index_ref, *refs):
        out_ref = refs[-1]
        for i in range(count):
            first = 0
            for ref in refs[:-1]:
                n = ref.shape[0]
                local = index_ref[i] - first

                @pl.when((local >= 0) & (local < n))
                def _(ref=ref, local=local, i=i):
                    out_ref[i] = ref[local]

                first += n

    return pl.pallas_call(
        body,
        grid_spec=pltpu.PrefetchScalarGridSpec(
            num_scalar_prefetch=1,
            grid=(1,),
            in_specs=[pl.BlockSpec(x.shape, lambda i, index: (0, 0, 0)) for x in sources],
            out_specs=pl.BlockSpec((count, rows, width), lambda i, index: (0, 0, 0)),
        ),
        out_shape=jax.ShapeDtypeStruct((count, rows, width), sources[0].dtype),
        compiler_params=params(),
        cost_estimate=cost(3),
        name="pick",
    )(index, *sources)


def pick_two_kernel(index_ref, slots_ref, gate_ref, out_ref):
    for h in range(H):
        gate_ref[h] = slots_ref[index_ref[h], :PS, :]
        out_ref[h] = slots_ref[index_ref[h], PS:, :]


def pick_two(slots, index):
    half = jax.ShapeDtypeStruct((H, PS, D), slots.dtype)
    return pl.pallas_call(
        pick_two_kernel,
        grid_spec=pltpu.PrefetchScalarGridSpec(
            num_scalar_prefetch=1,
            grid=(1,),
            in_specs=[pl.BlockSpec(slots.shape, lambda i, index: (0, 0, 0))],
            out_specs=[pl.BlockSpec((H, PS, D), lambda i, index: (0, 0, 0))] * 2,
        ),
        out_shape=(half, half),
        compiler_params=params(),
        cost_estimate=cost(6),
        name="pick_two",
    )(index, slots)


def deal(source, index, live, target=None, extra=None, single=None, joined=0):
    count = index.shape[0]
    rows, width = source.shape[1:]
    more = 0 if extra is None else extra.shape[0] // count
    plan = [index, live] if extra is None else [index, live, target]
    args = [source] if extra is None else [source, extra, single]

    def body(*refs):
        index_ref, live_ref = refs[:2]
        source_ref = refs[len(plan)]
        outs = refs[len(plan) + len(args) :]
        for k in range(count):
            value = source_ref[index_ref[k]]
            value = jnp.where(live_ref[k] > 0, value, jnp.zeros_like(value))
            if joined:
                outs[k // joined][k % joined] = value
            elif more:
                start = pl.multiple_of(refs[2][k] * more, 8)
                last = refs[len(plan) + 1][pl.ds(start, more), :]
                one = refs[len(plan) + 2][pl.ds(refs[2][k], 1), :]
                space = jnp.zeros((16 - more - 1, width), f32)
                last = jnp.concatenate([space, one, last], axis=0)
                outs[k][: rows - 16] = value[: rows - 16]
                outs[k][rows - 16 :] = (value[rows - 16 :].astype(f32) + last).astype(bf16)
            else:
                outs[k][...] = value

    def whole(shape):
        return pl.BlockSpec(shape, lambda i, *plan: (0,) * len(shape))

    if joined:
        shapes = [jax.ShapeDtypeStruct((joined, rows, width), source.dtype)] * (count // joined)
    else:
        shapes = [jax.ShapeDtypeStruct((rows, width), source.dtype)] * count
    return pl.pallas_call(
        body,
        grid_spec=pltpu.PrefetchScalarGridSpec(
            num_scalar_prefetch=len(plan),
            grid=(1,),
            in_specs=[whole(x.shape) for x in args],
            out_specs=[whole(x.shape) for x in shapes],
        ),
        out_shape=shapes,
        compiler_params=params(),
        cost_estimate=cost(3),
        name="deal",
    )(*plan, *args)


def adamw_update(weight, gradient, first_moment, second, average, step_rate):
    first_new = BETA_ONE * first_moment + (1.0 - BETA_ONE) * gradient
    second_new = BETA_TWO * second + (1.0 - BETA_TWO) * gradient * gradient
    correct_one = 1.0 - BETA_ONE**STEP
    correct_two = 1.0 - BETA_TWO**STEP
    normalized = first_new / correct_one / (jnp.sqrt(second_new / correct_two) + ADAM_EPS)
    weight_new = weight - step_rate * (normalized + WEIGHT_DECAY * weight)
    average_new = AVERAGE_KEEP * average + (1.0 - AVERAGE_KEEP) * weight_new
    return (weight_new, first_new, second_new, average_new)


def finish_kernel(
    code_ref, share_ref, w_ref, m_ref, v_ref, a_ref,
    w_out, m_out, v_out, a_out, small_ref, gain_ref, scr,
):
    count, rows, _ = share_ref.shape
    keys = 4 * NS // count
    total = jnp.zeros((1, D), f32)
    for i in range(count):
        share = share_ref[code_ref[i]].astype(f32)
        scr[i * keys : (i + 1) * keys, :] = share[rows - keys :]
        small_ref[i : i + 1, :] = share[rows - keys - 1 : rows - keys]
        total = total + share[:1]
    gain_ref[...] = jnp.broadcast_to(total, (8, D))
    new = adamw_update(
        w_ref[...], jnp.transpose(scr[...]), m_ref[...], v_ref[...], a_ref[...], MATRIX_RATE
    )
    for out, value in zip((w_out, m_out, v_out, a_out), new):
        out[...] = value


def finish_stage(code, shares, weight, first, second, ema):
    count = shares.shape[0]
    args = (shares, weight, first, second, ema)
    outs = [jax.ShapeDtypeStruct(weight.shape, f32)] * 4 + [
        jax.ShapeDtypeStruct((count, D), f32),
        jax.ShapeDtypeStruct((8, D), f32),
    ]

    def whole(shape):
        return pl.BlockSpec(shape, lambda i, code: (0,) * len(shape))

    return pl.pallas_call(
        finish_kernel,
        grid_spec=pltpu.PrefetchScalarGridSpec(
            num_scalar_prefetch=1,
            grid=(1,),
            in_specs=[whole(x.shape) for x in args],
            out_specs=[whole(x.shape) for x in outs],
            scratch_shapes=[pltpu.VMEM((4 * NS, D), f32)],
        ),
        out_shape=outs,
        compiler_params=params(),
        cost_estimate=cost(5),
        name="finish_stage",
    )(code, *args)


def make_local(n_dp, n_mp):
    per = H // n_mp
    direct = n_mp == 4 and n_dp == 8

    def swap(x, axis, size, bit):
        return lax.ppermute(x, axis, [(i, i ^ bit) for i in range(size)])

    def head_rows(mp_index):
        rows = jnp.arange(n_mp, dtype=jnp.int32)
        return jnp.bitwise_xor(rows, mp_index) if direct else rows

    def over_mp(x):
        if direct:
            far = swap(x, "mp", n_mp, 2)
            return [x, swap(x, "mp", n_mp, 1), far, swap(far, "mp", n_mp, 1)]
        copies = lax.all_gather(x, "mp", axis=0)
        return [copies[k] for k in range(n_mp)]

    def gather_dp(part):
        return [part[None]] + [swap(part, "dp", n_dp, k)[None] for k in range(1, n_dp)]

    def pick_own(pieces, owners, dp_index):
        return pick(pieces, jnp.bitwise_xor(owners, dp_index))

    def scatter_mp(grads):
        got = swap(jnp.stack([grads[1], grads[3]]), "mp", n_mp, 1)
        away = (grads[2].astype(f32) + got[1].astype(f32)).astype(bf16)
        mine = grads[0].astype(f32) + got[0].astype(f32)
        return mine + swap(away, "mp", n_mp, 2).astype(f32)

    def deal_targets(owners, targets):
        match = targets[:, None] == owners[None, :]
        return jnp.argmax(match, axis=1).astype(jnp.int32), jnp.any(match, axis=1).astype(jnp.int32)

    def gather_all(x, mp_index, dp_index):
        both = x[None]
        for axis, size, bit in (
            ("dp", n_dp, 2), ("dp", n_dp, 4), ("dp", n_dp, 1), ("mp", n_mp, 2), ("mp", n_mp, 1)
        ):
            both = jnp.concatenate([both, swap(both, axis, size, bit)], axis=0)
        far = jnp.bitwise_xor(jnp.arange(n_mp, dtype=jnp.int32), mp_index)[:, None]
        off = jnp.bitwise_xor(jnp.arange(n_dp, dtype=jnp.int32), dp_index)[None, :]
        code = ((off >> 1) & 3) + 4 * (off & 1) + 8 * (far >> 1) + 16 * (far & 1)
        return both, code.reshape(-1)

    def local(
        hidden_in, out_grad, seq_len, owner_list,
        block_master, block_first, block_second, block_ema,
        head_small, head_first, head_second, head_ema,
        bc_weight, bc_first, bc_second, bc_ema,
        shared_small, shared_first, shared_second, shared_ema,
    ):
        tokens = hidden_in.shape[0]
        mp_index = lax.axis_index("mp")
        dp_index = lax.axis_index("dp")
        owners = lax.dynamic_slice_in_dim(owner_list, mp_index * per, per)
        order = head_rows(mp_index)
        bounds = (mp_index + jnp.arange(2, dtype=jnp.int32)) * tokens % seq_len == 0
        starts = bounds[:1].reshape(1, 1)
        ends = bounds[1:].reshape(1, 1)
        meta = jnp.concatenate([mp_index.reshape(1), seq_len, order]).astype(jnp.int32)
        nexts = [(i, i + 1) for i in range(n_mp - 1)]
        prevs = [(i + 1, i) for i in range(n_mp - 1)]

        slot_t = jnp.transpose(block_master[0, 0]).astype(bf16)
        part_v = jnp.concatenate(
            [slot_t[PS : 2 * PS + 2], jnp.zeros((WV - PS - 2, D), bf16)], axis=0
        )
        part_go = jnp.concatenate([slot_t[:PS], slot_t[2 * PS + 2 :]], axis=0)
        if direct:
            pieces_v = gather_dp(part_v)
            mine_v = pick_own(pieces_v, owners, dp_index)
            far_v = swap(mine_v, "mp", n_mp, 2)
            near_v = swap(mine_v, "mp", n_mp, 1)
            slots = lax.all_gather(part_go, ("mp", "dp"), axis=0)
            rows_of = jnp.repeat(order, per)
            heads_of = rows_of * per + jnp.arange(H, dtype=jnp.int32) % per
            wg, wo = pick_two(slots, rows_of * n_dp + jnp.take(owner_list, heads_of))
        else:
            mine_v = pick([lax.all_gather(part_v, "dp", axis=0)], owners)
            wv = jnp.concatenate(over_mp(mine_v), axis=0)
            mine_go = pick([lax.all_gather(part_go, "dp", axis=0)], owners)
            all_go = over_mp(mine_go)
            wg = jnp.concatenate([x[:, :PS] for x in all_go], axis=0)
            wo = jnp.concatenate([x[:, PS:] for x in all_go], axis=0)
        wg = wg.reshape(CH, D)
        wo = wo.reshape(CH, D)

        hidden = hidden_in.astype(f32)
        gain_in = shared_small[K:].reshape(D)
        scale_in = lax.rsqrt(jnp.mean(hidden * hidden, axis=1, keepdims=True) + NORM_EPS)
        normed = (hidden * scale_in * gain_in).astype(bf16)
        from_left = lax.ppermute(normed[-HALO:], "mp", nexts)
        from_right = lax.ppermute(normed[:HALO], "mp", prevs)
        from_left = jnp.where(starts, jnp.zeros_like(from_left), from_left)
        from_right = jnp.where(ends, jnp.zeros_like(from_right), from_right)
        nx = jnp.concatenate(
            [normed, from_right, jnp.zeros((PAD - 2 * HALO, D), bf16), from_left], axis=0
        )

        heads = jnp.concatenate(over_mp(head_small), axis=0)
        taps_v = jnp.transpose(heads[:, 1 : 1 + K, :], (0, 2, 1)).reshape(CH, K)
        taps_v = jnp.pad(taps_v, ((0, 0), (0, 1)))
        cols = jnp.stack([heads[:, 0].reshape(CH), heads[:, K + 1].reshape(CH)], axis=1)
        cols = jnp.pad(cols, ((0, 0), (0, 6)))
        bias = heads[:, K + 2, :2]
        key_low = jnp.transpose(bc_weight).astype(bf16)
        taps_k = jnp.pad(jnp.transpose(shared_small[:K]), ((0, 0), (0, 1)))
        ids = jnp.arange(BL)
        tri = (ids[:, None] <= ids[None, :]).astype(f32)
        after = (ids[:, None] > ids[None, :]).astype(f32)

        key_proj, key_u, k4, scores = key_stage(nx, key_low, taps_k, tokens)
        if direct:
            far_v, k4 = lax.optimization_barrier((far_v, k4))
            wv = jnp.concatenate([mine_v, near_v, far_v, swap(far_v, "mp", n_mp, 1)], axis=0)
        v, u, s, rows, tot, sblk, sdev, tdev = value_stage(
            nx, wv, taps_v, bias, k4, tri, tokens
        )
        tot_hi = lax.reduce_precision(tdev, 8, 7)
        tot_mid = lax.reduce_precision(tdev - tot_hi, 8, 7)
        tot_low = tdev - tot_hi - tot_mid
        message = jnp.concatenate(
            [sdev, tot_hi.astype(bf16), tot_mid.astype(bf16), tot_low.astype(bf16)], axis=0
        )
        def twist(k, q):
            return q ^ k if direct else q

        o_intra = intra_stage(v, rows, scores)
        if direct:
            far = swap(message, "mp", n_mp, 2)
            near = swap(message, "mp", n_mp, 1)
            far, o_intra = lax.optimization_barrier((far, o_intra))
            messages = [message, near, far, swap(far, "mp", n_mp, 1)]
        else:
            messages = over_mp(message)
        far_tot = jnp.stack([x[CH:] for x in messages]).astype(f32)

        (s9,) = chain_stage(meta, sblk, tot, far_tot, messages, twist, tokens)
        hidden_out, result_t, dgate_t, do_t, dsblk, dsdev, rcc, dkc, small_mid = token_stage(
            o_intra, v, s9, k4, rows, tot, wg, wo, nx, hidden_in, out_grad, cols
        )
        if direct:
            far_d = swap(dsdev, "mp", n_mp, 2)
            near_d = swap(dsdev, "mp", n_mp, 1)
        grad_go, dn_gate = early_grad_stage(dgate_t, result_t, nx, out_grad, wg)
        grad_go = grad_go.reshape(n_mp, per * 2 * PS, D)
        if direct:
            far_d, grad_go = lax.optimization_barrier((far_d, grad_go))
            got = swap(jnp.stack([grad_go[1], grad_go[3]]), "mp", n_mp, 1)
            away = (grad_go[2].astype(f32) + got[1].astype(f32)).astype(bf16)
            far_go = swap(away, "mp", n_mp, 2)
            do_back, away = lax.optimization_barrier((do_t, away))
        else:
            do_back = do_t
        dvi, rci, dki = intra_back_stage(v, do_back, rows, scores, k4, dkc)
        to_prev = lax.ppermute(dki[NS : 2 * NS, :1].reshape(1, NS), "mp", prevs)
        to_next = lax.ppermute(dki[3 * NS :, tokens - 1 :].reshape(1, NS), "mp", nexts)
        if direct:
            messages = [dsdev, near_d, far_d, swap(far_d, "mp", n_mp, 1)]
        else:
            messages = over_mp(dsdev)
        natural = jnp.arange(n_dp, dtype=jnp.int32)
        ds9, x9 = chain_stage(meta, dsblk, tot, far_tot, messages, twist, tokens, s9)
        if direct:
            far_go, ds9, dvi = lax.optimization_barrier((far_go, ds9, dvi))
            mine_go = grad_go[0].astype(f32) + got[0].astype(f32) + far_go.astype(f32)
            mine_go = mine_go.astype(bf16)
        else:
            mine_go = lax.psum_scatter(grad_go, "mp", scatter_dimension=0, tiled=True)[0]
        if direct:
            bits = jnp.arange(n_dp, dtype=jnp.int32)
            bits = (bits >> 2) + 4 * ((bits >> 1) & 1) + 2 * (bits & 1)
            keep_go, send_go = deal(
                mine_go.reshape(per, 2 * PS, D),
                *deal_targets(owners, jnp.bitwise_xor(bits, dp_index)),
                joined=n_dp // 2,
            )
            keep_go, ds9 = lax.optimization_barrier((keep_go, ds9))
            keep_go = keep_go.astype(f32) + swap(send_go, "dp", n_dp, 1).astype(f32)
        else:
            (dealt,) = deal(
                mine_go.reshape(per, 2 * PS, D), *deal_targets(owners, natural), joined=n_dp
            )
            own_go = lax.psum_scatter(dealt, "dp", scatter_dimension=0, tiled=True)[0]
        dpre, dx, dk = cross_back_stage(
            dvi, v, do_t, u, ds9, k4, rows, rci, rcc, x9, dki, cols, after
        )
        if direct:
            keep_go, dpre, dk = lax.optimization_barrier((keep_go, dpre, dk))
            far_go = swap(keep_go[2:].astype(bf16), "dp", n_dp, 4)
        d_last, d_first = to_prev, to_next
        d_last = jnp.where(ends, 0.0, d_last)
        d_first = jnp.where(starts, 0.0, d_first)
        edge = jnp.transpose(jnp.concatenate([d_last, d_first, jnp.zeros((6, NS), f32)], axis=0))
        dpre_k = key_pre_stage(dk, key_u, edge)
        grad_v, dn_value, tap_v = value_back_stage(dpre, taps_v, s, dx, nx, wv)
        if direct:
            far_go, grad_v = lax.optimization_barrier((far_go, grad_v))
            keep_go = keep_go[:2] + far_go.astype(f32)
            last_go = swap(keep_go[1].astype(bf16), "dp", n_dp, 2)
            both = grad_v.reshape(n_mp, per * WV, D)
            got_v = swap(jnp.stack([both[1], both[3]]), "mp", n_mp, 1)
            away_v = (both[2].astype(f32) + got_v[1].astype(f32)).astype(bf16)
            away_v, dpre_k = lax.optimization_barrier((away_v, dpre_k))
            far_v = swap(away_v, "mp", n_mp, 2)
        grad_key, dn_key, tap_key = key_back_stage(meta, dpre_k, taps_k, key_proj, nx, key_low)
        if direct:
            far_v, last_go, grad_key, dn_key, tap_key = lax.optimization_barrier(
                (far_v, last_go, grad_key, dn_key, tap_key)
            )
            own_go = keep_go[0] + last_go.astype(f32)

        head_grad = jnp.concatenate(
            [
                small_mid[0, 0].reshape(H, 1, PS),
                jnp.transpose(
                    tap_v.reshape(NG, 8, GH, PS)[:, :K], (0, 2, 1, 3)
                ).reshape(H, K, PS),
                small_mid[1, 0].reshape(H, 1, PS),
                jnp.pad(jnp.transpose(jnp.sum(dx, axis=2)), ((0, 0), (0, PS - 2))).reshape(
                    H, 1, PS
                ),
            ],
            axis=1,
        )
        if direct:
            head_grad = jnp.take(head_grad.reshape(n_mp, per, 10, PS), order, axis=0)
        small_grad = jnp.concatenate(
            [head_grad.reshape(-1), tap_key[:K].reshape(-1)]
        )
        count = small_grad.shape[0]

        if direct:
            rows_key = (4 * NS) // (n_mp * n_dp)
            small_rows = jnp.pad(small_grad, (0, n_mp * n_dp * D - count)).reshape(n_mp, n_dp, D)
            small_rows = jnp.take(small_rows, order, axis=0).astype(bf16)
            extra = scatter_mp(jnp.concatenate([grad_key, small_rows], axis=1))
            mine_v = both[0].astype(f32) + got_v[0].astype(f32) + far_v.astype(f32)
            targets = jnp.bitwise_xor(natural, dp_index)
            dealt = deal(
                mine_v.astype(bf16).reshape(per, WV, D),
                *deal_targets(owners, targets),
                targets,
                extra[: n_dp * rows_key],
                extra[n_dp * rows_key :],
            )
            own_v = dealt[0].astype(f32)
            for k in range(1, n_dp):
                own_v = own_v + swap(dealt[k], "dp", n_dp, k).astype(f32)
        else:
            mine_v = lax.psum_scatter(
                grad_v.reshape(n_mp, per * WV, D), "mp", scatter_dimension=0, tiled=True
            )[0]
            (dealt,) = deal(
                mine_v.reshape(per, WV, D), *deal_targets(owners, natural), joined=n_dp
            )
            own_v = lax.psum_scatter(dealt, "dp", scatter_dimension=0, tiled=True)[0].astype(f32)

        right_halo = slice(tokens, tokens + HALO)
        halo_l = lax.ppermute(dn_key[right_halo] + dn_value[right_halo], "mp", nexts)
        halo_r = lax.ppermute(dn_key[-HALO:] + dn_value[-HALO:], "mp", prevs)
        halo_l = jnp.where(starts, 0.0, halo_l)
        halo_r = jnp.where(ends, 0.0, halo_r)
        edges = jnp.concatenate([halo_l, jnp.zeros((tokens - 2 * HALO, D), f32), halo_r], axis=0)
        dnormed = dn_gate + dn_key[:tokens] + dn_value[:tokens] + edges
        scaled = dnormed * gain_in
        gain_grad = jnp.sum(dnormed * hidden * scale_in, axis=0)
        cross_in = jnp.sum(scaled * hidden, axis=1, keepdims=True)
        hidden_grad = (
            out_grad.astype(f32) + scale_in * scaled - hidden * scale_in**3 * cross_in / D
        )

        own_v = lax.optimization_barrier(own_v)
        own_go = own_go.astype(f32)
        own_grad = jnp.concatenate([own_go[:PS], own_v[: PS + 2], own_go[PS:]], axis=0)
        own_grad = lax.optimization_barrier(own_grad.reshape(3 * PS + 2, 1, D))
        previous = [
            jnp.transpose(x[0], (2, 0, 1))
            for x in (block_master, block_first, block_second, block_ema)
        ]
        slot_new = adamw_update(
            previous[0], own_grad, previous[1], previous[2], previous[3], MATRIX_RATE
        )
        is_owner = jnp.any(owners == dp_index)
        slot_outs = [
            jnp.transpose(jnp.where(is_owner, renewed, before), (1, 2, 0))[None]
            for renewed, before in zip(slot_new, previous)
        ]
        if direct:
            share = jnp.concatenate(
                [jnp.broadcast_to(gain_grad, (15 - rows_key, D)), own_v[WV - rows_key - 1 :]],
                axis=0,
            ).astype(bf16)
            shares, code = gather_all(share, mp_index, dp_index)
            shares, slot_outs = lax.optimization_barrier((shares, slot_outs))
            *key_new, small_total, gain_total = finish_stage(
                code, shares, bc_weight, bc_first, bc_second, bc_ema
            )
            small_total = small_total.reshape(-1)[:count]
            gain_total = gain_total[0]
        else:
            key_total, small_total, gain_total = lax.psum(
                (grad_key.reshape(4 * NS, D).astype(f32), small_grad, gain_grad), ("dp", "mp")
            )
            key_new = adamw_update(
                bc_weight, jnp.transpose(key_total), bc_first, bc_second, bc_ema, MATRIX_RATE
            )
        head_total = lax.dynamic_slice_in_dim(
            small_total[: H * 10 * PS].reshape(H, 10, PS), mp_index * per, per
        )
        head_new = adamw_update(
            head_small, head_total, head_first, head_second, head_ema, SMALL_RATE
        )
        shared_total = jnp.concatenate(
            [
                small_total[H * 10 * PS :].reshape(K, 4 * NS),
                gain_total.reshape(-1, 4 * NS),
            ],
            axis=0,
        )
        shared_new = adamw_update(
            shared_small, shared_total, shared_first, shared_second, shared_ema, SMALL_RATE
        )
        return (hidden_out, hidden_grad, *slot_outs, *head_new, *key_new, *shared_new)

    return local


def solution(mesh):
    rows = P(("dp", "mp"), None)
    slot = P("mp", "dp", None, None)
    head = P("mp", None, None)
    return jax.shard_map(
        make_local(mesh.shape["dp"], mesh.shape["mp"]),
        mesh=mesh,
        in_specs=(rows, rows, P("dp"), P()) + (slot,) * 4 + (head,) * 4 + (P(),) * 8,
        out_specs=(rows, rows) + (slot,) * 4 + (head,) * 4 + (P(),) * 8,
        check_vma=False,
    )
```

```python
import jax
import jax.numpy as jnp
from jax import lax
from jax.experimental import pallas as pl
from jax.experimental.pallas import tpu as pltpu
from jax.sharding import PartitionSpec as P

D = 768
H = 24
PS = 64
NS = 64
K = 7
STEP = 3
CH = H * PS
BL = 128
GH = 8
NG = H // GH
WV = 80
PAD = 128
HALO = 8
NORM_EPS = 1e-05
BETA_ONE = 0.5
BETA_TWO = 0.5
ADAM_EPS = 1e-08
WEIGHT_DECAY = 0.1
MATRIX_RATE = 0.04
SMALL_RATE = 0.2
AVERAGE_KEEP = 0.75

f32 = jnp.float32
bf16 = jnp.bfloat16
LQ, RQ, KF, KR, WF, WR, EF, ER, XF, XR, RF, RR = range(12)
KINDS = 12


def params(mb=56):
    return pltpu.CompilerParams(
        dimension_semantics=("arbitrary",), vmem_limit_bytes=mb * 1024 * 1024
    )


def cost(micros):
    return pl.CostEstimate(flops=0, transcendentals=0, bytes_accessed=micros * 1_000_000)


def nt(a, b, precision=None):
    return lax.dot_general(
        a, b, (((1,), (1,)), ((), ())), preferred_element_type=f32, precision=precision
    )


def nn(a, b, precision=None):
    return lax.dot_general(
        a, b, (((1,), (0,)), ((), ())), preferred_element_type=f32, precision=precision
    )


def tn(a, b):
    return lax.dot_general(a, b, (((0,), (0,)), ((), ())), preferred_element_type=f32)


def lane_sums(x):
    ones = jnp.ones((8, x.shape[1]), bf16)
    high = x.astype(bf16)
    rest = (x - high.astype(f32)).astype(bf16)
    return nt(ones, high) + nt(ones, rest)


def sigmoid(v):
    return 1.0 / (1.0 + jnp.exp(-v))


def lane_first(shape):
    return lax.broadcasted_iota(jnp.int32, shape, len(shape) - 1) < NS


def conv_taps(signal, taps, sign):
    ext = signal.shape[1]
    total = None
    for k in range(K):
        shift = (sign * (k - K // 2)) % ext
        moved = signal if shift == 0 else pltpu.roll(signal, shift, axis=1)
        term = moved.astype(f32) * taps[:, k : k + 1]
        total = term if total is None else total + term
    return total


def causal_masks():
    row = lax.broadcasted_iota(jnp.int32, (BL, BL), 0)
    col = lax.broadcasted_iota(jnp.int32, (BL, BL), 1)
    return row < col, row > col


def stacked_keys(a, b):
    zero = jnp.zeros_like(a)
    return jnp.concatenate(
        [jnp.concatenate([a, zero], axis=1), jnp.concatenate([zero, b], axis=1)], axis=0
    )


def key_kernel(nx_ref, w_ref, taps_ref, p_ref, u_ref, k_ref, st_ref):
    tokens = u_ref.shape[1]
    proj = nt(w_ref[...], nx_ref[...])
    pre = conv_taps(proj, taps_ref[...], -1)
    key = pre * sigmoid(pre)
    ext = key.shape[1]
    b_f = key[:NS, :tokens].astype(bf16)
    c_f = pltpu.roll(key[NS : 2 * NS], 1, axis=1)[:, :tokens].astype(bf16)
    b_r = key[2 * NS : 3 * NS, :tokens].astype(bf16)
    c_r = pltpu.roll(key[3 * NS :], ext - 1, axis=1)[:, :tokens].astype(bf16)
    p_ref[...] = proj
    u_ref[...] = pre[:, :tokens]
    k_ref[...] = jnp.concatenate([b_f, c_f, b_r, c_r], axis=0)
    lower, upper = causal_masks()
    for blk in range(tokens // BL):
        part = slice(blk * BL, (blk + 1) * BL)
        s_f = tn(b_f[:, part], c_f[:, part])
        s_r = tn(b_r[:, part], c_r[:, part])
        st_ref[blk] = jnp.where(lower, s_f, jnp.where(upper, s_r, 0.0))


def key_stage(nx, key_low, taps, tokens):
    ext = nx.shape[0]
    blocks = tokens // BL
    return pl.pallas_call(
        key_kernel,
        out_shape=(
            jax.ShapeDtypeStruct((4 * NS, ext), f32),
            jax.ShapeDtypeStruct((4 * NS, tokens), f32),
            jax.ShapeDtypeStruct((4 * NS, tokens), bf16),
            jax.ShapeDtypeStruct((blocks, BL, BL), f32),
        ),
        compiler_params=pltpu.CompilerParams(vmem_limit_bytes=16 * 1024 * 1024),
        cost_estimate=cost(6),
        name="key_stage",
    )(nx, key_low, taps)


def value_kernel(
    nx_ref, wv_ref, taps_ref, bias_ref, k4_ref, tri_ref,
    v_ref, u_ref, s_ref, rows_ref, tot_ref, sblk_ref, sdev_ref, tdev_ref,
    p_scr, lhs_scr,
):
    tokens = v_ref.shape[1]
    blocks = tokens // BL
    p_scr[...] = nt(wv_ref[...].reshape(GH * WV, D), nx_ref[...])
    for h in range(GH):
        for c in range(PS // 16):
            src = h * WV + c * 16
            dst = h * PS + c * 16
            signal = p_scr[src : src + 16, :].astype(bf16)
            pre = conv_taps(signal, taps_ref[dst : dst + 16, :], -1)[:, :tokens]
            s_ref[dst : dst + 16, :] = signal
            u_ref[dst : dst + 16, :] = pre.astype(bf16)
            v_ref[dst : dst + 16, :] = (pre * sigmoid(pre)).astype(bf16)
    x_f = jnp.concatenate(
        [p_scr[h * WV + PS : h * WV + PS + 1, :tokens] for h in range(GH)], axis=0
    )
    x_r = jnp.concatenate(
        [p_scr[h * WV + PS + 1 : h * WV + PS + 2, :tokens] for h in range(GH)], axis=0
    )
    x_f = x_f + bias_ref[:, 0:1]
    x_r = x_r + bias_ref[:, 1:2]
    rate_f = jnp.maximum(x_f, 0.0) + jnp.log1p(jnp.exp(-jnp.abs(x_f)))
    rate_r = jnp.maximum(x_r, 0.0) + jnp.log1p(jnp.exp(-jnp.abs(x_r)))
    rows_ref[XF] = x_f
    rows_ref[XR] = x_r
    rows_ref[RF] = rate_f
    rows_ref[RR] = rate_r
    cuts = [slice(b * BL, (b + 1) * BL) for b in range(blocks)]
    stack = jnp.concatenate([rate_f[:, c] for c in cuts] + [rate_r[:, c] for c in cuts], axis=0)
    sums = -nn(stack, tri_ref[...], lax.Precision.HIGHEST)
    first = lane_first((GH, BL))
    cum_r = jnp.zeros((GH, BL), f32)
    cum_f = jnp.zeros((GH, BL), f32)
    state = jnp.zeros((GH * PS, BL), f32)
    for b in range(blocks):
        l_f = sums[b * GH : (b + 1) * GH]
        l_r = sums[(blocks + b) * GH : (blocks + b + 1) * GH]
        r_f = rate_f[:, cuts[b]]
        r_r = rate_r[:, cuts[b]]
        end_f = jnp.broadcast_to(l_f[:, BL - 1 : BL], (GH, BL))
        end_r = jnp.broadcast_to(l_r[:, BL - 1 : BL], (GH, BL))
        w_f = jnp.exp(end_f - l_f) * r_f
        w_r = jnp.exp(l_r + r_r) * r_r
        rows_ref[LQ, :, cuts[b]] = l_f + r_f
        rows_ref[RQ, :, cuts[b]] = -l_r
        rows_ref[KF, :, cuts[b]] = l_f - jnp.log(r_f)
        rows_ref[KR, :, cuts[b]] = -(l_r + r_r + jnp.log(r_r))
        rows_ref[WF, :, cuts[b]] = w_f
        rows_ref[WR, :, cuts[b]] = w_r
        rows_ref[EF, :, cuts[b]] = jnp.exp(l_f + r_f)
        rows_ref[ER, :, cuts[b]] = jnp.exp(end_r - l_r)
        tot_ref[b] = jnp.where(first, end_f, end_r)
        for h in range(GH):
            span = slice(h * PS, (h + 1) * PS)
            vals = v_ref[span, cuts[b]].astype(f32)
            lhs_scr[span, :BL] = (vals * w_f[h : h + 1]).astype(bf16)
            lhs_scr[span, BL:] = (vals * w_r[h : h + 1]).astype(bf16)
        keys = stacked_keys(k4_ref[:NS, cuts[b]], k4_ref[2 * NS : 3 * NS, cuts[b]])
        local_state = nt(lhs_scr[...], keys)
        sblk_ref[b] = local_state.astype(bf16)
        keep = jnp.where(first, jnp.exp(end_f), 1.0)
        gain = jnp.where(first, 1.0, jnp.exp(cum_r))
        state = jnp.concatenate(
            [
                state[h * PS : (h + 1) * PS] * keep[h : h + 1]
                + local_state[h * PS : (h + 1) * PS] * gain[h : h + 1]
                for h in range(GH)
            ],
            axis=0,
        )
        cum_f = cum_f + end_f
        cum_r = cum_r + end_r
    sdev_ref[...] = state.astype(bf16)
    tdev_ref[...] = jnp.where(first, cum_f, cum_r)


def value_stage(nx, wv, taps, bias, k4, tri, tokens):
    ext = nx.shape[0]
    blocks = tokens // BL
    rows = GH * PS
    return pl.pallas_call(
        value_kernel,
        grid=(NG,),
        in_specs=[
            pl.BlockSpec((ext, D), lambda g: (0, 0), pipeline_mode=pl.Buffered(1)),
            pl.BlockSpec((GH, WV, D), lambda g: (g, 0, 0)),
            pl.BlockSpec((rows, 8), lambda g: (g, 0)),
            pl.BlockSpec((GH, 2), lambda g: (g, 0)),
            pl.BlockSpec((4 * NS, tokens), lambda g: (0, 0)),
            pl.BlockSpec((BL, BL), lambda g: (0, 0)),
        ],
        out_specs=[
            pl.BlockSpec((rows, tokens), lambda g: (g, 0)),
            pl.BlockSpec((rows, tokens), lambda g: (g, 0)),
            pl.BlockSpec((rows, ext), lambda g: (g, 0)),
            pl.BlockSpec((KINDS, GH, tokens), lambda g: (0, g, 0)),
            pl.BlockSpec((blocks, GH, BL), lambda g: (0, g, 0)),
            pl.BlockSpec((blocks, rows, BL), lambda g: (0, g, 0)),
            pl.BlockSpec((rows, BL), lambda g: (g, 0)),
            pl.BlockSpec((GH, BL), lambda g: (g, 0)),
        ],
        out_shape=(
            jax.ShapeDtypeStruct((CH, tokens), bf16),
            jax.ShapeDtypeStruct((CH, tokens), bf16),
            jax.ShapeDtypeStruct((CH, ext), bf16),
            jax.ShapeDtypeStruct((KINDS, H, tokens), f32),
            jax.ShapeDtypeStruct((blocks, H, BL), f32),
            jax.ShapeDtypeStruct((blocks, CH, BL), bf16),
            jax.ShapeDtypeStruct((CH, BL), bf16),
            jax.ShapeDtypeStruct((H, BL), f32),
        ),
        scratch_shapes=[pltpu.VMEM((GH * WV, ext), f32), pltpu.VMEM((rows, 2 * BL), bf16)],
        compiler_params=params(),
        cost_estimate=cost(27),
        name="value_stage",
    )(nx, wv, taps, bias, k4, tri)


def chain_kernel(flip, copies, tokens, twist, meta_ref, sblk_ref, tot_ref, far_ref, *refs):
    states = refs[:copies]
    if flip:
        other_ref, out_ref, dot_ref = refs[copies:]
    else:
        (out_ref,) = refs[copies:]
    blocks = sblk_ref.shape[0]
    per = sblk_ref.shape[1] // PS
    step = pl.program_id(0)
    first = lane_first((1, BL))
    wide = lane_first((PS, BL))
    up_lanes = jnp.logical_not(wide) if flip else wide
    here = meta_ref[0]
    length = meta_ref[1]
    sequence = here * tokens // length
    places = [meta_ref[2 + k] for k in range(copies)]
    same = [(place * tokens // length) == sequence for place in places]
    for i in range(per):
        span = slice(i * PS, (i + 1) * PS)
        head = step * per + i
        totals = []
        for k in range(copies):
            place = twist(k, step) * per + i
            parts = [far_ref[k, pl.ds(part * H + place, 1), :] for part in range(3)]
            totals.append(parts[0] + parts[1] + parts[2])
        entering = jnp.zeros((PS, BL), f32)
        for k in range(copies):
            left = jnp.zeros((1, BL), f32)
            right = jnp.zeros((1, BL), f32)
            for q in range(copies):
                if q != k:
                    between = (places[q] > places[k]) & (places[q] < here)
                    left = left + totals[q] * between.astype(f32)
                    between = (places[q] < places[k]) & (places[q] > here)
                    right = right + totals[q] * between.astype(f32)
            from_left = jnp.exp(left) * (same[k] & (places[k] < here)).astype(f32)
            from_right = jnp.exp(right) * (same[k] & (places[k] > here)).astype(f32)
            if flip:
                weight = jnp.where(first, from_right, from_left)
            else:
                weight = jnp.where(first, from_left, from_right)
            entering = entering + weight * states[k][span, :].astype(f32)
        decay = [jnp.exp(tot_ref[b, pl.ds(head, 1), :]) for b in range(blocks)]
        locals_ = [sblk_ref[b, span, :].astype(f32) for b in range(blocks)]
        up = [entering]
        down = [entering]
        for b in range(blocks):
            up.append(up[-1] * decay[b] + locals_[b])
            rev = blocks - 1 - b
            down.append(down[-1] * decay[rev] + locals_[rev])
        down = down[::-1]
        for b in range(blocks):
            both = jnp.where(up_lanes, up[b], down[b + 1])
            out_ref[b, span, :] = both.astype(bf16)
            if flip:
                before = other_ref[b - 1 if b > 0 else blocks, span, :]
                beyond = other_ref[b + 1, span, :]
                far = jnp.where(wide, beyond.astype(f32), before.astype(f32))
                dot_ref[b, pl.ds(head, 1), :] = jnp.sum(both * far, axis=0, keepdims=True)
        if not flip:
            out_ref[blocks, span, :] = jnp.where(up_lanes, up[blocks], down[0]).astype(bf16)


def chain_stage(meta, sblk, tot, far_tot, states, twist, tokens, other=None):
    blocks = sblk.shape[0]
    copies = len(states)
    rows = CH // copies
    flip = other is not None
    in_specs = [
        pl.BlockSpec((blocks, rows, BL), lambda q, meta: (0, q, 0)),
        pl.BlockSpec((blocks, H, BL), lambda q, meta: (0, 0, 0)),
        pl.BlockSpec((copies, 3 * H, BL), lambda q, meta: (0, 0, 0)),
    ]
    for k in range(copies):
        in_specs.append(pl.BlockSpec((rows, BL), lambda q, meta, k=k: (twist(k, q), 0)))
    held = blocks if flip else blocks + 1
    out_specs = [pl.BlockSpec((held, rows, BL), lambda q, meta: (0, q, 0))]
    out_shape = [jax.ShapeDtypeStruct((held, CH, BL), bf16)]
    args = [meta, sblk, tot, far_tot, *states]
    if flip:
        in_specs.append(pl.BlockSpec((blocks + 1, rows, BL), lambda q, meta: (0, q, 0)))
        out_specs.append(pl.BlockSpec((blocks, H, BL), lambda q, meta: (0, 0, 0)))
        out_shape.append(jax.ShapeDtypeStruct((blocks, H, BL), f32))
        args.append(other)

    def body(*refs):
        chain_kernel(flip, copies, tokens, twist, *refs)

    return pl.pallas_call(
        body,
        grid_spec=pltpu.PrefetchScalarGridSpec(
            num_scalar_prefetch=1, grid=(copies,), in_specs=in_specs, out_specs=out_specs
        ),
        out_shape=out_shape,
        compiler_params=params(),
        cost_estimate=cost(7),
        name="chain_back" if flip else "chain_stage",
    )(*args)


def pair_blocks(value):
    zero = jnp.zeros((PS, BL), value.dtype)
    return jnp.concatenate(
        [
            jnp.concatenate([value[:PS], zero], axis=1),
            jnp.concatenate([zero, value[PS:]], axis=1),
        ],
        axis=0,
    )


def intra_kernel(v_ref, rows_ref, st_ref, o_ref):
    lower, _ = causal_masks()
    kf_cols = jnp.transpose(rows_ref[KF])
    kr_cols = jnp.transpose(rows_ref[KR])
    for pair in range(H // 2):
        mats = []
        for h in (2 * pair, 2 * pair + 1):
            gap = jnp.where(
                lower,
                rows_ref[LQ, h : h + 1, :] - kf_cols[:, h : h + 1],
                rows_ref[RQ, h : h + 1, :] - kr_cols[:, h : h + 1],
            )
            decay = jnp.exp(jnp.minimum(gap, 80.0))
            mats.append((decay * st_ref[0]).astype(bf16))
        span = slice(pair * 2 * PS, (pair + 1) * 2 * PS)
        out = nn(pair_blocks(v_ref[span, :]), jnp.concatenate(mats, axis=0))
        o_ref[span, :] = out.astype(o_ref.dtype)


def intra_stage(v, rows, scores):
    tokens = v.shape[1]
    return pl.pallas_call(
        intra_kernel,
        grid=(tokens // BL,),
        in_specs=[
            pl.BlockSpec((CH, BL), lambda b: (0, b)),
            pl.BlockSpec((KINDS, H, BL), lambda b: (0, 0, b)),
            pl.BlockSpec((1, BL, BL), lambda b: (b, 0, 0)),
        ],
        out_specs=pl.BlockSpec((CH, BL), lambda b: (0, b)),
        out_shape=jax.ShapeDtypeStruct((CH, tokens), bf16),
        compiler_params=params(),
        cost_estimate=cost(12),
        name="intra_stage",
    )(v, rows, scores)


def token_kernel(
    oi_ref, v_ref, s_ref, k4_ref, rows_ref, tot_ref, wg_ref, wo_ref,
    nx_ref, hid_ref, go_ref, cols_ref,
    ho_ref, r_ref, dg_ref, do_ref, dsblk_ref, dsdev_ref, rc_ref, dk_ref, small_ref,
    cross_scr, g_scr, dres_scr, mix_scr, gated_scr, lhs_scr, gain_scr, diag_scr,
    dev_scr, cum_scr, wide_scr,
):
    step = pl.program_id(0)
    last = pl.num_programs(0) - 1
    cuts = [slice(j * BL, (j + 1) * BL) for j in range(v_ref.shape[1] // BL)]

    @pl.when(step == 0)
    def _():
        gain_scr[...] = jnp.zeros_like(gain_scr)
        diag_scr[...] = jnp.zeros_like(diag_scr)
        dev_scr[...] = jnp.zeros_like(dev_scr)
        cum_scr[...] = jnp.zeros_like(cum_scr)
        wide_scr[0] = jnp.broadcast_to(cols_ref[:, 0:1], (CH, BL))
        wide_scr[1] = jnp.broadcast_to(cols_ref[:, 1:2], (CH, BL))

    keys = [stacked_keys(k4_ref[NS : 2 * NS, cut], k4_ref[3 * NS :, cut]) for cut in cuts]
    for j, both_keys in enumerate(keys):
        cross_scr[j] = nn(s_ref[j], both_keys)
    g_scr[...] = nt(wg_ref[...], nx_ref[...])
    dres_scr[...] = nt(wo_ref[...], go_ref[...])
    squares = [jnp.zeros((8, BL), f32) for _ in cuts]
    cross = [jnp.zeros((8, BL), f32) for _ in cuts]
    for h in range(H):
        span = slice(h * PS, (h + 1) * PS)
        gain = wide_scr[0, span, :]
        for j, cut in enumerate(cuts):
            part_f = cross_scr[j, span, :BL] * rows_ref[EF, h : h + 1, cut]
            part_r = cross_scr[j, span, BL:] * rows_ref[ER, h : h + 1, cut]
            mix = (
                oi_ref[span, cut].astype(f32)
                + part_f
                + part_r
                + wide_scr[1, span, :] * v_ref[span, cut].astype(f32)
            )
            gate = g_scr[span, cut]
            gated = mix * (gate * sigmoid(gate))
            mix_scr[span, cut] = mix
            gated_scr[span, cut] = gated
            squares[j] = squares[j] + jnp.sum((gated * gated).reshape(PS // 8, 8, BL), axis=0)
            flow = dres_scr[span, cut] * gain * gated
            cross[j] = cross[j] + jnp.sum(flow.reshape(PS // 8, 8, BL), axis=0)
    scales = [
        lax.rsqrt(jnp.sum(x, axis=0, keepdims=True) / CH + NORM_EPS) for x in squares
    ]
    pulls = [
        scale * scale * scale * (jnp.sum(x, axis=0, keepdims=True) / CH)
        for scale, x in zip(scales, cross)
    ]
    for h in range(H):
        span = slice(h * PS, (h + 1) * PS)
        gain = wide_scr[0, span, :]
        diags = diag_scr[span, :]
        gains = gain_scr[span, :]
        for j, cut in enumerate(cuts):
            gated = gated_scr[span, cut]
            normal = gated * scales[j]
            dres = dres_scr[span, cut]
            r_ref[span, cut] = (normal * gain).astype(bf16)
            gains = gains + dres * normal
            dgated = scales[j] * (dres * gain) - gated * pulls[j]
            gate = g_scr[span, cut]
            soft = sigmoid(gate)
            grad_mix = dgated * (gate * soft)
            dg_ref[span, cut] = (
                dgated * mix_scr[span, cut] * (soft * (1.0 + gate * (1.0 - soft)))
            ).astype(bf16)
            diags = diags + grad_mix * v_ref[span, cut].astype(f32)
            do_ref[span, cut] = grad_mix.astype(bf16)
            grad_f = grad_mix * rows_ref[EF, h : h + 1, cut]
            grad_r = grad_mix * rows_ref[ER, h : h + 1, cut]
            rc_ref[0, h : h + 1, cut] = jnp.sum(
                grad_f * cross_scr[j, span, :BL], axis=0, keepdims=True
            )
            rc_ref[1, h : h + 1, cut] = jnp.sum(
                grad_r * cross_scr[j, span, BL:], axis=0, keepdims=True
            )
            lhs_scr[j, span, :BL] = grad_f.astype(bf16)
            lhs_scr[j, span, BL:] = grad_r.astype(bf16)
        diag_scr[span, :] = diags
        gain_scr[span, :] = gains
    out = tn(r_ref[...], wo_ref[...])
    ho_ref[...] = (hid_ref[...].astype(f32) + out).astype(bf16)
    first = lane_first((H, BL))
    for j, cut in enumerate(cuts):
        dstate = nt(lhs_scr[j], keys[j])
        dkeys = tn(s_ref[j], lhs_scr[j])
        dk_ref[:NS, cut] = dkeys[:NS, :BL]
        dk_ref[NS:, cut] = dkeys[NS:, BL:]
        dsblk_ref[j] = dstate.astype(bf16)
        total = tot_ref[j]
        keep = jnp.where(first, 1.0, jnp.exp(total))
        grow = jnp.where(first, jnp.exp(cum_scr[...]), 1.0)
        for h in range(H):
            span = slice(h * PS, (h + 1) * PS)
            dev_scr[span, :] = (
                dev_scr[span, :] * keep[h : h + 1] + dstate[span, :] * grow[h : h + 1]
            )
        cum_scr[...] += total

    @pl.when(step == last)
    def _():
        dsdev_ref[...] = dev_scr[...].astype(bf16)
        small_ref[0] = lane_sums(gain_scr[...])
        small_ref[1] = lane_sums(diag_scr[...])


def token_stage(oi, v, s9, k4, rows, tot, wg, wo, nx, hid, go, cols):
    tokens = v.shape[1]
    blocks = tokens // BL
    two = 2
    wide = two * BL
    whole = dict(pipeline_mode=pl.Buffered(1))
    chan = pl.BlockSpec((CH, wide), lambda b: (0, b))
    toks = pl.BlockSpec((wide, D), lambda b: (b, 0))
    state = pl.BlockSpec((two, CH, BL), lambda b: (b, 0, 0))
    big = pltpu.VMEM((CH, BL), f32)
    large = pltpu.VMEM((CH, wide), f32)
    return pl.pallas_call(
        token_kernel,
        grid=(blocks // two,),
        in_specs=[
            chan,
            chan,
            state,
            pl.BlockSpec((4 * NS, wide), lambda b: (0, b)),
            pl.BlockSpec((KINDS, H, wide), lambda b: (0, 0, b)),
            pl.BlockSpec((two, H, BL), lambda b: (b, 0, 0)),
            pl.BlockSpec((CH, D), lambda b: (0, 0), **whole),
            pl.BlockSpec((CH, D), lambda b: (0, 0), **whole),
            toks,
            toks,
            toks,
            pl.BlockSpec((CH, 8), lambda b: (0, 0), **whole),
        ],
        out_specs=[
            toks,
            chan,
            chan,
            chan,
            state,
            pl.BlockSpec((CH, BL), lambda b: (0, 0)),
            pl.BlockSpec((2, H, wide), lambda b: (0, 0, b)),
            pl.BlockSpec((2 * NS, wide), lambda b: (0, b)),
            pl.BlockSpec((2, 8, CH), lambda b: (0, 0, 0)),
        ],
        out_shape=(
            jax.ShapeDtypeStruct((tokens, D), bf16),
            jax.ShapeDtypeStruct((CH, tokens), bf16),
            jax.ShapeDtypeStruct((CH, tokens), bf16),
            jax.ShapeDtypeStruct((CH, tokens), bf16),
            jax.ShapeDtypeStruct((blocks, CH, BL), bf16),
            jax.ShapeDtypeStruct((CH, BL), bf16),
            jax.ShapeDtypeStruct((2, H, tokens), f32),
            jax.ShapeDtypeStruct((2 * NS, tokens), f32),
            jax.ShapeDtypeStruct((2, 8, CH), f32),
        ),
        scratch_shapes=[pltpu.VMEM((two, CH, 2 * BL), f32)]
        + [large] * 4
        + [pltpu.VMEM((two, CH, 2 * BL), bf16)]
        + [big] * 3
        + [pltpu.VMEM((H, BL), f32), pltpu.VMEM((2, CH, BL), f32)],
        compiler_params=params(),
        cost_estimate=cost(35),
        name="token_stage",
    )(oi, v, s9, k4, rows, tot, wg, wo, nx, hid, go, cols)


def early_grad_kernel(dg_ref, r_ref, nx_ref, go_ref, wg_ref, out_ref, dn_ref):
    gate = nn(dg_ref[...], nx_ref[...]).astype(bf16)
    outp = nn(r_ref[...], go_ref[...]).astype(bf16)
    out_ref[:, :PS, :] = gate.reshape(GH, PS, D)
    out_ref[:, PS:, :] = outp.reshape(GH, PS, D)
    part = tn(dg_ref[...], wg_ref[...])
    step = pl.program_id(0)

    @pl.when(step == 0)
    def _():
        dn_ref[...] = part

    @pl.when(step > 0)
    def _():
        dn_ref[...] += part


def early_grad_stage(dgate, result, nx, go, wg):
    tokens = dgate.shape[1]
    rows = GH * PS
    return pl.pallas_call(
        early_grad_kernel,
        grid=(NG,),
        in_specs=[
            pl.BlockSpec((rows, tokens), lambda g: (g, 0)),
            pl.BlockSpec((rows, tokens), lambda g: (g, 0)),
            pl.BlockSpec((tokens, D), lambda g: (0, 0)),
            pl.BlockSpec((tokens, D), lambda g: (0, 0)),
            pl.BlockSpec((rows, D), lambda g: (g, 0)),
        ],
        out_specs=[
            pl.BlockSpec((GH, 2 * PS, D), lambda g: (g, 0, 0)),
            pl.BlockSpec((tokens, D), lambda g: (0, 0)),
        ],
        out_shape=(
            jax.ShapeDtypeStruct((H, 2 * PS, D), bf16),
            jax.ShapeDtypeStruct((tokens, D), f32),
        ),
        compiler_params=params(24),
        cost_estimate=cost(12),
        name="early_grad",
    )(dgate, result, nx, go, wg)


def intra_back_kernel(
    v_ref, do_ref, rows_ref, st_ref, k4_ref, dkc_ref, dv_ref, rc_ref, dk_ref
):
    lower, upper = causal_masks()
    kf_cols = jnp.transpose(rows_ref[KF])
    kr_cols = jnp.transpose(rows_ref[KR])
    score_grad = jnp.zeros((BL, BL), f32)
    for pair in range(H // 2):
        span = slice(pair * 2 * PS, (pair + 1) * 2 * PS)
        grads = pair_blocks(do_ref[span, :])
        mat_grads = tn(v_ref[span, :], grads)
        down = []
        over = []
        for i, h in enumerate((2 * pair, 2 * pair + 1)):
            gap = jnp.where(
                lower,
                rows_ref[LQ, h : h + 1, :] - kf_cols[:, h : h + 1],
                rows_ref[RQ, h : h + 1, :] - kr_cols[:, h : h + 1],
            )
            decay = jnp.exp(jnp.minimum(gap, 80.0))
            mat = decay * st_ref[0]
            term = decay * mat_grads[:, i * BL : (i + 1) * BL]
            score_grad = score_grad + term
            flow = term * st_ref[0]
            flow_f = jnp.where(lower, flow, 0.0)
            row_f = jnp.sum(flow_f, axis=0, keepdims=True)
            row_all = jnp.sum(flow, axis=0, keepdims=True)
            rc_ref[0, h : h + 1, :] = row_f
            rc_ref[1, h : h + 1, :] = row_all - row_f
            down.append(jnp.where(lower, mat, 0.0).astype(bf16))
            over.append(jnp.where(lower, 0.0, mat).astype(bf16))
        dv_f = nt(grads, jnp.concatenate(down, axis=1))
        dv_r = nt(grads, jnp.concatenate(over, axis=1))
        vals = v_ref[span, :].astype(f32)
        for i, h in enumerate((2 * pair, 2 * pair + 1)):
            half = slice(i * PS, (i + 1) * PS)
            rc_ref[2, h : h + 1, :] = jnp.sum(vals[half] * dv_f[half], axis=0, keepdims=True)
            rc_ref[3, h : h + 1, :] = jnp.sum(vals[half] * dv_r[half], axis=0, keepdims=True)
        dv_ref[span, :] = (dv_f + dv_r).astype(dv_ref.dtype)
    grad_f = jnp.where(lower, score_grad, 0.0).astype(bf16)
    grad_r = jnp.where(upper, score_grad, 0.0).astype(bf16)
    b_f = k4_ref[:NS, :]
    c_f = k4_ref[NS : 2 * NS, :]
    b_r = k4_ref[2 * NS : 3 * NS, :]
    c_r = k4_ref[3 * NS :, :]
    dk_ref[:NS, :] = nt(c_f, grad_f)
    dk_ref[NS : 2 * NS, :] = nn(b_f, grad_f) + dkc_ref[:NS, :]
    dk_ref[2 * NS : 3 * NS, :] = nt(c_r, grad_r)
    dk_ref[3 * NS :, :] = nn(b_r, grad_r) + dkc_ref[NS:, :]


def intra_back_stage(v, do, rows, scores, k4, dkc):
    tokens = v.shape[1]
    chan = pl.BlockSpec((CH, BL), lambda b: (0, b))
    return pl.pallas_call(
        intra_back_kernel,
        grid=(tokens // BL,),
        in_specs=[
            chan,
            chan,
            pl.BlockSpec((KINDS, H, BL), lambda b: (0, 0, b)),
            pl.BlockSpec((1, BL, BL), lambda b: (b, 0, 0)),
            pl.BlockSpec((4 * NS, BL), lambda b: (0, b)),
            pl.BlockSpec((2 * NS, BL), lambda b: (0, b)),
        ],
        out_specs=[
            chan,
            pl.BlockSpec((4, H, BL), lambda b: (0, 0, b)),
            pl.BlockSpec((4 * NS, BL), lambda b: (0, b)),
        ],
        out_shape=(
            jax.ShapeDtypeStruct((CH, tokens), bf16),
            jax.ShapeDtypeStruct((4, H, tokens), f32),
            jax.ShapeDtypeStruct((4 * NS, tokens), f32),
        ),
        compiler_params=params(),
        cost_estimate=cost(18),
        name="intra_back",
    )(v, do, rows, scores, k4, dkc)


def cross_back_kernel(
    dvi_ref, v_ref, do_ref, u_ref, ds_ref, k4_ref, rows_ref, rci_ref, rcc_ref,
    x_ref, dki_ref, cols_ref, after_ref,
    dpre_ref, dx_ref, dk_ref,
    cross_scr, lhs_scr, c_scr, wide_scr,
):
    b_f = k4_ref[:NS, :]
    b_r = k4_ref[2 * NS : 3 * NS, :]

    @pl.when(pl.program_id(0) == 0)
    def _():
        wide_scr[...] = jnp.broadcast_to(cols_ref[:, 1:2], (CH, BL))

    cross_scr[...] = nn(ds_ref[0], stacked_keys(b_f, b_r))
    for h in range(H):
        span = slice(h * PS, (h + 1) * PS)
        vals = v_ref[span, :].astype(f32)
        w_f = rows_ref[WF, h : h + 1, :]
        w_r = rows_ref[WR, h : h + 1, :]
        dv_f = cross_scr[span, :BL] * w_f
        dv_r = cross_scr[span, BL:] * w_r
        c_scr[0, h : h + 1, :] = jnp.sum(vals * dv_f, axis=0, keepdims=True)
        c_scr[1, h : h + 1, :] = jnp.sum(vals * dv_r, axis=0, keepdims=True)
        lhs_scr[span, :BL] = (vals * w_f).astype(bf16)
        lhs_scr[span, BL:] = (vals * w_r).astype(bf16)
        grad = (
            dvi_ref[span, :].astype(f32)
            + dv_f
            + dv_r
            + wide_scr[span, :] * do_ref[span, :].astype(f32)
        )
        pre = u_ref[span, :].astype(f32)
        soft = sigmoid(pre)
        dpre_ref[span, :] = (grad * (soft * (1.0 + pre * (1.0 - soft)))).astype(dpre_ref.dtype)
    dkeys = tn(ds_ref[0], lhs_scr[...])
    dk_ref[...] = dki_ref[...]
    dk_ref[:NS, :] += dkeys[:NS, :BL]
    dk_ref[2 * NS : 3 * NS, :] += dkeys[NS:, BL:]
    first = lane_first((H, BL))
    through_f = jnp.sum(jnp.where(first, x_ref[0], 0.0), axis=1, keepdims=True)
    through_r = jnp.sum(jnp.where(first, 0.0, x_ref[0]), axis=1, keepdims=True)
    row_f = rci_ref[0] + rcc_ref[0]
    row_r = rci_ref[1] + rcc_ref[1]
    col_f = rci_ref[2] + c_scr[0]
    col_r = rci_ref[3] + c_scr[1]
    after = after_ref[...]
    strict = lax.Precision.HIGHEST
    sum_f = nn(row_f, after, strict) - nn(col_f, after, strict) - col_f + through_f
    sum_r = nt(row_r, after, strict) - nt(col_r, after, strict) - col_r + through_r
    for kind, (total, col, x_kind, r_kind) in enumerate(
        ((sum_f, col_f, XF, RF), (sum_r, col_r, XR, RR))
    ):
        soft = sigmoid(rows_ref[x_kind])
        rate = rows_ref[r_kind]
        live = rate > 0.0
        ratio = jnp.where(live, soft / jnp.where(live, rate, 1.0), 1.0)
        dx_ref[kind] = col * ratio - total * soft


def cross_back_stage(dvi, v, do, u, ds9, k4, rows, rci, rcc, x9, dki, cols, after):
    tokens = v.shape[1]
    chan = pl.BlockSpec((CH, BL), lambda b: (0, b))
    keys = pl.BlockSpec((4 * NS, BL), lambda b: (0, b))
    return pl.pallas_call(
        cross_back_kernel,
        grid=(tokens // BL,),
        in_specs=[
            chan,
            chan,
            chan,
            chan,
            pl.BlockSpec((1, CH, BL), lambda b: (b, 0, 0)),
            keys,
            pl.BlockSpec((KINDS, H, BL), lambda b: (0, 0, b)),
            pl.BlockSpec((4, H, BL), lambda b: (0, 0, b)),
            pl.BlockSpec((2, H, BL), lambda b: (0, 0, b)),
            pl.BlockSpec((1, H, BL), lambda b: (b, 0, 0)),
            keys,
            pl.BlockSpec((CH, 8), lambda b: (0, 0)),
            pl.BlockSpec((BL, BL), lambda b: (0, 0)),
        ],
        out_specs=[chan, pl.BlockSpec((2, H, BL), lambda b: (0, 0, b)), keys],
        out_shape=(
            jax.ShapeDtypeStruct((CH, tokens), bf16),
            jax.ShapeDtypeStruct((2, H, tokens), f32),
            jax.ShapeDtypeStruct((4 * NS, tokens), f32),
        ),
        scratch_shapes=[
            pltpu.VMEM((CH, 2 * BL), f32),
            pltpu.VMEM((CH, 2 * BL), bf16),
            pltpu.VMEM((2, H, BL), f32),
            pltpu.VMEM((CH, BL), f32),
        ],
        compiler_params=params(),
        cost_estimate=cost(16),
        name="cross_back",
    )(dvi, v, do, u, ds9, k4, rows, rci, rcc, x9, dki, cols, after)


def key_pre_kernel(dk_ref, u_ref, edge_ref, out_ref):
    tokens = u_ref.shape[1]
    lane = lax.broadcasted_iota(jnp.int32, (NS, tokens), 1)
    d_cf = pltpu.roll(dk_ref[NS : 2 * NS, :], tokens - 1, axis=1)
    d_cf = jnp.where(lane == tokens - 1, edge_ref[:, 0:1], d_cf)
    d_cr = pltpu.roll(dk_ref[3 * NS :, :], 1, axis=1)
    d_cr = jnp.where(lane == 0, edge_ref[:, 1:2], d_cr)
    grad = jnp.concatenate([dk_ref[:NS, :], d_cf, dk_ref[2 * NS : 3 * NS, :], d_cr], axis=0)
    pre = u_ref[...]
    soft = sigmoid(pre)
    out_ref[...] = grad * (soft * (1.0 + pre * (1.0 - soft)))


def key_pre_stage(dk, u, edge):
    return pl.pallas_call(
        key_pre_kernel,
        out_shape=jax.ShapeDtypeStruct(u.shape, f32),
        compiler_params=pltpu.CompilerParams(vmem_limit_bytes=16 * 1024 * 1024),
        cost_estimate=cost(3),
        name="key_pre",
    )(dk, u, edge)


def conv_back_rows(dpre, taps, signal):
    rows, tokens = dpre.shape
    ext = signal.shape[1]
    wide = jnp.concatenate([dpre, jnp.zeros((rows, ext - tokens), dpre.dtype)], axis=1)
    total = None
    sums = []
    for k in range(K):
        shift = (k - K // 2) % ext
        moved = wide if shift == 0 else pltpu.roll(wide, shift, axis=1)
        moved = moved.astype(f32)
        term = moved * taps[:, k : k + 1]
        total = term if total is None else total + term
        prod = moved * signal
        part = prod[:, :BL]
        for b in range(1, ext // BL):
            part = part + prod[:, b * BL : (b + 1) * BL]
        sums.append(part)
    return total, sums


def key_back_kernel(
    meta_ref, dpre_ref, taps_ref, p_ref, nx_ref, w_ref, g_ref, dn_ref, t_ref, low_scr, g_scr, t_scr
):
    for c in range(4 * NS // 16):
        span = slice(c * 16, (c + 1) * 16)
        total, sums = conv_back_rows(dpre_ref[span, :], taps_ref[span, :], p_ref[span, :])
        low_scr[span, :] = total.astype(bf16)
        for k in range(K):
            t_scr[k, span, :] = sums[k]
    for k in range(K):
        t_ref[k : k + 1, :] = lane_sums(t_scr[k])[:1]
    t_ref[K : K + 1, :] = jnp.zeros((1, 4 * NS), f32)
    g_scr[...] = nn(low_scr[...], nx_ref[...])
    count, rows, _ = g_ref.shape
    for q in range(count):
        start = pl.multiple_of(meta_ref[2 + q] * rows, 8)
        g_ref[q] = g_scr[pl.ds(start, rows), :].astype(g_ref.dtype)
    dn_ref[...] = tn(low_scr[...], w_ref[...])


def key_back_stage(meta, dpre, taps, proj, nx, key_low):
    ext = nx.shape[0]
    count = meta.shape[0] - 2
    args = (dpre, taps, proj, nx, key_low)
    outs = (
        jax.ShapeDtypeStruct((count, 4 * NS // count, D), bf16),
        jax.ShapeDtypeStruct((ext, D), f32),
        jax.ShapeDtypeStruct((8, 4 * NS), f32),
    )

    def whole(shape):
        return pl.BlockSpec(shape, lambda i, meta: (0,) * len(shape))

    return pl.pallas_call(
        key_back_kernel,
        grid_spec=pltpu.PrefetchScalarGridSpec(
            num_scalar_prefetch=1,
            grid=(1,),
            in_specs=[whole(x.shape) for x in args],
            out_specs=[whole(x.shape) for x in outs],
            scratch_shapes=[
                pltpu.VMEM((4 * NS, ext), bf16),
                pltpu.VMEM((4 * NS, D), f32),
                pltpu.VMEM((K, 4 * NS, BL), f32),
            ],
        ),
        out_shape=outs,
        compiler_params=params(16),
        cost_estimate=cost(8),
        name="key_back",
    )(meta, *args)


def value_back_kernel(
    dpre_ref, taps_ref, s_ref, dx_ref, nx_ref, wv_ref, g_ref, dn_ref, t_ref, low_scr, tap_scr
):
    tokens = dpre_ref.shape[1]
    ext = s_ref.shape[1]
    step = pl.program_id(0)
    for h in range(GH):
        for c in range(PS // 16):
            src = h * PS + c * 16
            span = slice(src, src + 16)
            total, sums = conv_back_rows(
                dpre_ref[span, :], taps_ref[span, :], s_ref[span, :].astype(f32)
            )
            low_scr[h * WV + c * 16 : h * WV + (c + 1) * 16, :] = total.astype(bf16)
            for k in range(K):
                tap_scr[k, span, :] = sums[k]
        tail = jnp.concatenate(
            [
                dx_ref[0, h : h + 1, :],
                dx_ref[1, h : h + 1, :],
                jnp.zeros((14, tokens), f32),
            ],
            axis=0,
        )
        low_scr[h * WV + PS : (h + 1) * WV, :tokens] = tail.astype(bf16)
        low_scr[h * WV + PS : (h + 1) * WV, tokens:] = jnp.zeros((16, ext - tokens), bf16)
    for k in range(K):
        t_ref[0, k : k + 1, :] = lane_sums(tap_scr[k])[:1]
    t_ref[0, K : K + 1, :] = jnp.zeros((1, GH * PS), f32)
    g_ref[...] = nn(low_scr[...], nx_ref[...]).reshape(GH, WV, D).astype(g_ref.dtype)
    part = tn(low_scr[...], wv_ref[...].reshape(GH * WV, D))

    @pl.when(step == 0)
    def _():
        dn_ref[...] = part

    @pl.when(step > 0)
    def _():
        dn_ref[...] += part


def value_back_stage(dpre, taps, s, dx, nx, wv):
    tokens = dpre.shape[1]
    ext = nx.shape[0]
    rows = GH * PS
    return pl.pallas_call(
        value_back_kernel,
        grid=(NG,),
        in_specs=[
            pl.BlockSpec((rows, tokens), lambda g: (g, 0)),
            pl.BlockSpec((rows, 8), lambda g: (g, 0)),
            pl.BlockSpec((rows, ext), lambda g: (g, 0)),
            pl.BlockSpec((2, GH, tokens), lambda g: (0, g, 0)),
            pl.BlockSpec((ext, D), lambda g: (0, 0), pipeline_mode=pl.Buffered(1)),
            pl.BlockSpec((GH, WV, D), lambda g: (g, 0, 0)),
        ],
        out_specs=[
            pl.BlockSpec((GH, WV, D), lambda g: (g, 0, 0)),
            pl.BlockSpec((ext, D), lambda g: (0, 0)),
            pl.BlockSpec((1, 8, rows), lambda g: (g, 0, 0)),
        ],
        out_shape=(
            jax.ShapeDtypeStruct((H, WV, D), bf16),
            jax.ShapeDtypeStruct((ext, D), f32),
            jax.ShapeDtypeStruct((NG, 8, rows), f32),
        ),
        scratch_shapes=[
            pltpu.VMEM((GH * WV, ext), bf16),
            pltpu.VMEM((K, rows, BL), f32),
        ],
        compiler_params=params(),
        cost_estimate=cost(27),
        name="value_back",
    )(dpre, taps, s, dx, nx, wv)


def pick(sources, index):
    count = index.shape[0]
    rows, width = sources[0].shape[1:]

    def body(index_ref, *refs):
        out_ref = refs[-1]
        for i in range(count):
            first = 0
            for ref in refs[:-1]:
                n = ref.shape[0]
                local = index_ref[i] - first

                @pl.when((local >= 0) & (local < n))
                def _(ref=ref, local=local, i=i):
                    out_ref[i] = ref[local]

                first += n

    return pl.pallas_call(
        body,
        grid_spec=pltpu.PrefetchScalarGridSpec(
            num_scalar_prefetch=1,
            grid=(1,),
            in_specs=[pl.BlockSpec(x.shape, lambda i, index: (0, 0, 0)) for x in sources],
            out_specs=pl.BlockSpec((count, rows, width), lambda i, index: (0, 0, 0)),
        ),
        out_shape=jax.ShapeDtypeStruct((count, rows, width), sources[0].dtype),
        compiler_params=params(16),
        cost_estimate=cost(3),
        name="pick",
    )(index, *sources)


def pick_two_kernel(index_ref, slots_ref, gate_ref, out_ref):
    for h in range(H):
        gate_ref[h] = slots_ref[index_ref[h], :PS, :]
        out_ref[h] = slots_ref[index_ref[h], PS:, :]


def pick_two(slots, index):
    half = jax.ShapeDtypeStruct((H, PS, D), slots.dtype)
    return pl.pallas_call(
        pick_two_kernel,
        grid_spec=pltpu.PrefetchScalarGridSpec(
            num_scalar_prefetch=1,
            grid=(1,),
            in_specs=[pl.BlockSpec(slots.shape, lambda i, index: (0, 0, 0))],
            out_specs=[pl.BlockSpec((H, PS, D), lambda i, index: (0, 0, 0))] * 2,
        ),
        out_shape=(half, half),
        compiler_params=params(),
        cost_estimate=cost(6),
        name="pick_two",
    )(index, slots)


def deal(source, index, live, target=None, extra=None, single=None, joined=0):
    count = index.shape[0]
    rows, width = source.shape[1:]
    more = 0 if extra is None else extra.shape[0] // count
    plan = [index, live] if extra is None else [index, live, target]
    args = [source] if extra is None else [source, extra, single]

    def body(*refs):
        index_ref, live_ref = refs[:2]
        source_ref = refs[len(plan)]
        outs = refs[len(plan) + len(args) :]
        for k in range(count):
            value = source_ref[index_ref[k]]
            value = jnp.where(live_ref[k] > 0, value, jnp.zeros_like(value))
            if joined:
                outs[k // joined][k % joined] = value
            elif more:
                start = pl.multiple_of(refs[2][k] * more, 8)
                last = refs[len(plan) + 1][pl.ds(start, more), :]
                one = refs[len(plan) + 2][pl.ds(refs[2][k], 1), :]
                space = jnp.zeros((16 - more - 1, width), f32)
                last = jnp.concatenate([space, one, last], axis=0)
                outs[k][: rows - 16] = value[: rows - 16]
                outs[k][rows - 16 :] = (value[rows - 16 :].astype(f32) + last).astype(bf16)
            else:
                outs[k][...] = value

    def whole(shape):
        return pl.BlockSpec(shape, lambda i, *plan: (0,) * len(shape))

    if joined:
        shapes = [jax.ShapeDtypeStruct((joined, rows, width), source.dtype)] * (count // joined)
    else:
        shapes = [jax.ShapeDtypeStruct((rows, width), source.dtype)] * count
    return pl.pallas_call(
        body,
        grid_spec=pltpu.PrefetchScalarGridSpec(
            num_scalar_prefetch=len(plan),
            grid=(1,),
            in_specs=[whole(x.shape) for x in args],
            out_specs=[whole(x.shape) for x in shapes],
        ),
        out_shape=shapes,
        compiler_params=params(16),
        cost_estimate=cost(3),
        name="deal",
    )(*plan, *args)


def adamw_update(weight, gradient, first_moment, second, average, step_rate):
    first_new = BETA_ONE * first_moment + (1.0 - BETA_ONE) * gradient
    second_new = BETA_TWO * second + (1.0 - BETA_TWO) * gradient * gradient
    correct_one = 1.0 - BETA_ONE**STEP
    correct_two = 1.0 - BETA_TWO**STEP
    normalized = first_new / correct_one / (jnp.sqrt(second_new / correct_two) + ADAM_EPS)
    weight_new = weight - step_rate * (normalized + WEIGHT_DECAY * weight)
    average_new = AVERAGE_KEEP * average + (1.0 - AVERAGE_KEEP) * weight_new
    return (weight_new, first_new, second_new, average_new)


def finish_kernel(
    code_ref, share_ref, w_ref, m_ref, v_ref, a_ref,
    w_out, m_out, v_out, a_out, small_ref, gain_ref, scr,
):
    count, rows, _ = share_ref.shape
    keys = 4 * NS // count
    total = jnp.zeros((1, D), f32)
    for i in range(count):
        share = share_ref[code_ref[i]].astype(f32)
        scr[i * keys : (i + 1) * keys, :] = share[rows - keys :]
        small_ref[i : i + 1, :] = share[rows - keys - 1 : rows - keys]
        total = total + share[:1]
    gain_ref[...] = jnp.broadcast_to(total, (8, D))
    new = adamw_update(
        w_ref[...], jnp.transpose(scr[...]), m_ref[...], v_ref[...], a_ref[...], MATRIX_RATE
    )
    for out, value in zip((w_out, m_out, v_out, a_out), new):
        out[...] = value


def finish_stage(code, shares, weight, first, second, ema):
    count = shares.shape[0]
    args = (shares, weight, first, second, ema)
    outs = [jax.ShapeDtypeStruct(weight.shape, f32)] * 4 + [
        jax.ShapeDtypeStruct((count, D), f32),
        jax.ShapeDtypeStruct((8, D), f32),
    ]

    def whole(shape):
        return pl.BlockSpec(shape, lambda i, code: (0,) * len(shape))

    return pl.pallas_call(
        finish_kernel,
        grid_spec=pltpu.PrefetchScalarGridSpec(
            num_scalar_prefetch=1,
            grid=(1,),
            in_specs=[whole(x.shape) for x in args],
            out_specs=[whole(x.shape) for x in outs],
            scratch_shapes=[pltpu.VMEM((4 * NS, D), f32)],
        ),
        out_shape=outs,
        compiler_params=params(16),
        cost_estimate=cost(5),
        name="finish_stage",
    )(code, *args)


def make_local(n_dp, n_mp):
    per = H // n_mp
    direct = n_mp == 4 and n_dp == 8

    def swap(x, axis, size, bit):
        return lax.ppermute(x, axis, [(i, i ^ bit) for i in range(size)])

    def head_rows(mp_index):
        rows = jnp.arange(n_mp, dtype=jnp.int32)
        return jnp.bitwise_xor(rows, mp_index) if direct else rows

    def over_mp(x):
        if direct:
            far = swap(x, "mp", n_mp, 2)
            return [x, swap(x, "mp", n_mp, 1), far, swap(far, "mp", n_mp, 1)]
        copies = lax.all_gather(x, "mp", axis=0)
        return [copies[k] for k in range(n_mp)]

    def gather_dp(part):
        return [part[None]] + [swap(part, "dp", n_dp, k)[None] for k in range(1, n_dp)]

    def pick_own(pieces, owners, dp_index):
        return pick(pieces, jnp.bitwise_xor(owners, dp_index))

    def scatter_mp(grads):
        got = swap(jnp.stack([grads[1], grads[3]]), "mp", n_mp, 1)
        away = (grads[2].astype(f32) + got[1].astype(f32)).astype(bf16)
        mine = grads[0].astype(f32) + got[0].astype(f32)
        return mine + swap(away, "mp", n_mp, 2).astype(f32)

    def deal_targets(owners, targets):
        match = targets[:, None] == owners[None, :]
        return jnp.argmax(match, axis=1).astype(jnp.int32), jnp.any(match, axis=1).astype(jnp.int32)

    def gather_all(x, mp_index, dp_index):
        both = x[None]
        for axis, size, bit in (
            ("dp", n_dp, 2), ("dp", n_dp, 4), ("dp", n_dp, 1), ("mp", n_mp, 2), ("mp", n_mp, 1)
        ):
            both = jnp.concatenate([both, swap(both, axis, size, bit)], axis=0)
        far = jnp.bitwise_xor(jnp.arange(n_mp, dtype=jnp.int32), mp_index)[:, None]
        off = jnp.bitwise_xor(jnp.arange(n_dp, dtype=jnp.int32), dp_index)[None, :]
        code = ((off >> 1) & 3) + 4 * (off & 1) + 8 * (far >> 1) + 16 * (far & 1)
        return both, code.reshape(-1)

    def local(
        hidden_in, out_grad, seq_len, owner_list,
        block_master, block_first, block_second, block_ema,
        head_small, head_first, head_second, head_ema,
        bc_weight, bc_first, bc_second, bc_ema,
        shared_small, shared_first, shared_second, shared_ema,
    ):
        tokens = hidden_in.shape[0]
        mp_index = lax.axis_index("mp")
        dp_index = lax.axis_index("dp")
        owners = lax.dynamic_slice_in_dim(owner_list, mp_index * per, per)
        order = head_rows(mp_index)
        bounds = (mp_index + jnp.arange(2, dtype=jnp.int32)) * tokens % seq_len == 0
        starts = bounds[:1].reshape(1, 1)
        ends = bounds[1:].reshape(1, 1)
        meta = jnp.concatenate([mp_index.reshape(1), seq_len, order]).astype(jnp.int32)
        nexts = [(i, i + 1) for i in range(n_mp - 1)]
        prevs = [(i + 1, i) for i in range(n_mp - 1)]

        slot_t = jnp.transpose(block_master[0, 0]).astype(bf16)
        part_v = jnp.concatenate(
            [slot_t[PS : 2 * PS + 2], jnp.zeros((WV - PS - 2, D), bf16)], axis=0
        )
        part_go = jnp.concatenate([slot_t[:PS], slot_t[2 * PS + 2 :]], axis=0)
        if direct:
            pieces_v = gather_dp(part_v)
            mine_v = pick_own(pieces_v, owners, dp_index)
            far_v = swap(mine_v, "mp", n_mp, 2)
            near_v = swap(mine_v, "mp", n_mp, 1)
            slots = lax.all_gather(part_go, ("mp", "dp"), axis=0)
            rows_of = jnp.repeat(order, per)
            heads_of = rows_of * per + jnp.arange(H, dtype=jnp.int32) % per
            wg, wo = pick_two(slots, rows_of * n_dp + jnp.take(owner_list, heads_of))
        else:
            mine_v = pick([lax.all_gather(part_v, "dp", axis=0)], owners)
            wv = jnp.concatenate(over_mp(mine_v), axis=0)
            mine_go = pick([lax.all_gather(part_go, "dp", axis=0)], owners)
            all_go = over_mp(mine_go)
            wg = jnp.concatenate([x[:, :PS] for x in all_go], axis=0)
            wo = jnp.concatenate([x[:, PS:] for x in all_go], axis=0)
        wg = wg.reshape(CH, D)
        wo = wo.reshape(CH, D)

        hidden = hidden_in.astype(f32)
        gain_in = shared_small[K:].reshape(D)
        scale_in = lax.rsqrt(jnp.mean(hidden * hidden, axis=1, keepdims=True) + NORM_EPS)
        normed = (hidden * scale_in * gain_in).astype(bf16)
        from_left = lax.ppermute(normed[-HALO:], "mp", nexts)
        from_right = lax.ppermute(normed[:HALO], "mp", prevs)
        from_left = jnp.where(starts, jnp.zeros_like(from_left), from_left)
        from_right = jnp.where(ends, jnp.zeros_like(from_right), from_right)
        nx = jnp.concatenate(
            [normed, from_right, jnp.zeros((PAD - 2 * HALO, D), bf16), from_left], axis=0
        )

        heads = jnp.concatenate(over_mp(head_small), axis=0)
        taps_v = jnp.transpose(heads[:, 1 : 1 + K, :], (0, 2, 1)).reshape(CH, K)
        taps_v = jnp.pad(taps_v, ((0, 0), (0, 1)))
        cols = jnp.stack([heads[:, 0].reshape(CH), heads[:, K + 1].reshape(CH)], axis=1)
        cols = jnp.pad(cols, ((0, 0), (0, 6)))
        bias = heads[:, K + 2, :2]
        key_low = jnp.transpose(bc_weight).astype(bf16)
        taps_k = jnp.pad(jnp.transpose(shared_small[:K]), ((0, 0), (0, 1)))
        ids = jnp.arange(BL)
        tri = (ids[:, None] <= ids[None, :]).astype(f32)
        after = (ids[:, None] > ids[None, :]).astype(f32)

        key_proj, key_u, k4, scores = key_stage(nx, key_low, taps_k, tokens)
        if direct:
            far_v, k4 = lax.optimization_barrier((far_v, k4))
            wv = jnp.concatenate([mine_v, near_v, far_v, swap(far_v, "mp", n_mp, 1)], axis=0)
        v, u, s, rows, tot, sblk, sdev, tdev = value_stage(
            nx, wv, taps_v, bias, k4, tri, tokens
        )
        tot_hi = lax.reduce_precision(tdev, 8, 7)
        tot_mid = lax.reduce_precision(tdev - tot_hi, 8, 7)
        tot_low = tdev - tot_hi - tot_mid
        message = jnp.concatenate(
            [sdev, tot_hi.astype(bf16), tot_mid.astype(bf16), tot_low.astype(bf16)], axis=0
        )
        def twist(k, q):
            return q ^ k if direct else q

        o_intra = intra_stage(v, rows, scores)
        if direct:
            far = swap(message, "mp", n_mp, 2)
            near = swap(message, "mp", n_mp, 1)
            far, o_intra = lax.optimization_barrier((far, o_intra))
            messages = [message, near, far, swap(far, "mp", n_mp, 1)]
        else:
            messages = over_mp(message)
        far_tot = jnp.stack([x[CH:] for x in messages]).astype(f32)

        (s9,) = chain_stage(meta, sblk, tot, far_tot, messages, twist, tokens)
        hidden_out, result_t, dgate_t, do_t, dsblk, dsdev, rcc, dkc, small_mid = token_stage(
            o_intra, v, s9, k4, rows, tot, wg, wo, nx, hidden_in, out_grad, cols
        )
        if direct:
            far_d = swap(dsdev, "mp", n_mp, 2)
            near_d = swap(dsdev, "mp", n_mp, 1)
        grad_go, dn_gate = early_grad_stage(dgate_t, result_t, nx, out_grad, wg)
        grad_go = grad_go.reshape(n_mp, per * 2 * PS, D)
        if direct:
            far_d, grad_go = lax.optimization_barrier((far_d, grad_go))
            got = swap(jnp.stack([grad_go[1], grad_go[3]]), "mp", n_mp, 1)
            away = (grad_go[2].astype(f32) + got[1].astype(f32)).astype(bf16)
            far_go = swap(away, "mp", n_mp, 2)
            do_back, away = lax.optimization_barrier((do_t, away))
        else:
            do_back = do_t
        dvi, rci, dki = intra_back_stage(v, do_back, rows, scores, k4, dkc)
        to_prev = lax.ppermute(dki[NS : 2 * NS, :1].reshape(1, NS), "mp", prevs)
        to_next = lax.ppermute(dki[3 * NS :, tokens - 1 :].reshape(1, NS), "mp", nexts)
        if direct:
            messages = [dsdev, near_d, far_d, swap(far_d, "mp", n_mp, 1)]
        else:
            messages = over_mp(dsdev)
        natural = jnp.arange(n_dp, dtype=jnp.int32)
        ds9, x9 = chain_stage(meta, dsblk, tot, far_tot, messages, twist, tokens, s9)
        if direct:
            far_go, ds9, dvi = lax.optimization_barrier((far_go, ds9, dvi))
            mine_go = grad_go[0].astype(f32) + got[0].astype(f32) + far_go.astype(f32)
            mine_go = mine_go.astype(bf16)
        else:
            mine_go = lax.psum_scatter(grad_go, "mp", scatter_dimension=0, tiled=True)[0]
        if direct:
            bits = jnp.arange(n_dp, dtype=jnp.int32)
            bits = (bits >> 2) + 4 * ((bits >> 1) & 1) + 2 * (bits & 1)
            keep_go, send_go = deal(
                mine_go.reshape(per, 2 * PS, D),
                *deal_targets(owners, jnp.bitwise_xor(bits, dp_index)),
                joined=n_dp // 2,
            )
            keep_go, ds9 = lax.optimization_barrier((keep_go, ds9))
            keep_go = keep_go.astype(f32) + swap(send_go, "dp", n_dp, 1).astype(f32)
        else:
            (dealt,) = deal(
                mine_go.reshape(per, 2 * PS, D), *deal_targets(owners, natural), joined=n_dp
            )
            own_go = lax.psum_scatter(dealt, "dp", scatter_dimension=0, tiled=True)[0]
        dpre, dx, dk = cross_back_stage(
            dvi, v, do_t, u, ds9, k4, rows, rci, rcc, x9, dki, cols, after
        )
        d_last, d_first = to_prev, to_next
        d_last = jnp.where(ends, 0.0, d_last)
        d_first = jnp.where(starts, 0.0, d_first)
        edge = jnp.transpose(jnp.concatenate([d_last, d_first, jnp.zeros((6, NS), f32)], axis=0))
        if direct:
            keep_go, dpre, dk, edge = lax.optimization_barrier((keep_go, dpre, dk, edge))
            far_go = swap(keep_go[2:].astype(bf16), "dp", n_dp, 4)
        grad_v, dn_value, tap_v = value_back_stage(dpre, taps_v, s, dx, nx, wv)
        if direct:
            far_go, grad_v = lax.optimization_barrier((far_go, grad_v))
            keep_go = keep_go[:2] + far_go.astype(f32)
            last_go = swap(keep_go[1].astype(bf16), "dp", n_dp, 2)
            both = grad_v.reshape(n_mp, per * WV, D)
            got_v = swap(jnp.stack([both[1], both[3]]), "mp", n_mp, 1)
            away_v = (both[2].astype(f32) + got_v[1].astype(f32)).astype(bf16)
            away_v, dk = lax.optimization_barrier((away_v, dk))
            far_v = swap(away_v, "mp", n_mp, 2)
        dpre_k = key_pre_stage(dk, key_u, edge)
        grad_key, dn_key, tap_key = key_back_stage(meta, dpre_k, taps_k, key_proj, nx, key_low)
        if direct:
            far_v, last_go, grad_key, dn_key, tap_key = lax.optimization_barrier(
                (far_v, last_go, grad_key, dn_key, tap_key)
            )
            own_go = keep_go[0] + last_go.astype(f32)

        head_grad = jnp.concatenate(
            [
                small_mid[0, 0].reshape(H, 1, PS),
                jnp.transpose(
                    tap_v.reshape(NG, 8, GH, PS)[:, :K], (0, 2, 1, 3)
                ).reshape(H, K, PS),
                small_mid[1, 0].reshape(H, 1, PS),
                jnp.pad(jnp.transpose(jnp.sum(dx, axis=2)), ((0, 0), (0, PS - 2))).reshape(
                    H, 1, PS
                ),
            ],
            axis=1,
        )
        if direct:
            head_grad = jnp.take(head_grad.reshape(n_mp, per, 10, PS), order, axis=0)
        small_grad = jnp.concatenate(
            [head_grad.reshape(-1), tap_key[:K].reshape(-1)]
        )
        count = small_grad.shape[0]

        if direct:
            rows_key = (4 * NS) // (n_mp * n_dp)
            small_rows = jnp.pad(small_grad, (0, n_mp * n_dp * D - count)).reshape(n_mp, n_dp, D)
            small_rows = jnp.take(small_rows, order, axis=0).astype(bf16)
            extra = scatter_mp(jnp.concatenate([grad_key, small_rows], axis=1))
            mine_v = both[0].astype(f32) + got_v[0].astype(f32) + far_v.astype(f32)
            targets = jnp.bitwise_xor(natural, dp_index)
            dealt = deal(
                mine_v.astype(bf16).reshape(per, WV, D),
                *deal_targets(owners, targets),
                targets,
                extra[: n_dp * rows_key],
                extra[n_dp * rows_key :],
            )
            own_v = dealt[0].astype(f32)
            for k in range(1, n_dp):
                own_v = own_v + swap(dealt[k], "dp", n_dp, k).astype(f32)
        else:
            mine_v = lax.psum_scatter(
                grad_v.reshape(n_mp, per * WV, D), "mp", scatter_dimension=0, tiled=True
            )[0]
            (dealt,) = deal(
                mine_v.reshape(per, WV, D), *deal_targets(owners, natural), joined=n_dp
            )
            own_v = lax.psum_scatter(dealt, "dp", scatter_dimension=0, tiled=True)[0].astype(f32)

        right_halo = slice(tokens, tokens + HALO)
        halo_l = lax.ppermute(dn_key[right_halo] + dn_value[right_halo], "mp", nexts)
        halo_r = lax.ppermute(dn_key[-HALO:] + dn_value[-HALO:], "mp", prevs)
        halo_l = jnp.where(starts, 0.0, halo_l)
        halo_r = jnp.where(ends, 0.0, halo_r)
        edges = jnp.concatenate([halo_l, jnp.zeros((tokens - 2 * HALO, D), f32), halo_r], axis=0)
        dnormed = dn_gate + dn_key[:tokens] + dn_value[:tokens] + edges
        scaled = dnormed * gain_in
        gain_grad = jnp.sum(dnormed * hidden * scale_in, axis=0)
        cross_in = jnp.sum(scaled * hidden, axis=1, keepdims=True)
        hidden_grad = (
            out_grad.astype(f32) + scale_in * scaled - hidden * scale_in**3 * cross_in / D
        )

        own_v = lax.optimization_barrier(own_v)
        own_go = own_go.astype(f32)
        own_grad = jnp.concatenate([own_go[:PS], own_v[: PS + 2], own_go[PS:]], axis=0)
        own_grad = lax.optimization_barrier(own_grad.reshape(3 * PS + 2, 1, D))
        previous = [
            jnp.transpose(x[0], (2, 0, 1))
            for x in (block_master, block_first, block_second, block_ema)
        ]
        slot_new = adamw_update(
            previous[0], own_grad, previous[1], previous[2], previous[3], MATRIX_RATE
        )
        is_owner = jnp.any(owners == dp_index)
        slot_new = [
            jnp.where(is_owner, renewed, before) for renewed, before in zip(slot_new, previous)
        ]
        if direct:
            share = jnp.concatenate(
                [jnp.broadcast_to(gain_grad, (15 - rows_key, D)), own_v[WV - rows_key - 1 :]],
                axis=0,
            ).astype(bf16)
            shares, code = gather_all(share, mp_index, dp_index)
            shares, slot_new = lax.optimization_barrier((shares, slot_new))
            *key_new, small_total, gain_total = finish_stage(
                code, shares, bc_weight, bc_first, bc_second, bc_ema
            )
            small_total = small_total.reshape(-1)[:count]
            gain_total = gain_total[0]
        else:
            key_total, small_total, gain_total = lax.psum(
                (grad_key.reshape(4 * NS, D).astype(f32), small_grad, gain_grad), ("dp", "mp")
            )
            key_new = adamw_update(
                bc_weight, jnp.transpose(key_total), bc_first, bc_second, bc_ema, MATRIX_RATE
            )
        slot_outs = [jnp.transpose(x, (1, 2, 0))[None] for x in slot_new]
        head_total = lax.dynamic_slice_in_dim(
            small_total[: H * 10 * PS].reshape(H, 10, PS), mp_index * per, per
        )
        head_new = adamw_update(
            head_small, head_total, head_first, head_second, head_ema, SMALL_RATE
        )
        shared_total = jnp.concatenate(
            [
                small_total[H * 10 * PS :].reshape(K, 4 * NS),
                gain_total.reshape(-1, 4 * NS),
            ],
            axis=0,
        )
        shared_new = adamw_update(
            shared_small, shared_total, shared_first, shared_second, shared_ema, SMALL_RATE
        )
        return (hidden_out, hidden_grad, *slot_outs, *head_new, *key_new, *shared_new)

    return local


def solution(mesh):
    rows = P(("dp", "mp"), None)
    slot = P("mp", "dp", None, None)
    head = P("mp", None, None)
    return jax.shard_map(
        make_local(mesh.shape["dp"], mesh.shape["mp"]),
        mesh=mesh,
        in_specs=(rows, rows, P("dp"), P()) + (slot,) * 4 + (head,) * 4 + (P(),) * 8,
        out_specs=(rows, rows) + (slot,) * 4 + (head,) * 4 + (P(),) * 8,
        check_vma=False,
    )
```

```python
import jax
import jax.numpy as jnp
from jax import lax
from jax.experimental import pallas as pl
from jax.experimental.pallas import tpu as pltpu
from jax.sharding import PartitionSpec as P

D = 768
H = 24
PS = 64
NS = 64
K = 7
STEP = 3
CH = H * PS
BL = 128
GH = 8
NG = H // GH
WV = 80
PAD = 128
HALO = 8
NORM_EPS = 1e-05
BETA_ONE = 0.5
BETA_TWO = 0.5
ADAM_EPS = 1e-08
WEIGHT_DECAY = 0.1
MATRIX_RATE = 0.04
SMALL_RATE = 0.2
AVERAGE_KEEP = 0.75

f32 = jnp.float32
bf16 = jnp.bfloat16
LQ, RQ, KF, KR, WF, WR, EF, ER, XF, XR, RF, RR = range(12)
KINDS = 12


def params(mb=56):
    return pltpu.CompilerParams(
        dimension_semantics=("arbitrary",), vmem_limit_bytes=mb * 1024 * 1024
    )


def cost(micros):
    return pl.CostEstimate(flops=0, transcendentals=0, bytes_accessed=micros * 1_000_000)


def nt(a, b, precision=None):
    return lax.dot_general(
        a, b, (((1,), (1,)), ((), ())), preferred_element_type=f32, precision=precision
    )


def nn(a, b, precision=None):
    return lax.dot_general(
        a, b, (((1,), (0,)), ((), ())), preferred_element_type=f32, precision=precision
    )


def tn(a, b):
    return lax.dot_general(a, b, (((0,), (0,)), ((), ())), preferred_element_type=f32)


def lane_sums(x):
    ones = jnp.ones((8, x.shape[1]), bf16)
    high = x.astype(bf16)
    rest = (x - high.astype(f32)).astype(bf16)
    return nt(ones, high) + nt(ones, rest)


def sigmoid(v):
    return 1.0 / (1.0 + jnp.exp(-v))


def lane_first(shape):
    return lax.broadcasted_iota(jnp.int32, shape, len(shape) - 1) < NS


def conv_taps(signal, taps, sign):
    ext = signal.shape[1]
    total = None
    for k in range(K):
        shift = (sign * (k - K // 2)) % ext
        moved = signal if shift == 0 else pltpu.roll(signal, shift, axis=1)
        term = moved.astype(f32) * taps[:, k : k + 1]
        total = term if total is None else total + term
    return total


def causal_masks():
    row = lax.broadcasted_iota(jnp.int32, (BL, BL), 0)
    col = lax.broadcasted_iota(jnp.int32, (BL, BL), 1)
    return row < col, row > col


def stacked_keys(a, b):
    zero = jnp.zeros_like(a)
    return jnp.concatenate(
        [jnp.concatenate([a, zero], axis=1), jnp.concatenate([zero, b], axis=1)], axis=0
    )


def key_kernel(nx_ref, w_ref, taps_ref, p_ref, u_ref, k_ref, st_ref):
    tokens = k_ref.shape[1]
    proj = nt(w_ref[...], nx_ref[...])
    pre = conv_taps(proj, taps_ref[...], -1)
    key = pre * sigmoid(pre)
    ext = key.shape[1]
    b_f = key[:NS, :tokens].astype(bf16)
    c_f = pltpu.roll(key[NS : 2 * NS], 1, axis=1)[:, :tokens].astype(bf16)
    b_r = key[2 * NS : 3 * NS, :tokens].astype(bf16)
    c_r = pltpu.roll(key[3 * NS :], ext - 1, axis=1)[:, :tokens].astype(bf16)
    p_ref[...] = proj
    u_ref[...] = pre
    k_ref[...] = jnp.concatenate([b_f, c_f, b_r, c_r], axis=0)
    lower, upper = causal_masks()
    for blk in range(tokens // BL):
        part = slice(blk * BL, (blk + 1) * BL)
        s_f = tn(b_f[:, part], c_f[:, part])
        s_r = tn(b_r[:, part], c_r[:, part])
        st_ref[blk] = jnp.where(lower, s_f, jnp.where(upper, s_r, 0.0))


def key_stage(nx, key_low, taps, tokens):
    ext = nx.shape[0]
    blocks = tokens // BL
    return pl.pallas_call(
        key_kernel,
        out_shape=(
            jax.ShapeDtypeStruct((4 * NS, ext), f32),
            jax.ShapeDtypeStruct((4 * NS, ext), f32),
            jax.ShapeDtypeStruct((4 * NS, tokens), bf16),
            jax.ShapeDtypeStruct((blocks, BL, BL), f32),
        ),
        compiler_params=pltpu.CompilerParams(vmem_limit_bytes=16 * 1024 * 1024),
        cost_estimate=cost(6),
        name="key_stage",
    )(nx, key_low, taps)


def value_kernel(
    nx_ref, wv_ref, taps_ref, bias_ref, k4_ref, tri_ref,
    v_ref, u_ref, s_ref, rows_ref, tot_ref, sblk_ref, sdev_ref, tdev_ref,
    p_scr, lhs_scr,
):
    tokens = v_ref.shape[1]
    blocks = tokens // BL
    p_scr[...] = nt(wv_ref[...].reshape(GH * WV, D), nx_ref[...])
    for h in range(GH):
        for c in range(PS // 16):
            src = h * WV + c * 16
            dst = h * PS + c * 16
            signal = p_scr[src : src + 16, :].astype(bf16)
            pre = conv_taps(signal, taps_ref[dst : dst + 16, :], -1)[:, :tokens]
            s_ref[dst : dst + 16, :] = signal
            u_ref[dst : dst + 16, :] = pre.astype(bf16)
            v_ref[dst : dst + 16, :] = (pre * sigmoid(pre)).astype(bf16)
    x_f = jnp.concatenate(
        [p_scr[h * WV + PS : h * WV + PS + 1, :tokens] for h in range(GH)], axis=0
    )
    x_r = jnp.concatenate(
        [p_scr[h * WV + PS + 1 : h * WV + PS + 2, :tokens] for h in range(GH)], axis=0
    )
    x_f = x_f + bias_ref[:, 0:1]
    x_r = x_r + bias_ref[:, 1:2]
    rate_f = jnp.maximum(x_f, 0.0) + jnp.log1p(jnp.exp(-jnp.abs(x_f)))
    rate_r = jnp.maximum(x_r, 0.0) + jnp.log1p(jnp.exp(-jnp.abs(x_r)))
    rows_ref[XF] = x_f
    rows_ref[XR] = x_r
    rows_ref[RF] = rate_f
    rows_ref[RR] = rate_r
    cuts = [slice(b * BL, (b + 1) * BL) for b in range(blocks)]
    stack = jnp.concatenate([rate_f[:, c] for c in cuts] + [rate_r[:, c] for c in cuts], axis=0)
    sums = -nn(stack, tri_ref[...], lax.Precision.HIGHEST)
    first = lane_first((GH, BL))
    cum_r = jnp.zeros((GH, BL), f32)
    cum_f = jnp.zeros((GH, BL), f32)
    state = jnp.zeros((GH * PS, BL), f32)
    for b in range(blocks):
        l_f = sums[b * GH : (b + 1) * GH]
        l_r = sums[(blocks + b) * GH : (blocks + b + 1) * GH]
        r_f = rate_f[:, cuts[b]]
        r_r = rate_r[:, cuts[b]]
        end_f = jnp.broadcast_to(l_f[:, BL - 1 : BL], (GH, BL))
        end_r = jnp.broadcast_to(l_r[:, BL - 1 : BL], (GH, BL))
        w_f = jnp.exp(end_f - l_f) * r_f
        w_r = jnp.exp(l_r + r_r) * r_r
        rows_ref[LQ, :, cuts[b]] = l_f + r_f
        rows_ref[RQ, :, cuts[b]] = -l_r
        rows_ref[KF, :, cuts[b]] = l_f - jnp.log(r_f)
        rows_ref[KR, :, cuts[b]] = -(l_r + r_r + jnp.log(r_r))
        rows_ref[WF, :, cuts[b]] = w_f
        rows_ref[WR, :, cuts[b]] = w_r
        rows_ref[EF, :, cuts[b]] = jnp.exp(l_f + r_f)
        rows_ref[ER, :, cuts[b]] = jnp.exp(end_r - l_r)
        tot_ref[b] = jnp.where(first, end_f, end_r)
        for h in range(GH):
            span = slice(h * PS, (h + 1) * PS)
            vals = v_ref[span, cuts[b]].astype(f32)
            lhs_scr[span, :BL] = (vals * w_f[h : h + 1]).astype(bf16)
            lhs_scr[span, BL:] = (vals * w_r[h : h + 1]).astype(bf16)
        keys = stacked_keys(k4_ref[:NS, cuts[b]], k4_ref[2 * NS : 3 * NS, cuts[b]])
        local_state = nt(lhs_scr[...], keys)
        sblk_ref[b] = local_state.astype(bf16)
        keep = jnp.where(first, jnp.exp(end_f), 1.0)
        gain = jnp.where(first, 1.0, jnp.exp(cum_r))
        state = jnp.concatenate(
            [
                state[h * PS : (h + 1) * PS] * keep[h : h + 1]
                + local_state[h * PS : (h + 1) * PS] * gain[h : h + 1]
                for h in range(GH)
            ],
            axis=0,
        )
        cum_f = cum_f + end_f
        cum_r = cum_r + end_r
    sdev_ref[...] = state.astype(bf16)
    tdev_ref[...] = jnp.where(first, cum_f, cum_r)


def value_stage(nx, wv, taps, bias, k4, tri, tokens):
    ext = nx.shape[0]
    blocks = tokens // BL
    rows = GH * PS
    return pl.pallas_call(
        value_kernel,
        grid=(NG,),
        in_specs=[
            pl.BlockSpec((ext, D), lambda g: (0, 0), pipeline_mode=pl.Buffered(1)),
            pl.BlockSpec((GH, WV, D), lambda g: (g, 0, 0)),
            pl.BlockSpec((rows, 8), lambda g: (g, 0)),
            pl.BlockSpec((GH, 2), lambda g: (g, 0)),
            pl.BlockSpec((4 * NS, tokens), lambda g: (0, 0)),
            pl.BlockSpec((BL, BL), lambda g: (0, 0)),
        ],
        out_specs=[
            pl.BlockSpec((rows, tokens), lambda g: (g, 0)),
            pl.BlockSpec((rows, tokens), lambda g: (g, 0)),
            pl.BlockSpec((rows, ext), lambda g: (g, 0)),
            pl.BlockSpec((KINDS, GH, tokens), lambda g: (0, g, 0)),
            pl.BlockSpec((blocks, GH, BL), lambda g: (0, g, 0)),
            pl.BlockSpec((blocks, rows, BL), lambda g: (0, g, 0)),
            pl.BlockSpec((rows, BL), lambda g: (g, 0)),
            pl.BlockSpec((GH, BL), lambda g: (g, 0)),
        ],
        out_shape=(
            jax.ShapeDtypeStruct((CH, tokens), bf16),
            jax.ShapeDtypeStruct((CH, tokens), bf16),
            jax.ShapeDtypeStruct((CH, ext), bf16),
            jax.ShapeDtypeStruct((KINDS, H, tokens), f32),
            jax.ShapeDtypeStruct((blocks, H, BL), f32),
            jax.ShapeDtypeStruct((blocks, CH, BL), bf16),
            jax.ShapeDtypeStruct((CH, BL), bf16),
            jax.ShapeDtypeStruct((H, BL), f32),
        ),
        scratch_shapes=[pltpu.VMEM((GH * WV, ext), f32), pltpu.VMEM((rows, 2 * BL), bf16)],
        compiler_params=params(),
        cost_estimate=cost(27),
        name="value_stage",
    )(nx, wv, taps, bias, k4, tri)


def chain_kernel(flip, copies, tokens, twist, meta_ref, sblk_ref, tot_ref, far_ref, *refs):
    states = refs[:copies]
    if flip:
        other_ref, out_ref, dot_ref = refs[copies:]
    else:
        (out_ref,) = refs[copies:]
    blocks = sblk_ref.shape[0]
    per = sblk_ref.shape[1] // PS
    step = pl.program_id(0)
    first = lane_first((1, BL))
    wide = lane_first((PS, BL))
    up_lanes = jnp.logical_not(wide) if flip else wide
    here = meta_ref[0]
    length = meta_ref[1]
    sequence = here * tokens // length
    places = [meta_ref[2 + k] for k in range(copies)]
    same = [(place * tokens // length) == sequence for place in places]
    for i in range(per):
        span = slice(i * PS, (i + 1) * PS)
        head = step * per + i
        totals = []
        for k in range(copies):
            place = twist(k, step) * per + i
            parts = [far_ref[k, pl.ds(part * H + place, 1), :] for part in range(3)]
            totals.append(parts[0] + parts[1] + parts[2])
        entering = jnp.zeros((PS, BL), f32)
        for k in range(copies):
            left = jnp.zeros((1, BL), f32)
            right = jnp.zeros((1, BL), f32)
            for q in range(copies):
                if q != k:
                    between = (places[q] > places[k]) & (places[q] < here)
                    left = left + totals[q] * between.astype(f32)
                    between = (places[q] < places[k]) & (places[q] > here)
                    right = right + totals[q] * between.astype(f32)
            from_left = jnp.exp(left) * (same[k] & (places[k] < here)).astype(f32)
            from_right = jnp.exp(right) * (same[k] & (places[k] > here)).astype(f32)
            if flip:
                weight = jnp.where(first, from_right, from_left)
            else:
                weight = jnp.where(first, from_left, from_right)
            entering = entering + weight * states[k][span, :].astype(f32)
        decay = [jnp.exp(tot_ref[b, pl.ds(head, 1), :]) for b in range(blocks)]
        locals_ = [sblk_ref[b, span, :].astype(f32) for b in range(blocks)]
        up = [entering]
        down = [entering]
        for b in range(blocks):
            up.append(up[-1] * decay[b] + locals_[b])
            rev = blocks - 1 - b
            down.append(down[-1] * decay[rev] + locals_[rev])
        down = down[::-1]
        for b in range(blocks):
            both = jnp.where(up_lanes, up[b], down[b + 1])
            out_ref[b, span, :] = both.astype(bf16)
            if flip:
                before = other_ref[b - 1 if b > 0 else blocks, span, :]
                beyond = other_ref[b + 1, span, :]
                far = jnp.where(wide, beyond.astype(f32), before.astype(f32))
                dot_ref[b, pl.ds(head, 1), :] = jnp.sum(both * far, axis=0, keepdims=True)
        if not flip:
            out_ref[blocks, span, :] = jnp.where(up_lanes, up[blocks], down[0]).astype(bf16)


def chain_stage(meta, sblk, tot, far_tot, states, twist, tokens, other=None):
    blocks = sblk.shape[0]
    copies = len(states)
    rows = CH // copies
    flip = other is not None
    in_specs = [
        pl.BlockSpec((blocks, rows, BL), lambda q, meta: (0, q, 0)),
        pl.BlockSpec((blocks, H, BL), lambda q, meta: (0, 0, 0)),
        pl.BlockSpec((copies, 3 * H, BL), lambda q, meta: (0, 0, 0)),
    ]
    for k in range(copies):
        in_specs.append(pl.BlockSpec((rows, BL), lambda q, meta, k=k: (twist(k, q), 0)))
    held = blocks if flip else blocks + 1
    out_specs = [pl.BlockSpec((held, rows, BL), lambda q, meta: (0, q, 0))]
    out_shape = [jax.ShapeDtypeStruct((held, CH, BL), bf16)]
    args = [meta, sblk, tot, far_tot, *states]
    if flip:
        in_specs.append(pl.BlockSpec((blocks + 1, rows, BL), lambda q, meta: (0, q, 0)))
        out_specs.append(pl.BlockSpec((blocks, H, BL), lambda q, meta: (0, 0, 0)))
        out_shape.append(jax.ShapeDtypeStruct((blocks, H, BL), f32))
        args.append(other)

    def body(*refs):
        chain_kernel(flip, copies, tokens, twist, *refs)

    return pl.pallas_call(
        body,
        grid_spec=pltpu.PrefetchScalarGridSpec(
            num_scalar_prefetch=1, grid=(copies,), in_specs=in_specs, out_specs=out_specs
        ),
        out_shape=out_shape,
        compiler_params=params(),
        cost_estimate=cost(7),
        name="chain_back" if flip else "chain_stage",
    )(*args)


def pair_blocks(value):
    zero = jnp.zeros((PS, BL), value.dtype)
    return jnp.concatenate(
        [
            jnp.concatenate([value[:PS], zero], axis=1),
            jnp.concatenate([zero, value[PS:]], axis=1),
        ],
        axis=0,
    )


def intra_kernel(v_ref, rows_ref, st_ref, o_ref):
    lower, _ = causal_masks()
    kf_cols = jnp.transpose(rows_ref[KF])
    kr_cols = jnp.transpose(rows_ref[KR])
    for pair in range(H // 2):
        mats = []
        for h in (2 * pair, 2 * pair + 1):
            gap = jnp.where(
                lower,
                rows_ref[LQ, h : h + 1, :] - kf_cols[:, h : h + 1],
                rows_ref[RQ, h : h + 1, :] - kr_cols[:, h : h + 1],
            )
            decay = jnp.exp(jnp.minimum(gap, 80.0))
            mats.append((decay * st_ref[0]).astype(bf16))
        span = slice(pair * 2 * PS, (pair + 1) * 2 * PS)
        out = nn(pair_blocks(v_ref[span, :]), jnp.concatenate(mats, axis=0))
        o_ref[span, :] = out.astype(o_ref.dtype)


def intra_stage(v, rows, scores):
    tokens = v.shape[1]
    return pl.pallas_call(
        intra_kernel,
        grid=(tokens // BL,),
        in_specs=[
            pl.BlockSpec((CH, BL), lambda b: (0, b)),
            pl.BlockSpec((KINDS, H, BL), lambda b: (0, 0, b)),
            pl.BlockSpec((1, BL, BL), lambda b: (b, 0, 0)),
        ],
        out_specs=pl.BlockSpec((CH, BL), lambda b: (0, b)),
        out_shape=jax.ShapeDtypeStruct((CH, tokens), bf16),
        compiler_params=params(),
        cost_estimate=cost(12),
        name="intra_stage",
    )(v, rows, scores)


def token_kernel(
    oi_ref, v_ref, s_ref, k4_ref, rows_ref, tot_ref, wg_ref, wo_ref,
    nx_ref, hid_ref, go_ref, cols_ref,
    ho_ref, r_ref, dg_ref, do_ref, dsblk_ref, dsdev_ref, rc_ref, dk_ref, small_ref,
    cross_scr, g_scr, dres_scr, mix_scr, gated_scr, lhs_scr, gain_scr, diag_scr,
    dev_scr, cum_scr, wide_scr,
):
    step = pl.program_id(0)
    last = pl.num_programs(0) - 1
    cuts = [slice(j * BL, (j + 1) * BL) for j in range(v_ref.shape[1] // BL)]

    @pl.when(step == 0)
    def _():
        gain_scr[...] = jnp.zeros_like(gain_scr)
        diag_scr[...] = jnp.zeros_like(diag_scr)
        dev_scr[...] = jnp.zeros_like(dev_scr)
        cum_scr[...] = jnp.zeros_like(cum_scr)
        wide_scr[0] = jnp.broadcast_to(cols_ref[:, 0:1], (CH, BL))
        wide_scr[1] = jnp.broadcast_to(cols_ref[:, 1:2], (CH, BL))

    keys = [stacked_keys(k4_ref[NS : 2 * NS, cut], k4_ref[3 * NS :, cut]) for cut in cuts]
    for j, both_keys in enumerate(keys):
        cross_scr[j] = nn(s_ref[j], both_keys)
    g_scr[...] = nt(wg_ref[...], nx_ref[...])
    dres_scr[...] = nt(wo_ref[...], go_ref[...])
    squares = [jnp.zeros((8, BL), f32) for _ in cuts]
    cross = [jnp.zeros((8, BL), f32) for _ in cuts]
    for h in range(H):
        span = slice(h * PS, (h + 1) * PS)
        gain = wide_scr[0, span, :]
        for j, cut in enumerate(cuts):
            part_f = cross_scr[j, span, :BL] * rows_ref[EF, h : h + 1, cut]
            part_r = cross_scr[j, span, BL:] * rows_ref[ER, h : h + 1, cut]
            mix = (
                oi_ref[span, cut].astype(f32)
                + part_f
                + part_r
                + wide_scr[1, span, :] * v_ref[span, cut].astype(f32)
            )
            gate = g_scr[span, cut]
            gated = mix * (gate * sigmoid(gate))
            mix_scr[span, cut] = mix
            gated_scr[span, cut] = gated
            squares[j] = squares[j] + jnp.sum((gated * gated).reshape(PS // 8, 8, BL), axis=0)
            flow = dres_scr[span, cut] * gain * gated
            cross[j] = cross[j] + jnp.sum(flow.reshape(PS // 8, 8, BL), axis=0)
    scales = [
        lax.rsqrt(jnp.sum(x, axis=0, keepdims=True) / CH + NORM_EPS) for x in squares
    ]
    pulls = [
        scale * scale * scale * (jnp.sum(x, axis=0, keepdims=True) / CH)
        for scale, x in zip(scales, cross)
    ]
    for h in range(H):
        span = slice(h * PS, (h + 1) * PS)
        gain = wide_scr[0, span, :]
        diags = diag_scr[span, :]
        gains = gain_scr[span, :]
        for j, cut in enumerate(cuts):
            gated = gated_scr[span, cut]
            normal = gated * scales[j]
            dres = dres_scr[span, cut]
            r_ref[span, cut] = (normal * gain).astype(bf16)
            gains = gains + dres * normal
            dgated = scales[j] * (dres * gain) - gated * pulls[j]
            gate = g_scr[span, cut]
            soft = sigmoid(gate)
            grad_mix = dgated * (gate * soft)
            dg_ref[span, cut] = (
                dgated * mix_scr[span, cut] * (soft * (1.0 + gate * (1.0 - soft)))
            ).astype(bf16)
            diags = diags + grad_mix * v_ref[span, cut].astype(f32)
            do_ref[span, cut] = grad_mix.astype(bf16)
            grad_f = grad_mix * rows_ref[EF, h : h + 1, cut]
            grad_r = grad_mix * rows_ref[ER, h : h + 1, cut]
            rc_ref[0, h : h + 1, cut] = jnp.sum(
                grad_f * cross_scr[j, span, :BL], axis=0, keepdims=True
            )
            rc_ref[1, h : h + 1, cut] = jnp.sum(
                grad_r * cross_scr[j, span, BL:], axis=0, keepdims=True
            )
            lhs_scr[j, span, :BL] = grad_f.astype(bf16)
            lhs_scr[j, span, BL:] = grad_r.astype(bf16)
        diag_scr[span, :] = diags
        gain_scr[span, :] = gains
    out = tn(r_ref[...], wo_ref[...])
    ho_ref[...] = (hid_ref[...].astype(f32) + out).astype(bf16)
    first = lane_first((H, BL))
    for j, cut in enumerate(cuts):
        dstate = nt(lhs_scr[j], keys[j])
        dkeys = tn(s_ref[j], lhs_scr[j])
        dk_ref[:NS, cut] = dkeys[:NS, :BL]
        dk_ref[NS:, cut] = dkeys[NS:, BL:]
        dsblk_ref[j] = dstate.astype(bf16)
        total = tot_ref[j]
        keep = jnp.where(first, 1.0, jnp.exp(total))
        grow = jnp.where(first, jnp.exp(cum_scr[...]), 1.0)
        for h in range(H):
            span = slice(h * PS, (h + 1) * PS)
            dev_scr[span, :] = (
                dev_scr[span, :] * keep[h : h + 1] + dstate[span, :] * grow[h : h + 1]
            )
        cum_scr[...] += total

    @pl.when(step == last)
    def _():
        dsdev_ref[...] = dev_scr[...].astype(bf16)
        small_ref[0] = lane_sums(gain_scr[...])
        small_ref[1] = lane_sums(diag_scr[...])


def token_stage(oi, v, s9, k4, rows, tot, wg, wo, nx, hid, go, cols):
    tokens = v.shape[1]
    blocks = tokens // BL
    two = 2
    wide = two * BL
    whole = dict(pipeline_mode=pl.Buffered(1))
    chan = pl.BlockSpec((CH, wide), lambda b: (0, b))
    toks = pl.BlockSpec((wide, D), lambda b: (b, 0))
    state = pl.BlockSpec((two, CH, BL), lambda b: (b, 0, 0))
    big = pltpu.VMEM((CH, BL), f32)
    large = pltpu.VMEM((CH, wide), f32)
    return pl.pallas_call(
        token_kernel,
        grid=(blocks // two,),
        in_specs=[
            chan,
            chan,
            state,
            pl.BlockSpec((4 * NS, wide), lambda b: (0, b)),
            pl.BlockSpec((KINDS, H, wide), lambda b: (0, 0, b)),
            pl.BlockSpec((two, H, BL), lambda b: (b, 0, 0)),
            pl.BlockSpec((CH, D), lambda b: (0, 0), **whole),
            pl.BlockSpec((CH, D), lambda b: (0, 0), **whole),
            toks,
            toks,
            toks,
            pl.BlockSpec((CH, 8), lambda b: (0, 0), **whole),
        ],
        out_specs=[
            toks,
            chan,
            chan,
            chan,
            state,
            pl.BlockSpec((CH, BL), lambda b: (0, 0)),
            pl.BlockSpec((2, H, wide), lambda b: (0, 0, b)),
            pl.BlockSpec((2 * NS, wide), lambda b: (0, b)),
            pl.BlockSpec((2, 8, CH), lambda b: (0, 0, 0)),
        ],
        out_shape=(
            jax.ShapeDtypeStruct((tokens, D), bf16),
            jax.ShapeDtypeStruct((CH, tokens), bf16),
            jax.ShapeDtypeStruct((CH, tokens), bf16),
            jax.ShapeDtypeStruct((CH, tokens), bf16),
            jax.ShapeDtypeStruct((blocks, CH, BL), bf16),
            jax.ShapeDtypeStruct((CH, BL), bf16),
            jax.ShapeDtypeStruct((2, H, tokens), f32),
            jax.ShapeDtypeStruct((2 * NS, tokens), f32),
            jax.ShapeDtypeStruct((2, 8, CH), f32),
        ),
        scratch_shapes=[pltpu.VMEM((two, CH, 2 * BL), f32)]
        + [large] * 4
        + [pltpu.VMEM((two, CH, 2 * BL), bf16)]
        + [big] * 3
        + [pltpu.VMEM((H, BL), f32), pltpu.VMEM((2, CH, BL), f32)],
        compiler_params=params(),
        cost_estimate=cost(35),
        name="token_stage",
    )(oi, v, s9, k4, rows, tot, wg, wo, nx, hid, go, cols)


def early_grad_kernel(dg_ref, r_ref, nx_ref, go_ref, wg_ref, out_ref, dn_ref):
    gate = nn(dg_ref[...], nx_ref[...]).astype(bf16)
    outp = nn(r_ref[...], go_ref[...]).astype(bf16)
    out_ref[:, :PS, :] = gate.reshape(GH, PS, D)
    out_ref[:, PS:, :] = outp.reshape(GH, PS, D)
    part = tn(dg_ref[...], wg_ref[...])
    step = pl.program_id(0)

    @pl.when(step == 0)
    def _():
        dn_ref[...] = part

    @pl.when(step > 0)
    def _():
        dn_ref[...] += part


def early_grad_stage(dgate, result, nx, go, wg):
    tokens = dgate.shape[1]
    rows = GH * PS
    return pl.pallas_call(
        early_grad_kernel,
        grid=(NG,),
        in_specs=[
            pl.BlockSpec((rows, tokens), lambda g: (g, 0)),
            pl.BlockSpec((rows, tokens), lambda g: (g, 0)),
            pl.BlockSpec((tokens, D), lambda g: (0, 0)),
            pl.BlockSpec((tokens, D), lambda g: (0, 0)),
            pl.BlockSpec((rows, D), lambda g: (g, 0)),
        ],
        out_specs=[
            pl.BlockSpec((GH, 2 * PS, D), lambda g: (g, 0, 0)),
            pl.BlockSpec((tokens, D), lambda g: (0, 0)),
        ],
        out_shape=(
            jax.ShapeDtypeStruct((H, 2 * PS, D), bf16),
            jax.ShapeDtypeStruct((tokens, D), f32),
        ),
        compiler_params=params(24),
        cost_estimate=cost(12),
        name="early_grad",
    )(dgate, result, nx, go, wg)


def intra_back_kernel(
    v_ref, do_ref, rows_ref, st_ref, k4_ref, dkc_ref, dv_ref, rc_ref, dk_ref
):
    lower, upper = causal_masks()
    kf_cols = jnp.transpose(rows_ref[KF])
    kr_cols = jnp.transpose(rows_ref[KR])
    score_grad = jnp.zeros((BL, BL), f32)
    for pair in range(H // 2):
        span = slice(pair * 2 * PS, (pair + 1) * 2 * PS)
        grads = pair_blocks(do_ref[span, :])
        mat_grads = tn(v_ref[span, :], grads)
        down = []
        over = []
        for i, h in enumerate((2 * pair, 2 * pair + 1)):
            gap = jnp.where(
                lower,
                rows_ref[LQ, h : h + 1, :] - kf_cols[:, h : h + 1],
                rows_ref[RQ, h : h + 1, :] - kr_cols[:, h : h + 1],
            )
            decay = jnp.exp(jnp.minimum(gap, 80.0))
            mat = decay * st_ref[0]
            term = decay * mat_grads[:, i * BL : (i + 1) * BL]
            score_grad = score_grad + term
            flow = term * st_ref[0]
            flow_f = jnp.where(lower, flow, 0.0)
            row_f = jnp.sum(flow_f, axis=0, keepdims=True)
            row_all = jnp.sum(flow, axis=0, keepdims=True)
            rc_ref[0, h : h + 1, :] = row_f
            rc_ref[1, h : h + 1, :] = row_all - row_f
            down.append(jnp.where(lower, mat, 0.0).astype(bf16))
            over.append(jnp.where(lower, 0.0, mat).astype(bf16))
        dv_f = nt(grads, jnp.concatenate(down, axis=1))
        dv_r = nt(grads, jnp.concatenate(over, axis=1))
        vals = v_ref[span, :].astype(f32)
        for i, h in enumerate((2 * pair, 2 * pair + 1)):
            half = slice(i * PS, (i + 1) * PS)
            rc_ref[2, h : h + 1, :] = jnp.sum(vals[half] * dv_f[half], axis=0, keepdims=True)
            rc_ref[3, h : h + 1, :] = jnp.sum(vals[half] * dv_r[half], axis=0, keepdims=True)
        dv_ref[span, :] = (dv_f + dv_r).astype(dv_ref.dtype)
    grad_f = jnp.where(lower, score_grad, 0.0).astype(bf16)
    grad_r = jnp.where(upper, score_grad, 0.0).astype(bf16)
    b_f = k4_ref[:NS, :]
    c_f = k4_ref[NS : 2 * NS, :]
    b_r = k4_ref[2 * NS : 3 * NS, :]
    c_r = k4_ref[3 * NS :, :]
    dk_ref[:NS, :] = nt(c_f, grad_f)
    dk_ref[NS : 2 * NS, :] = nn(b_f, grad_f) + dkc_ref[:NS, :]
    dk_ref[2 * NS : 3 * NS, :] = nt(c_r, grad_r)
    dk_ref[3 * NS :, :] = nn(b_r, grad_r) + dkc_ref[NS:, :]


def intra_back_stage(v, do, rows, scores, k4, dkc):
    tokens = v.shape[1]
    chan = pl.BlockSpec((CH, BL), lambda b: (0, b))
    return pl.pallas_call(
        intra_back_kernel,
        grid=(tokens // BL,),
        in_specs=[
            chan,
            chan,
            pl.BlockSpec((KINDS, H, BL), lambda b: (0, 0, b)),
            pl.BlockSpec((1, BL, BL), lambda b: (b, 0, 0)),
            pl.BlockSpec((4 * NS, BL), lambda b: (0, b)),
            pl.BlockSpec((2 * NS, BL), lambda b: (0, b)),
        ],
        out_specs=[
            chan,
            pl.BlockSpec((4, H, BL), lambda b: (0, 0, b)),
            pl.BlockSpec((4 * NS, BL), lambda b: (0, b)),
        ],
        out_shape=(
            jax.ShapeDtypeStruct((CH, tokens), bf16),
            jax.ShapeDtypeStruct((4, H, tokens), f32),
            jax.ShapeDtypeStruct((4 * NS, tokens), f32),
        ),
        compiler_params=params(),
        cost_estimate=cost(18),
        name="intra_back",
    )(v, do, rows, scores, k4, dkc)


def cross_back_kernel(
    dvi_ref, v_ref, do_ref, u_ref, ds_ref, k4_ref, rows_ref, rci_ref, rcc_ref,
    x_ref, dki_ref, cols_ref, after_ref,
    dpre_ref, dx_ref, dk_ref,
    cross_scr, lhs_scr, c_scr, wide_scr,
):
    b_f = k4_ref[:NS, :]
    b_r = k4_ref[2 * NS : 3 * NS, :]

    @pl.when(pl.program_id(0) == 0)
    def _():
        wide_scr[...] = jnp.broadcast_to(cols_ref[:, 1:2], (CH, BL))

    cross_scr[...] = nn(ds_ref[0], stacked_keys(b_f, b_r))
    for h in range(H):
        span = slice(h * PS, (h + 1) * PS)
        vals = v_ref[span, :].astype(f32)
        w_f = rows_ref[WF, h : h + 1, :]
        w_r = rows_ref[WR, h : h + 1, :]
        dv_f = cross_scr[span, :BL] * w_f
        dv_r = cross_scr[span, BL:] * w_r
        c_scr[0, h : h + 1, :] = jnp.sum(vals * dv_f, axis=0, keepdims=True)
        c_scr[1, h : h + 1, :] = jnp.sum(vals * dv_r, axis=0, keepdims=True)
        lhs_scr[span, :BL] = (vals * w_f).astype(bf16)
        lhs_scr[span, BL:] = (vals * w_r).astype(bf16)
        grad = (
            dvi_ref[span, :].astype(f32)
            + dv_f
            + dv_r
            + wide_scr[span, :] * do_ref[span, :].astype(f32)
        )
        pre = u_ref[span, :].astype(f32)
        soft = sigmoid(pre)
        dpre_ref[span, :] = (grad * (soft * (1.0 + pre * (1.0 - soft)))).astype(dpre_ref.dtype)
    dkeys = tn(ds_ref[0], lhs_scr[...])
    dk_ref[...] = dki_ref[...]
    dk_ref[:NS, :] += dkeys[:NS, :BL]
    dk_ref[2 * NS : 3 * NS, :] += dkeys[NS:, BL:]
    first = lane_first((H, BL))
    through_f = jnp.sum(jnp.where(first, x_ref[0], 0.0), axis=1, keepdims=True)
    through_r = jnp.sum(jnp.where(first, 0.0, x_ref[0]), axis=1, keepdims=True)
    row_f = rci_ref[0] + rcc_ref[0]
    row_r = rci_ref[1] + rcc_ref[1]
    col_f = rci_ref[2] + c_scr[0]
    col_r = rci_ref[3] + c_scr[1]
    after = after_ref[...]
    strict = lax.Precision.HIGHEST
    sum_f = nn(row_f, after, strict) - nn(col_f, after, strict) - col_f + through_f
    sum_r = nt(row_r, after, strict) - nt(col_r, after, strict) - col_r + through_r
    for kind, (total, col, x_kind, r_kind) in enumerate(
        ((sum_f, col_f, XF, RF), (sum_r, col_r, XR, RR))
    ):
        soft = sigmoid(rows_ref[x_kind])
        rate = rows_ref[r_kind]
        live = rate > 0.0
        ratio = jnp.where(live, soft / jnp.where(live, rate, 1.0), 1.0)
        dx_ref[kind] = col * ratio - total * soft


def cross_back_stage(dvi, v, do, u, ds9, k4, rows, rci, rcc, x9, dki, cols, after):
    tokens = v.shape[1]
    chan = pl.BlockSpec((CH, BL), lambda b: (0, b))
    keys = pl.BlockSpec((4 * NS, BL), lambda b: (0, b))
    return pl.pallas_call(
        cross_back_kernel,
        grid=(tokens // BL,),
        in_specs=[
            chan,
            chan,
            chan,
            chan,
            pl.BlockSpec((1, CH, BL), lambda b: (b, 0, 0)),
            keys,
            pl.BlockSpec((KINDS, H, BL), lambda b: (0, 0, b)),
            pl.BlockSpec((4, H, BL), lambda b: (0, 0, b)),
            pl.BlockSpec((2, H, BL), lambda b: (0, 0, b)),
            pl.BlockSpec((1, H, BL), lambda b: (b, 0, 0)),
            keys,
            pl.BlockSpec((CH, 8), lambda b: (0, 0)),
            pl.BlockSpec((BL, BL), lambda b: (0, 0)),
        ],
        out_specs=[chan, pl.BlockSpec((2, H, BL), lambda b: (0, 0, b)), keys],
        out_shape=(
            jax.ShapeDtypeStruct((CH, tokens), bf16),
            jax.ShapeDtypeStruct((2, H, tokens), f32),
            jax.ShapeDtypeStruct((4 * NS, tokens), f32),
        ),
        scratch_shapes=[
            pltpu.VMEM((CH, 2 * BL), f32),
            pltpu.VMEM((CH, 2 * BL), bf16),
            pltpu.VMEM((2, H, BL), f32),
            pltpu.VMEM((CH, BL), f32),
        ],
        compiler_params=params(),
        cost_estimate=cost(16),
        name="cross_back",
    )(dvi, v, do, u, ds9, k4, rows, rci, rcc, x9, dki, cols, after)


def key_pre_kernel(dk_ref, u_ref, out_ref):
    ext = u_ref.shape[1]
    tail = jnp.zeros((4 * NS, ext - dk_ref.shape[1]), f32)
    wide = jnp.concatenate([dk_ref[...], tail], axis=1)
    d_cf = pltpu.roll(wide[NS : 2 * NS], ext - 1, axis=1)
    d_cr = pltpu.roll(wide[3 * NS :], 1, axis=1)
    grad = jnp.concatenate([wide[:NS], d_cf, wide[2 * NS : 3 * NS], d_cr], axis=0)
    pre = u_ref[...]
    soft = sigmoid(pre)
    out_ref[...] = grad * (soft * (1.0 + pre * (1.0 - soft)))


def key_pre_stage(dk, u):
    return pl.pallas_call(
        key_pre_kernel,
        out_shape=jax.ShapeDtypeStruct(u.shape, f32),
        compiler_params=pltpu.CompilerParams(vmem_limit_bytes=16 * 1024 * 1024),
        cost_estimate=cost(3),
        name="key_pre",
    )(dk, u)


def conv_back_rows(dpre, taps, signal):
    rows, tokens = dpre.shape
    ext = signal.shape[1]
    wide = dpre
    if tokens < ext:
        wide = jnp.concatenate([dpre, jnp.zeros((rows, ext - tokens), dpre.dtype)], axis=1)
    total = None
    sums = []
    for k in range(K):
        shift = (k - K // 2) % ext
        moved = wide if shift == 0 else pltpu.roll(wide, shift, axis=1)
        moved = moved.astype(f32)
        term = moved * taps[:, k : k + 1]
        total = term if total is None else total + term
        prod = moved * signal
        part = prod[:, :BL]
        for b in range(1, ext // BL):
            part = part + prod[:, b * BL : (b + 1) * BL]
        sums.append(part)
    return total, sums


def key_back_kernel(
    meta_ref, dpre_ref, taps_ref, p_ref, nx_ref, w_ref, g_ref, dn_ref, t_ref, low_scr, g_scr, t_scr
):
    for c in range(4 * NS // 16):
        span = slice(c * 16, (c + 1) * 16)
        total, sums = conv_back_rows(dpre_ref[span, :], taps_ref[span, :], p_ref[span, :])
        low_scr[span, :] = total.astype(bf16)
        for k in range(K):
            t_scr[k, span, :] = sums[k]
    for k in range(K):
        t_ref[k : k + 1, :] = lane_sums(t_scr[k])[:1]
    t_ref[K : K + 1, :] = jnp.zeros((1, 4 * NS), f32)
    g_scr[...] = nn(low_scr[...], nx_ref[...])
    count, rows, _ = g_ref.shape
    for q in range(count):
        start = pl.multiple_of(meta_ref[2 + q] * rows, 8)
        g_ref[q] = g_scr[pl.ds(start, rows), :].astype(g_ref.dtype)
    dn_ref[...] = tn(low_scr[...], w_ref[...])


def key_back_stage(meta, dpre, taps, proj, nx, key_low):
    ext = nx.shape[0]
    count = meta.shape[0] - 2
    args = (dpre, taps, proj, nx, key_low)
    outs = (
        jax.ShapeDtypeStruct((count, 4 * NS // count, D), bf16),
        jax.ShapeDtypeStruct((ext, D), f32),
        jax.ShapeDtypeStruct((8, 4 * NS), f32),
    )

    def whole(shape):
        return pl.BlockSpec(shape, lambda i, meta: (0,) * len(shape))

    return pl.pallas_call(
        key_back_kernel,
        grid_spec=pltpu.PrefetchScalarGridSpec(
            num_scalar_prefetch=1,
            grid=(1,),
            in_specs=[whole(x.shape) for x in args],
            out_specs=[whole(x.shape) for x in outs],
            scratch_shapes=[
                pltpu.VMEM((4 * NS, ext), bf16),
                pltpu.VMEM((4 * NS, D), f32),
                pltpu.VMEM((K, 4 * NS, BL), f32),
            ],
        ),
        out_shape=outs,
        compiler_params=params(16),
        cost_estimate=cost(8),
        name="key_back",
    )(meta, *args)


def value_back_kernel(
    dpre_ref, taps_ref, s_ref, dx_ref, nx_ref, wv_ref, g_ref, dn_ref, t_ref, low_scr, tap_scr
):
    tokens = dpre_ref.shape[1]
    ext = s_ref.shape[1]
    step = pl.program_id(0)
    for h in range(GH):
        for c in range(PS // 16):
            src = h * PS + c * 16
            span = slice(src, src + 16)
            total, sums = conv_back_rows(
                dpre_ref[span, :], taps_ref[span, :], s_ref[span, :].astype(f32)
            )
            low_scr[h * WV + c * 16 : h * WV + (c + 1) * 16, :] = total.astype(bf16)
            for k in range(K):
                tap_scr[k, span, :] = sums[k]
        tail = jnp.concatenate(
            [
                dx_ref[0, h : h + 1, :],
                dx_ref[1, h : h + 1, :],
                jnp.zeros((14, tokens), f32),
            ],
            axis=0,
        )
        low_scr[h * WV + PS : (h + 1) * WV, :tokens] = tail.astype(bf16)
        low_scr[h * WV + PS : (h + 1) * WV, tokens:] = jnp.zeros((16, ext - tokens), bf16)
    for k in range(K):
        t_ref[0, k : k + 1, :] = lane_sums(tap_scr[k])[:1]
    t_ref[0, K : K + 1, :] = jnp.zeros((1, GH * PS), f32)
    g_ref[...] = nn(low_scr[...], nx_ref[...]).reshape(GH, WV, D).astype(g_ref.dtype)
    part = tn(low_scr[...], wv_ref[...].reshape(GH * WV, D))

    @pl.when(step == 0)
    def _():
        dn_ref[...] = part

    @pl.when(step > 0)
    def _():
        dn_ref[...] += part


def value_back_stage(dpre, taps, s, dx, nx, wv):
    tokens = dpre.shape[1]
    ext = nx.shape[0]
    rows = GH * PS
    return pl.pallas_call(
        value_back_kernel,
        grid=(NG,),
        in_specs=[
            pl.BlockSpec((rows, tokens), lambda g: (g, 0)),
            pl.BlockSpec((rows, 8), lambda g: (g, 0)),
            pl.BlockSpec((rows, ext), lambda g: (g, 0)),
            pl.BlockSpec((2, GH, tokens), lambda g: (0, g, 0)),
            pl.BlockSpec((ext, D), lambda g: (0, 0), pipeline_mode=pl.Buffered(1)),
            pl.BlockSpec((GH, WV, D), lambda g: (g, 0, 0)),
        ],
        out_specs=[
            pl.BlockSpec((GH, WV, D), lambda g: (g, 0, 0)),
            pl.BlockSpec((ext, D), lambda g: (0, 0)),
            pl.BlockSpec((1, 8, rows), lambda g: (g, 0, 0)),
        ],
        out_shape=(
            jax.ShapeDtypeStruct((H, WV, D), bf16),
            jax.ShapeDtypeStruct((ext, D), f32),
            jax.ShapeDtypeStruct((NG, 8, rows), f32),
        ),
        scratch_shapes=[
            pltpu.VMEM((GH * WV, ext), bf16),
            pltpu.VMEM((K, rows, BL), f32),
        ],
        compiler_params=params(),
        cost_estimate=cost(27),
        name="value_back",
    )(dpre, taps, s, dx, nx, wv)


def pick(sources, index):
    count = index.shape[0]
    rows, width = sources[0].shape[1:]

    def body(index_ref, *refs):
        out_ref = refs[-1]
        for i in range(count):
            first = 0
            for ref in refs[:-1]:
                n = ref.shape[0]
                local = index_ref[i] - first

                @pl.when((local >= 0) & (local < n))
                def _(ref=ref, local=local, i=i):
                    out_ref[i] = ref[local]

                first += n

    return pl.pallas_call(
        body,
        grid_spec=pltpu.PrefetchScalarGridSpec(
            num_scalar_prefetch=1,
            grid=(1,),
            in_specs=[pl.BlockSpec(x.shape, lambda i, index: (0, 0, 0)) for x in sources],
            out_specs=pl.BlockSpec((count, rows, width), lambda i, index: (0, 0, 0)),
        ),
        out_shape=jax.ShapeDtypeStruct((count, rows, width), sources[0].dtype),
        compiler_params=params(16),
        cost_estimate=cost(3),
        name="pick",
    )(index, *sources)


def pick_two_kernel(index_ref, slots_ref, gate_ref, out_ref):
    for h in range(H):
        gate_ref[h] = slots_ref[index_ref[h], :PS, :]
        out_ref[h] = slots_ref[index_ref[h], PS:, :]


def pick_two(slots, index):
    half = jax.ShapeDtypeStruct((H, PS, D), slots.dtype)
    return pl.pallas_call(
        pick_two_kernel,
        grid_spec=pltpu.PrefetchScalarGridSpec(
            num_scalar_prefetch=1,
            grid=(1,),
            in_specs=[pl.BlockSpec(slots.shape, lambda i, index: (0, 0, 0))],
            out_specs=[pl.BlockSpec((H, PS, D), lambda i, index: (0, 0, 0))] * 2,
        ),
        out_shape=(half, half),
        compiler_params=params(),
        cost_estimate=cost(6),
        name="pick_two",
    )(index, slots)


def deal(source, index, live, target=None, extra=None, single=None, joined=0):
    count = index.shape[0]
    rows, width = source.shape[1:]
    more = 0 if extra is None else extra.shape[0] // count
    plan = [index, live] if extra is None else [index, live, target]
    args = [source] if extra is None else [source, extra, single]

    def body(*refs):
        index_ref, live_ref = refs[:2]
        source_ref = refs[len(plan)]
        outs = refs[len(plan) + len(args) :]
        for k in range(count):
            value = source_ref[index_ref[k]]
            value = jnp.where(live_ref[k] > 0, value, jnp.zeros_like(value))
            if joined:
                outs[k // joined][k % joined] = value
            elif more:
                start = pl.multiple_of(refs[2][k] * more, 8)
                last = refs[len(plan) + 1][pl.ds(start, more), :]
                one = refs[len(plan) + 2][pl.ds(refs[2][k], 1), :]
                space = jnp.zeros((16 - more - 1, width), f32)
                last = jnp.concatenate([space, one, last], axis=0)
                outs[k][: rows - 16] = value[: rows - 16]
                outs[k][rows - 16 :] = (value[rows - 16 :].astype(f32) + last).astype(bf16)
            else:
                outs[k][...] = value

    def whole(shape):
        return pl.BlockSpec(shape, lambda i, *plan: (0,) * len(shape))

    if joined:
        shapes = [jax.ShapeDtypeStruct((joined, rows, width), source.dtype)] * (count // joined)
    else:
        shapes = [jax.ShapeDtypeStruct((rows, width), source.dtype)] * count
    return pl.pallas_call(
        body,
        grid_spec=pltpu.PrefetchScalarGridSpec(
            num_scalar_prefetch=len(plan),
            grid=(1,),
            in_specs=[whole(x.shape) for x in args],
            out_specs=[whole(x.shape) for x in shapes],
        ),
        out_shape=shapes,
        compiler_params=params(16),
        cost_estimate=cost(3),
        name="deal",
    )(*plan, *args)


def adamw_update(weight, gradient, first_moment, second, average, step_rate):
    first_new = BETA_ONE * first_moment + (1.0 - BETA_ONE) * gradient
    second_new = BETA_TWO * second + (1.0 - BETA_TWO) * gradient * gradient
    correct_one = 1.0 - BETA_ONE**STEP
    correct_two = 1.0 - BETA_TWO**STEP
    normalized = first_new / correct_one / (jnp.sqrt(second_new / correct_two) + ADAM_EPS)
    weight_new = weight - step_rate * (normalized + WEIGHT_DECAY * weight)
    average_new = AVERAGE_KEEP * average + (1.0 - AVERAGE_KEEP) * weight_new
    return (weight_new, first_new, second_new, average_new)


def finish_kernel(
    code_ref, share_ref, w_ref, m_ref, v_ref, a_ref,
    w_out, m_out, v_out, a_out, small_ref, gain_ref, scr,
):
    count, rows, _ = share_ref.shape
    keys = 4 * NS // count
    total = jnp.zeros((1, D), f32)
    for i in range(count):
        share = share_ref[code_ref[i]].astype(f32)
        scr[i * keys : (i + 1) * keys, :] = share[rows - keys :]
        small_ref[i : i + 1, :] = share[rows - keys - 1 : rows - keys]
        total = total + share[:1]
    gain_ref[...] = jnp.broadcast_to(total, (8, D))
    new = adamw_update(
        w_ref[...], jnp.transpose(scr[...]), m_ref[...], v_ref[...], a_ref[...], MATRIX_RATE
    )
    for out, value in zip((w_out, m_out, v_out, a_out), new):
        out[...] = value


def finish_stage(code, shares, weight, first, second, ema):
    count = shares.shape[0]
    args = (shares, weight, first, second, ema)
    outs = [jax.ShapeDtypeStruct(weight.shape, f32)] * 4 + [
        jax.ShapeDtypeStruct((count, D), f32),
        jax.ShapeDtypeStruct((8, D), f32),
    ]

    def whole(shape):
        return pl.BlockSpec(shape, lambda i, code: (0,) * len(shape))

    return pl.pallas_call(
        finish_kernel,
        grid_spec=pltpu.PrefetchScalarGridSpec(
            num_scalar_prefetch=1,
            grid=(1,),
            in_specs=[whole(x.shape) for x in args],
            out_specs=[whole(x.shape) for x in outs],
            scratch_shapes=[pltpu.VMEM((4 * NS, D), f32)],
        ),
        out_shape=outs,
        compiler_params=params(16),
        cost_estimate=cost(5),
        name="finish_stage",
    )(code, *args)


def make_local(n_dp, n_mp):
    per = H // n_mp
    direct = n_mp == 4 and n_dp == 8

    def swap(x, axis, size, bit):
        return lax.ppermute(x, axis, [(i, i ^ bit) for i in range(size)])

    def head_rows(mp_index):
        rows = jnp.arange(n_mp, dtype=jnp.int32)
        return jnp.bitwise_xor(rows, mp_index) if direct else rows

    def over_mp(x):
        if direct:
            far = swap(x, "mp", n_mp, 2)
            return [x, swap(x, "mp", n_mp, 1), far, swap(far, "mp", n_mp, 1)]
        copies = lax.all_gather(x, "mp", axis=0)
        return [copies[k] for k in range(n_mp)]

    def gather_dp(part):
        return [part[None]] + [swap(part, "dp", n_dp, k)[None] for k in range(1, n_dp)]

    def pick_own(pieces, owners, dp_index):
        return pick(pieces, jnp.bitwise_xor(owners, dp_index))

    def scatter_mp(grads):
        got = swap(jnp.stack([grads[1], grads[3]]), "mp", n_mp, 1)
        away = (grads[2].astype(f32) + got[1].astype(f32)).astype(bf16)
        mine = grads[0].astype(f32) + got[0].astype(f32)
        return mine + swap(away, "mp", n_mp, 2).astype(f32)

    def deal_targets(owners, targets):
        match = targets[:, None] == owners[None, :]
        return jnp.argmax(match, axis=1).astype(jnp.int32), jnp.any(match, axis=1).astype(jnp.int32)

    def gather_all(x, mp_index, dp_index):
        both = x[None]
        for axis, size, bit in (
            ("dp", n_dp, 2), ("dp", n_dp, 4), ("dp", n_dp, 1), ("mp", n_mp, 2), ("mp", n_mp, 1)
        ):
            both = jnp.concatenate([both, swap(both, axis, size, bit)], axis=0)
        far = jnp.bitwise_xor(jnp.arange(n_mp, dtype=jnp.int32), mp_index)[:, None]
        off = jnp.bitwise_xor(jnp.arange(n_dp, dtype=jnp.int32), dp_index)[None, :]
        code = ((off >> 1) & 3) + 4 * (off & 1) + 8 * (far >> 1) + 16 * (far & 1)
        return both, code.reshape(-1)

    def local(
        hidden_in, out_grad, seq_len, owner_list,
        block_master, block_first, block_second, block_ema,
        head_small, head_first, head_second, head_ema,
        bc_weight, bc_first, bc_second, bc_ema,
        shared_small, shared_first, shared_second, shared_ema,
    ):
        tokens = hidden_in.shape[0]
        mp_index = lax.axis_index("mp")
        dp_index = lax.axis_index("dp")
        owners = lax.dynamic_slice_in_dim(owner_list, mp_index * per, per)
        order = head_rows(mp_index)
        bounds = (mp_index + jnp.arange(2, dtype=jnp.int32)) * tokens % seq_len == 0
        starts = bounds[:1].reshape(1, 1)
        ends = bounds[1:].reshape(1, 1)
        meta = jnp.concatenate([mp_index.reshape(1), seq_len, order]).astype(jnp.int32)
        nexts = [(i, i + 1) for i in range(n_mp - 1)]
        prevs = [(i + 1, i) for i in range(n_mp - 1)]

        slot_t = jnp.transpose(block_master[0, 0]).astype(bf16)
        part_v = jnp.concatenate(
            [slot_t[PS : 2 * PS + 2], jnp.zeros((WV - PS - 2, D), bf16)], axis=0
        )
        part_go = jnp.concatenate([slot_t[:PS], slot_t[2 * PS + 2 :]], axis=0)
        if direct:
            pieces_v = gather_dp(part_v)
            mine_v = pick_own(pieces_v, owners, dp_index)
            far_v = swap(mine_v, "mp", n_mp, 2)
            near_v = swap(mine_v, "mp", n_mp, 1)
            slots = lax.all_gather(part_go, ("mp", "dp"), axis=0)
            rows_of = jnp.repeat(order, per)
            heads_of = rows_of * per + jnp.arange(H, dtype=jnp.int32) % per
            wg, wo = pick_two(slots, rows_of * n_dp + jnp.take(owner_list, heads_of))
        else:
            mine_v = pick([lax.all_gather(part_v, "dp", axis=0)], owners)
            wv = jnp.concatenate(over_mp(mine_v), axis=0)
            mine_go = pick([lax.all_gather(part_go, "dp", axis=0)], owners)
            all_go = over_mp(mine_go)
            wg = jnp.concatenate([x[:, :PS] for x in all_go], axis=0)
            wo = jnp.concatenate([x[:, PS:] for x in all_go], axis=0)
        wg = wg.reshape(CH, D)
        wo = wo.reshape(CH, D)

        hidden = hidden_in.astype(f32)
        gain_in = shared_small[K:].reshape(D)
        scale_in = lax.rsqrt(jnp.mean(hidden * hidden, axis=1, keepdims=True) + NORM_EPS)
        normed = (hidden * scale_in * gain_in).astype(bf16)
        from_left = lax.ppermute(normed[-HALO:], "mp", nexts)
        from_right = lax.ppermute(normed[:HALO], "mp", prevs)
        from_left = jnp.where(starts, jnp.zeros_like(from_left), from_left)
        from_right = jnp.where(ends, jnp.zeros_like(from_right), from_right)
        nx = jnp.concatenate(
            [normed, from_right, jnp.zeros((PAD - 2 * HALO, D), bf16), from_left], axis=0
        )

        heads = jnp.concatenate(over_mp(head_small), axis=0)
        taps_v = jnp.transpose(heads[:, 1 : 1 + K, :], (0, 2, 1)).reshape(CH, K)
        taps_v = jnp.pad(taps_v, ((0, 0), (0, 1)))
        cols = jnp.stack([heads[:, 0].reshape(CH), heads[:, K + 1].reshape(CH)], axis=1)
        cols = jnp.pad(cols, ((0, 0), (0, 6)))
        bias = heads[:, K + 2, :2]
        key_low = jnp.transpose(bc_weight).astype(bf16)
        taps_k = jnp.pad(jnp.transpose(shared_small[:K]), ((0, 0), (0, 1)))
        ids = jnp.arange(BL)
        tri = (ids[:, None] <= ids[None, :]).astype(f32)
        after = (ids[:, None] > ids[None, :]).astype(f32)

        key_proj, key_u, k4, scores = key_stage(nx, key_low, taps_k, tokens)
        if direct:
            far_v, k4 = lax.optimization_barrier((far_v, k4))
            wv = jnp.concatenate([mine_v, near_v, far_v, swap(far_v, "mp", n_mp, 1)], axis=0)
        v, u, s, rows, tot, sblk, sdev, tdev = value_stage(
            nx, wv, taps_v, bias, k4, tri, tokens
        )
        tot_hi = lax.reduce_precision(tdev, 8, 7)
        tot_mid = lax.reduce_precision(tdev - tot_hi, 8, 7)
        tot_low = tdev - tot_hi - tot_mid
        message = jnp.concatenate(
            [sdev, tot_hi.astype(bf16), tot_mid.astype(bf16), tot_low.astype(bf16)], axis=0
        )
        def twist(k, q):
            return q ^ k if direct else q

        o_intra = intra_stage(v, rows, scores)
        if direct:
            far = swap(message, "mp", n_mp, 2)
            near = swap(message, "mp", n_mp, 1)
            far, o_intra = lax.optimization_barrier((far, o_intra))
            messages = [message, near, far, swap(far, "mp", n_mp, 1)]
        else:
            messages = over_mp(message)
        far_tot = jnp.stack([x[CH:] for x in messages]).astype(f32)

        (s9,) = chain_stage(meta, sblk, tot, far_tot, messages, twist, tokens)
        hidden_out, result_t, dgate_t, do_t, dsblk, dsdev, rcc, dkc, small_mid = token_stage(
            o_intra, v, s9, k4, rows, tot, wg, wo, nx, hidden_in, out_grad, cols
        )
        if direct:
            far_d = swap(dsdev, "mp", n_mp, 2)
            near_d = swap(dsdev, "mp", n_mp, 1)
        grad_go, dn_gate = early_grad_stage(dgate_t, result_t, nx, out_grad, wg)
        grad_go = grad_go.reshape(n_mp, per * 2 * PS, D)
        if direct:
            far_d, grad_go = lax.optimization_barrier((far_d, grad_go))
            got = swap(jnp.stack([grad_go[1], grad_go[3]]), "mp", n_mp, 1)
            away = (grad_go[2].astype(f32) + got[1].astype(f32)).astype(bf16)
            far_go = swap(away, "mp", n_mp, 2)
            do_back, away = lax.optimization_barrier((do_t, away))
        else:
            do_back = do_t
        dvi, rci, dki = intra_back_stage(v, do_back, rows, scores, k4, dkc)
        if direct:
            messages = [dsdev, near_d, far_d, swap(far_d, "mp", n_mp, 1)]
        else:
            messages = over_mp(dsdev)
        natural = jnp.arange(n_dp, dtype=jnp.int32)
        ds9, x9 = chain_stage(meta, dsblk, tot, far_tot, messages, twist, tokens, s9)
        if direct:
            far_go, ds9, dvi = lax.optimization_barrier((far_go, ds9, dvi))
            mine_go = grad_go[0].astype(f32) + got[0].astype(f32) + far_go.astype(f32)
            mine_go = mine_go.astype(bf16)
        else:
            mine_go = lax.psum_scatter(grad_go, "mp", scatter_dimension=0, tiled=True)[0]
        if direct:
            bits = jnp.arange(n_dp, dtype=jnp.int32)
            bits = (bits >> 2) + 4 * ((bits >> 1) & 1) + 2 * (bits & 1)
            keep_go, send_go = deal(
                mine_go.reshape(per, 2 * PS, D),
                *deal_targets(owners, jnp.bitwise_xor(bits, dp_index)),
                joined=n_dp // 2,
            )
            keep_go, ds9 = lax.optimization_barrier((keep_go, ds9))
            keep_go = keep_go.astype(f32) + swap(send_go, "dp", n_dp, 1).astype(f32)
        else:
            (dealt,) = deal(
                mine_go.reshape(per, 2 * PS, D), *deal_targets(owners, natural), joined=n_dp
            )
            own_go = lax.psum_scatter(dealt, "dp", scatter_dimension=0, tiled=True)[0]
        dpre, dx, dk = cross_back_stage(
            dvi, v, do_t, u, ds9, k4, rows, rci, rcc, x9, dki, cols, after
        )
        if direct:
            keep_go, dpre, dk = lax.optimization_barrier((keep_go, dpre, dk))
            far_go = swap(keep_go[2:].astype(bf16), "dp", n_dp, 4)
        grad_v, dn_value, tap_v = value_back_stage(dpre, taps_v, s, dx, nx, wv)
        if direct:
            far_go, grad_v = lax.optimization_barrier((far_go, grad_v))
            keep_go = keep_go[:2] + far_go.astype(f32)
            last_go = swap(keep_go[1].astype(bf16), "dp", n_dp, 2)
            both = grad_v.reshape(n_mp, per * WV, D)
            got_v = swap(jnp.stack([both[1], both[3]]), "mp", n_mp, 1)
            away_v = (both[2].astype(f32) + got_v[1].astype(f32)).astype(bf16)
            away_v, dk = lax.optimization_barrier((away_v, dk))
            far_v = swap(away_v, "mp", n_mp, 2)
        dpre_k = key_pre_stage(dk, key_u)
        grad_key, dn_key, tap_key = key_back_stage(meta, dpre_k, taps_k, key_proj, nx, key_low)
        if direct:
            far_v, last_go, grad_key, dn_key, tap_key = lax.optimization_barrier(
                (far_v, last_go, grad_key, dn_key, tap_key)
            )
            own_go = keep_go[0] + last_go.astype(f32)

        head_grad = jnp.concatenate(
            [
                small_mid[0, 0].reshape(H, 1, PS),
                jnp.transpose(
                    tap_v.reshape(NG, 8, GH, PS)[:, :K], (0, 2, 1, 3)
                ).reshape(H, K, PS),
                small_mid[1, 0].reshape(H, 1, PS),
                jnp.pad(jnp.transpose(jnp.sum(dx, axis=2)), ((0, 0), (0, PS - 2))).reshape(
                    H, 1, PS
                ),
            ],
            axis=1,
        )
        if direct:
            head_grad = jnp.take(head_grad.reshape(n_mp, per, 10, PS), order, axis=0)
        small_grad = jnp.concatenate(
            [head_grad.reshape(-1), tap_key[:K].reshape(-1)]
        )
        count = small_grad.shape[0]

        if direct:
            rows_key = (4 * NS) // (n_mp * n_dp)
            small_rows = jnp.pad(small_grad, (0, n_mp * n_dp * D - count)).reshape(n_mp, n_dp, D)
            small_rows = jnp.take(small_rows, order, axis=0).astype(bf16)
            extra = scatter_mp(jnp.concatenate([grad_key, small_rows], axis=1))
            mine_v = both[0].astype(f32) + got_v[0].astype(f32) + far_v.astype(f32)
            targets = jnp.bitwise_xor(natural, dp_index)
            dealt = deal(
                mine_v.astype(bf16).reshape(per, WV, D),
                *deal_targets(owners, targets),
                targets,
                extra[: n_dp * rows_key],
                extra[n_dp * rows_key :],
            )
            own_v = dealt[0].astype(f32)
            for k in range(1, n_dp):
                own_v = own_v + swap(dealt[k], "dp", n_dp, k).astype(f32)
        else:
            mine_v = lax.psum_scatter(
                grad_v.reshape(n_mp, per * WV, D), "mp", scatter_dimension=0, tiled=True
            )[0]
            (dealt,) = deal(
                mine_v.reshape(per, WV, D), *deal_targets(owners, natural), joined=n_dp
            )
            own_v = lax.psum_scatter(dealt, "dp", scatter_dimension=0, tiled=True)[0].astype(f32)

        right_halo = slice(tokens, tokens + HALO)
        halo_l = lax.ppermute(dn_key[right_halo] + dn_value[right_halo], "mp", nexts)
        halo_r = lax.ppermute(dn_key[-HALO:] + dn_value[-HALO:], "mp", prevs)
        halo_l = jnp.where(starts, 0.0, halo_l)
        halo_r = jnp.where(ends, 0.0, halo_r)
        edges = jnp.concatenate([halo_l, jnp.zeros((tokens - 2 * HALO, D), f32), halo_r], axis=0)
        dnormed = dn_gate + dn_key[:tokens] + dn_value[:tokens] + edges
        scaled = dnormed * gain_in
        gain_grad = jnp.sum(dnormed * hidden * scale_in, axis=0)
        cross_in = jnp.sum(scaled * hidden, axis=1, keepdims=True)
        hidden_grad = (
            out_grad.astype(f32) + scale_in * scaled - hidden * scale_in**3 * cross_in / D
        )

        own_v = lax.optimization_barrier(own_v)
        own_go = own_go.astype(f32)
        own_grad = jnp.concatenate([own_go[:PS], own_v[: PS + 2], own_go[PS:]], axis=0)
        own_grad = lax.optimization_barrier(own_grad.reshape(3 * PS + 2, 1, D))
        previous = [
            jnp.transpose(x[0], (2, 0, 1))
            for x in (block_master, block_first, block_second, block_ema)
        ]
        slot_new = adamw_update(
            previous[0], own_grad, previous[1], previous[2], previous[3], MATRIX_RATE
        )
        is_owner = jnp.any(owners == dp_index)
        slot_new = [
            jnp.where(is_owner, renewed, before) for renewed, before in zip(slot_new, previous)
        ]
        if direct:
            share = jnp.concatenate(
                [jnp.broadcast_to(gain_grad, (15 - rows_key, D)), own_v[WV - rows_key - 1 :]],
                axis=0,
            ).astype(bf16)
            shares, code = gather_all(share, mp_index, dp_index)
            shares, slot_new = lax.optimization_barrier((shares, slot_new))
            *key_new, small_total, gain_total = finish_stage(
                code, shares, bc_weight, bc_first, bc_second, bc_ema
            )
            small_total = small_total.reshape(-1)[:count]
            gain_total = gain_total[0]
        else:
            key_total, small_total, gain_total = lax.psum(
                (grad_key.reshape(4 * NS, D).astype(f32), small_grad, gain_grad), ("dp", "mp")
            )
            key_new = adamw_update(
                bc_weight, jnp.transpose(key_total), bc_first, bc_second, bc_ema, MATRIX_RATE
            )
        slot_outs = [jnp.transpose(x, (1, 2, 0))[None] for x in slot_new]
        head_total = lax.dynamic_slice_in_dim(
            small_total[: H * 10 * PS].reshape(H, 10, PS), mp_index * per, per
        )
        head_new = adamw_update(
            head_small, head_total, head_first, head_second, head_ema, SMALL_RATE
        )
        shared_total = jnp.concatenate(
            [
                small_total[H * 10 * PS :].reshape(K, 4 * NS),
                gain_total.reshape(-1, 4 * NS),
            ],
            axis=0,
        )
        shared_new = adamw_update(
            shared_small, shared_total, shared_first, shared_second, shared_ema, SMALL_RATE
        )
        return (hidden_out, hidden_grad, *slot_outs, *head_new, *key_new, *shared_new)

    return local


def solution(mesh):
    rows = P(("dp", "mp"), None)
    slot = P("mp", "dp", None, None)
    head = P("mp", None, None)
    return jax.shard_map(
        make_local(mesh.shape["dp"], mesh.shape["mp"]),
        mesh=mesh,
        in_specs=(rows, rows, P("dp"), P()) + (slot,) * 4 + (head,) * 4 + (P(),) * 8,
        out_specs=(rows, rows) + (slot,) * 4 + (head,) * 4 + (P(),) * 8,
        check_vma=False,
    )
```
